32 devices in a mesh: rep: 2 (over core), shard: 16 (over z, y, x).
Axes of the slice: x: 2, y: 2, z: 4, core: 2. Of those that a mesh axis runs over, the one named last changes fastest.
Arguments:
- tokens: bfloat16 [16384, 768], P(('rep', 'shard')), may hold values from -6 to 6
- w_query: bfloat16 [768, 768], P('shard'), may hold values from -0.21875 to 0.21875
- b_query: bfloat16 [768], P('shard'), may hold values from -3 to 3
- w_key: bfloat16 [768, 768], P('shard'), may hold values from -0.21875 to 0.21875
- w_value: bfloat16 [768, 768], P('shard'), may hold values from -0.21875 to 0.21875
- b_value: bfloat16 [768], P('shard'), may hold values from -3 to 3
- w_attout: bfloat16 [768, 768], P('shard'), may hold values from -3.5 to 3.5
- b_attout: bfloat16 [768], P('shard'), may hold values from -3 to 3
- gain_first: bfloat16 [768], P('shard'), may hold values from 0.099609375 to 1.8984375
- beta_first: bfloat16 [768], P('shard'), may hold values from -3 to 3
- w_inner: bfloat16 [768, 3072], P('shard'), may hold values from -0.21875 to 0.21875
- b_inner: bfloat16 [3072], P('shard'), may hold values from -3 to 3
- w_outer: bfloat16 [3072, 768], P('shard'), may hold values from -0.109375 to 0.109375
- b_outer: bfloat16 [768], P('shard'), may hold values from -3 to 3
- gain_second: bfloat16 [768], P('shard'), may hold values from 0.099609375 to 1.8984375
- beta_second: bfloat16 [768], P('shard'), may hold values from -3 to 3
- cotangent: bfloat16 [16384, 768], P(('rep', 'shard')), may hold values from -6 to 6
- prompt_ids: int32 [16, 512], replicated, may hold values from 0 to 3, never falling along the last dimension, each value on 1 to 256 neighbouring positions
- cont_ids: int32 [16, 512], replicated, may hold values from 0 to 3, never falling along the last dimension, each value on 1 to 256 neighbouring positions
- offsets: int32 [16, 4], replicated, may hold values from 128 to 512
Outputs:
- result: float32 [16384, 768], P(('rep', 'shard'))
- grad_tokens: float32 [16384, 768], P(('rep', 'shard'))
- grad_w_query: float32 [768, 768], P('shard')
- grad_b_query: float32 [768], P('shard')
- grad_w_key: float32 [768, 768], P('shard')
- grad_w_value: float32 [768, 768], P('shard')
- grad_b_value: float32 [768], P('shard')
- grad_w_attout: float32 [768, 768], P('shard')
- grad_b_attout: float32 [768], P('shard')
- grad_gain_first: float32 [768], P('shard')
- grad_beta_first: float32 [768], P('shard')
- grad_w_inner: float32 [768, 3072], P('shard')
- grad_b_inner: float32 [3072], P('shard')
- grad_w_outer: float32 [3072, 768], P('shard')
- grad_b_outer: float32 [768], P('shard')
- grad_gain_second: float32 [768], P('shard')
- grad_beta_second: float32 [768], P('shard')
The draws below stay inside these ranges and needn't reach their ends.
Inputs may be any that keep to these rules, and one draw needn't show every extreme that they name: `prompt_ids`: in each group the ids never fall, every id of 0 to 3 occurs, and one document has exactly 256 tokens. `cont_ids`: in each group the ids never fall, every id occurs, and one continuation has exactly 256 tokens.
All inputs are finite; a program needn't handle non-finite values.
Results may differ from the reference program's by a relative error of at most 0.013.
Values may be sent and summed in bfloat16 or wider, within the bound.
A program may use at most 192 MiB of HBM per device.

```python
import math
import jax
import jax.numpy as jnp
import numpy as np
from jax import lax

D = 768
H = 12
DH = 64
FF = 3072
CLEN = 128
CONTS = 4
PROMPT = 512
GROUPS = 16
TOKENS = 16384
N_REP = 2
N_SHARD = 16


def with_ends(array, stream_key, least, high):
    longest = array.shape.index(max(array.shape))
    spots = []
    for shift in (0, 1):
        where = [jax.random.randint(jax.random.fold_in(stream_key, axis), (), 0, length) for axis, length in enumerate(array.shape)]
        where[longest] = (where[longest] + shift) % array.shape[longest]
        spots.append(tuple(where))
    return array.at[spots[0]].set(least).at[spots[1]].set(high)


def steps_of(stream_key, dims, split, least, high):
    loudness = 1.0
    for axis_at, blocks in split:
        heights = jax.random.uniform(jax.random.fold_in(jax.random.fold_in(stream_key, 6), axis_at), (blocks,), jnp.float32, least / len(split), high / len(split))
        loudness = loudness * jnp.repeat(jnp.exp(heights), dims[axis_at] // blocks).reshape((-1,) + (1,) * (len(dims) - 1 - axis_at))
    return loudness


def length_profile(number_of, total, reach, lean):
    portions = [(1 << 20) // math.isqrt(rank ** lean) + 1 for rank in range(2, number_of + 1)]
    surplus, given = total - reach - (number_of - 1), [1] * (number_of - 1)
    while surplus > 0:
        candidates = [i for i in range(number_of - 1) if given[i] < reach]
        pool, budget = sum([portions[i] for i in candidates]), surplus
        for i in candidates:
            addition = min(reach - given[i], max(1, budget * portions[i] // pool), surplus)
            given[i] = given[i] + addition
            surplus = surplus - addition
    return np.array([reach] + given)


def ragged(rng, amount, total, reach, skew):
    if amount == 2:
        one = jax.random.randint(rng, (), max(1, total - reach), min(reach, total - 1) + 1)
        return jnp.stack([one, total - one])
    sizes = jnp.asarray(length_profile(amount, total, reach, skew), jnp.int32)
    twos = (amount - 1) // 2
    source_of, receiver = sizes[1:1 + 2 * twos:2], sizes[2:2 + 2 * twos:2]
    margin = jnp.minimum(source_of - 1, reach - receiver)
    shifted = jax.random.randint(jax.random.fold_in(rng, 1), (twos,), 0, 1 << 20) % (margin + 1)
    sizes = sizes.at[1:1 + 2 * twos:2].set(source_of - shifted).at[2:2 + 2 * twos:2].set(receiver + shifted)
    return sizes[jax.random.permutation(jax.random.fold_in(rng, 2), amount)]


def normal_values(own_key, dims, width, reach, split=(), kind=jnp.bfloat16):
    entries = width * jax.random.normal(own_key, dims, jnp.float32)
    if split:
        entries = entries * steps_of(own_key, dims, split, -0.22, 0.18)
    return jnp.clip(entries, -reach, reach).astype(kind)


def setup_inputs(seed: int = 0) -> dict:
    key_list = jax.random.split(jax.random.key(seed), 21)
    tokens = normal_values(key_list[0], (TOKENS, D), 1.0, 6.0, ((0, 32),))
    w_query = normal_values(key_list[1], (D, D), D ** -0.5, 0.21875, ((0, 16),))
    b_query = normal_values(key_list[2], (D,), 0.5, 3.0, ((0, 16),))
    w_key = normal_values(key_list[3], (D, D), D ** -0.5, 0.21875, ((0, 16),))
    w_value = normal_values(key_list[4], (D, D), D ** -0.5, 0.21875, ((0, 16),))
    b_value = normal_values(key_list[5], (D,), 0.5, 3.0, ((0, 16),))
    w_attout = normal_values(key_list[6], (D, D), (max(D // 256, 1)) ** -0.5, 3.5, ((0, 16),))
    b_attout = normal_values(key_list[7], (D,), 0.5, 3.0, ((0, 16),))
    gain_first = jnp.clip(1.0 + 0.18 * jax.random.normal(key_list[8], (D,), jnp.float32), 0.099609375, 1.8984375).astype(jnp.bfloat16)
    beta_first = normal_values(key_list[9], (D,), 0.5, 3.0, ((0, 16),))
    w_inner = normal_values(key_list[10], (D, FF), D ** -0.5, 0.21875, ((0, 16),))
    b_inner = normal_values(key_list[11], (FF,), 0.5, 3.0, ((0, 16),))
    w_outer = normal_values(key_list[12], (FF, D), FF ** -0.5, 0.109375, ((0, 16),))
    b_outer = normal_values(key_list[13], (D,), 0.5, 3.0, ((0, 16),))
    gain_second = jnp.clip(1.0 + 0.18 * jax.random.normal(key_list[14], (D,), jnp.float32), 0.099609375, 1.8984375).astype(jnp.bfloat16)
    beta_second = normal_values(key_list[15], (D,), 0.5, 3.0, ((0, 16),))
    cotangent = normal_values(key_list[16], (TOKENS, D), 1.0, 6.0, ((0, 32),))
    prompt_ids = jax.vmap(lambda own: jnp.searchsorted(jnp.cumsum(ragged(own, 4, PROMPT, PROMPT // 2, 1)), jnp.arange(PROMPT), side="right"))(jax.random.split(key_list[17], GROUPS)).reshape((GROUPS, PROMPT)).astype(jnp.int32)
    cont_ids = jax.vmap(lambda own: jnp.searchsorted(jnp.cumsum(ragged(own, CONTS, PROMPT, 2 * CLEN, 1)), jnp.arange(PROMPT), side="right"))(jax.random.split(key_list[18], GROUPS)).reshape((GROUPS, PROMPT)).astype(jnp.int32)
    offsets = with_ends(jax.random.randint(key_list[19], (GROUPS, CONTS), PROMPT // 4, PROMPT + 1), jax.random.fold_in(key_list[19], 1), PROMPT // 4, PROMPT).astype(jnp.int32)
    return dict(tokens=tokens, w_query=w_query, b_query=b_query, w_key=w_key, w_value=w_value, b_value=b_value, w_attout=w_attout, b_attout=b_attout, gain_first=gain_first, beta_first=beta_first, w_inner=w_inner, b_inner=b_inner, w_outer=w_outer, b_outer=b_outer, gain_second=gain_second, beta_second=beta_second, cotangent=cotangent, prompt_ids=prompt_ids, cont_ids=cont_ids, offsets=offsets)


@jax.custom_vjp
def low(v):
    return lax.optimization_barrier(v.astype(jnp.bfloat16)).astype(jnp.float32)

@jax.custom_vjp
def low_back(v):
    return v

def low_keep(v):
    return (low(v), None)

def low_pass(kept, grad):
    return (grad,)

def back_keep(v):
    return (v, None)

def back_low(kept, grad):
    return (low(grad),)
low.defvjp(low_keep, low_pass)
low_back.defvjp(back_keep, back_low)
EPSILON = 1e-12

def matmul(left, right):
    return jnp.dot(left, right, precision=lax.Precision.HIGHEST)

def layer_norm(values, gain, beta):
    average = lax.optimization_barrier(jnp.mean(values, axis=-1, keepdims=True))
    centered = values - average
    variance = lax.optimization_barrier(jnp.mean(centered * centered, axis=-1, keepdims=True))
    return centered * lax.rsqrt(variance + EPSILON) * gain + beta

def row_offsets(cont_group, offset_group):
    choose = cont_group[:, None] == jnp.arange(offset_group.shape[0], dtype=jnp.int32)[None, :]
    return lax.optimization_barrier(jnp.sum(jnp.where(choose, offset_group[None, :], 0), axis=1)).astype(jnp.int32)

def allowed(row_cont, row_label, row_limit, prompt_group, cont_group):
    length = prompt_group.shape[0]
    columns = jnp.arange(length, dtype=jnp.int32)
    first = jnp.where(row_cont[:, None], columns[None, :] < row_limit[:, None], prompt_group[None, :] == row_label[:, None])
    second = row_cont[:, None] & (cont_group[None, :] == row_label[:, None])
    return jnp.concatenate([first, second], axis=1)

def group_forward(rows, params, prompt_group, cont_group, offset_group):
    w_query, b_query, w_key, w_value, b_value, w_attout, b_attout, gain_first, beta_first, w_inner, b_inner, w_outer, b_outer, gain_second, beta_second = params
    length = prompt_group.shape[0]
    total = rows.shape[0]
    scale = 1.0 / math.sqrt(DH)
    query = low(low_back(matmul(rows, w_query) + b_query))
    keys = low(low_back(matmul(rows, w_key)))
    values = low(low_back(matmul(rows, w_value) + b_value))
    heads_query = query.reshape(total, H, DH)
    heads_keys = keys.reshape(total, H, DH)
    heads_values = values.reshape(total, H, DH)
    scores = low_back(jnp.einsum('qhd,khd->hqk', heads_query, heads_keys, precision=lax.Precision.HIGHEST) * scale)
    row_cont = jnp.arange(total, dtype=jnp.int32) >= length
    row_label = jnp.concatenate([prompt_group, cont_group])
    row_limit = jnp.concatenate([jnp.zeros((length,), jnp.int32), row_offsets(cont_group, offset_group)])
    mask = allowed(row_cont, row_label, row_limit, prompt_group, cont_group)
    scores = jnp.where(mask[None], scores, -1e+30)
    probs = low(jax.nn.softmax(scores, axis=-1))
    mixed = jnp.einsum('hqk,khd->qhd', probs, heads_values, precision=lax.Precision.HIGHEST)
    mixed = low(low_back(mixed.reshape(total, D)))
    branch = low_back(matmul(mixed, w_attout) + b_attout)
    normed = layer_norm(rows + branch, gain_first, beta_first)
    hidden = low_back(matmul(low(normed), w_inner) + b_inner)
    active = low(jax.nn.gelu(hidden, approximate=False))
    output = low_back(matmul(active, w_outer) + b_outer)
    return layer_norm(normed + output, gain_second, beta_second)

def to_groups(values):
    arranged = values.reshape(N_REP, 2, N_SHARD // 2, PROMPT, D)
    return jnp.transpose(arranged, (0, 2, 1, 3, 4)).reshape(GROUPS, 2 * PROMPT, D)

def from_groups(values):
    arranged = values.reshape(N_REP, N_SHARD // 2, 2, PROMPT, D)
    return jnp.transpose(arranged, (0, 2, 1, 3, 4)).reshape(TOKENS, D)

def reference(tokens, w_query, b_query, w_key, w_value, b_value, w_attout, b_attout, gain_first, beta_first, w_inner, b_inner, w_outer, b_outer, gain_second, beta_second, cotangent, prompt_ids, cont_ids, offsets):
    params = (w_query, b_query, w_key, w_value, b_value, w_attout, b_attout, gain_first, beta_first, w_inner, b_inner, w_outer, b_outer, gain_second, beta_second)
    params = tuple((item.astype(jnp.float32) for item in params))
    rows = to_groups(tokens.astype(jnp.float32))
    cots = to_groups(cotangent.astype(jnp.float32))

    def one_group(carry, inputs):
        rows_group, cot_group, prompt_group, cont_group, offset_group = inputs

        def forward(rows_in, params_in):
            return group_forward(rows_in, params_in, prompt_group, cont_group, offset_group)
        outcome, pullback = jax.vjp(forward, rows_group, params)
        grad_rows, grad_params = pullback(cot_group)
        carry = jax.tree.map(jnp.add, carry, grad_params)
        return (carry, (outcome, grad_rows))
    zeros = jax.tree.map(jnp.zeros_like, params)
    sums, (outcomes, grads_in) = lax.scan(one_group, zeros, (rows, cots, prompt_ids, cont_ids, offsets))
    return (from_groups(outcomes), from_groups(grads_in), sums[0], sums[1], sums[2], sums[3], sums[4], sums[5], sums[6], sums[7], sums[8], sums[9], sums[10], sums[11], sums[12], sums[13], sums[14])
```

```python
from functools import partial

import jax
import jax.numpy as jnp
from jax import lax
from jax.experimental import pallas as pl
from jax.experimental.pallas import tpu as pltpu
from jax.sharding import PartitionSpec as P

D = 768
H = 12
DH = 64


EPSILON = 1e-12


MESHID = pl.DeviceIdType.MESH
BF16 = jnp.bfloat16
F32 = jnp.float32


def line_order(n):
    depth = n // 4
    order = []
    for z in range(depth):
        others = [k for k in range(depth) if k != z]
        others.sort(key=lambda k: (k // 2 != z // 2, abs(k - z), k))
        order.append([z] + others)
    return depth, order


def pick(table, z):
    out = table[-1]
    for i in range(len(table) - 2, -1, -1):
        out = jnp.where(z == i, table[i], out)
    return out


def place_of(n):
    depth, order = line_order(n)
    s = lax.axis_index("shard")
    r = lax.axis_index("rep")
    z, q = s // 4, s % 4
    y, x = q // 2, q % 2
    core = r % 2
    qx = y * 2 + 1 - x
    qy = (1 - y) * 2 + x
    qd = (1 - y) * 2 + 1 - x

    def device(rr, ss):
        return {"rep": rr, "shard": ss}

    half = depth // 2
    return dict(
        depth=depth,
        order=order,
        z=z,
        q=q,
        core=core,
        s=s,
        r=r,
        qx=qx,
        qy=qy,
        qd=qd,
        half=half,
        near_x=device(r, z * 4 + qx),
        near_y=device(r, z * 4 + qy),
        up=device(r, s + 4),
        down=device(r, s - 4),
        sibling=device(r + 1 - 2 * core, s),
        ahead=device(r, s + 4 * half),
        behind=device(r, s - 4 * half),
        device=device,
    )


def entry_barrier(p):
    bar = pltpu.get_barrier_semaphore()
    z, depth, half = p["z"], p["depth"], p["half"]

    def signal(where):
        pl.semaphore_signal(bar, inc=1, device_id=where, device_id_type=MESHID)

    signal(p["near_x"])
    signal(p["near_y"])
    signal(p["sibling"])
    pl.when(z + 1 < depth)(lambda: signal(p["up"]))
    pl.when(z > 0)(lambda: signal(p["down"]))
    pl.when(z < half)(lambda: signal(p["ahead"]))
    pl.when(z >= half)(lambda: signal(p["behind"]))
    pl.semaphore_wait(bar, 4 + jnp.where(z > 0, 1, 0) + jnp.where(z + 1 < depth, 1, 0))


def part_of(rows, quarter):
    top = (rows // 2 + 7) // 8 * 8
    if quarter is None:
        return 0, rows
    return (0, top) if quarter == 0 else (top, rows - top)


class Gather:
    def __init__(self, place, src, dst, send, recv, local, base):
        self.p, self.src, self.dst = place, src, dst
        self.rows, self.cols = src.shape[1], src.shape[2]
        self.send, self.recv, self.local, self.base = send, recv, local, base
        depth = place["depth"]
        self.names = {}
        for name in ("x", "y", "dx", "dy", "sx", "sy", "s0", "s1", "sz"):
            for i in range(depth):
                self.names[(name, i)] = len(self.names)
        self.line = len(self.names)
        self.count = self.line + 2 * depth

    def piece(self, chip, half, quarter=None):
        width = self.cols // 2
        cols = pl.ds(pl.multiple_of(half * width, width), width)
        first, size = part_of(self.rows, quarter)
        return self.dst.at[:, pl.ds(pl.multiple_of(chip * self.rows + first, 8), size), cols]

    def copy(self, sem, chip, where, quarter=None, own=False, half=None):
        half = self.p["core"] if half is None else half
        dst = self.piece(chip, half, quarter)
        src = dst
        if own:
            width = self.cols // 2
            src = self.src.at[:, :, pl.ds(pl.multiple_of(half * width, width), width)]
        i = self.base + (self.names[sem] if isinstance(sem, tuple) else self.line + sem)
        return pltpu.make_async_remote_copy(
            src_ref=src,
            dst_ref=dst,
            send_sem=self.send.at[i],
            recv_sem=self.recv.at[i],
            device_id=where,
            device_id_type=MESHID,
        )

    def item(self, i):
        return pick([line[i] for line in self.p["order"]], self.p["z"])

    def chips(self, i):
        k = self.item(i)
        p = self.p
        return tuple(k * 4 + p[name] for name in ("q", "qx", "qy", "qd"))

    def own_copy(self):
        me = self.p["s"]
        rows = pl.ds(pl.multiple_of(me * self.rows, self.rows), self.rows)
        return pltpu.make_async_copy(self.src, self.dst.at[:, rows, :], self.local)

    def start(self):
        p = self.p
        me, depth = p["s"], p["depth"]
        self.own_copy().start()
        pl.when(p["z"] + 1 < depth)(lambda: self.copy(0, me, p["up"], own=True).start())
        pl.when(p["z"] > 0)(lambda: self.copy(depth, me, p["down"], own=True).start())
        self.copy(("x", 0), me, p["near_x"], own=True).start()
        self.copy(("y", 0), me, p["near_y"], own=True).start()

    def flow(self, i):
        p = self.p
        z, s, depth = p["z"], p["s"], p["depth"]
        k = self.item(i)
        upward = k < z
        sem = jnp.where(upward, z - k - 1, depth + k - z - 1)
        onward = jnp.where(upward, z + 1 < depth, z > 0)
        target = p["device"](p["r"], jnp.where(upward, s + 4, s - 4))
        return sem, onward, target

    def take(self, i):
        p = self.p
        chip = self.chips(i)[0]
        sem, onward, target = self.flow(i)
        self.copy(sem, chip, p["sibling"]).wait_recv()
        pl.when(onward)(lambda: self.copy(sem + 1, chip, target).start())
        self.copy(("x", i), chip, p["near_x"]).start()
        self.copy(("y", i), chip, p["near_y"]).start()
        self.copy(("sz", i), chip, p["sibling"]).start()

    def spread(self, i):
        p = self.p
        _, cx, cy, _ = self.chips(i)
        self.copy(("x", i), cx, p["sibling"]).wait_recv()
        self.copy(("dy", i), cx, p["near_y"], quarter=0).start()
        self.copy(("sx", i), cx, p["sibling"]).start()
        self.copy(("y", i), cy, p["sibling"]).wait_recv()
        self.copy(("dx", i), cy, p["near_x"], quarter=1).start()
        self.copy(("sy", i), cy, p["sibling"]).start()

    def corner(self, i):
        p = self.p
        cd = self.chips(i)[3]
        self.copy(("dy", i), cd, p["sibling"], quarter=0).wait_recv()
        self.copy(("s0", i), cd, p["sibling"], quarter=0).start()
        self.copy(("dx", i), cd, p["sibling"], quarter=1).wait_recv()
        self.copy(("s1", i), cd, p["sibling"], quarter=1).start()

    def arrived(self):
        p = self.p
        other = 1 - p["core"]
        self.own_copy().wait()
        for i in range(p["depth"]):
            cm, cx, cy, cd = self.chips(i)
            if i:
                self.copy(("sz", i), cm, p["sibling"], half=other).wait_recv()
            self.copy(("sx", i), cx, p["sibling"], half=other).wait_recv()
            self.copy(("sy", i), cy, p["sibling"], half=other).wait_recv()
            self.copy(("s0", i), cd, p["sibling"], quarter=0, half=other).wait_recv()
            self.copy(("s1", i), cd, p["sibling"], quarter=1, half=other).wait_recv()

    def drain(self):
        p = self.p
        depth = p["depth"]
        me = p["s"]
        pl.when(p["z"] + 1 < depth)(lambda: self.copy(0, me, p["up"], own=True).wait_send())
        pl.when(p["z"] > 0)(lambda: self.copy(depth, me, p["down"], own=True).wait_send())
        for i in range(depth):
            cm, cx, cy, cd = self.chips(i)
            if i:
                sem, onward, target = self.flow(i)
                pl.when(onward)(
                    lambda sem=sem, target=target, cm=cm: self.copy(sem + 1, cm, target).wait_send()
                )
                self.copy(("sz", i), cm, p["sibling"]).wait_send()
            self.copy(("x", i), cm, p["near_x"]).wait_send()
            self.copy(("y", i), cm, p["near_y"]).wait_send()
            self.copy(("dy", i), cx, p["near_y"], quarter=0).wait_send()
            self.copy(("dx", i), cy, p["near_x"], quarter=1).wait_send()
            self.copy(("sx", i), cx, p["sibling"]).wait_send()
            self.copy(("sy", i), cy, p["sibling"]).wait_send()
            self.copy(("s0", i), cd, p["sibling"], quarter=0).wait_send()
            self.copy(("s1", i), cd, p["sibling"], quarter=1).wait_send()

    def early(self):
        return [
            self.start,
            partial(self.take, 1),
            partial(self.spread, 0),
            partial(self.spread, 1),
            partial(self.corner, 0),
            partial(self.corner, 1),
        ]

    def late(self):
        depth = self.p["depth"]
        steps = []
        for i in range(2, depth + 2):
            if i < depth:
                steps.append(partial(self.take, i))
            if 2 <= i - 1 < depth:
                steps.append(partial(self.spread, i - 1))
            if 2 <= i - 2 < depth:
                steps.append(partial(self.corner, i - 2))
        return steps


class Scatter:
    def __init__(self, place, given, grad, out, pair, diag, side, line, send, recv, base):
        self.p, self.given, self.grad, self.out = place, given, grad, out
        self.rows, self.cols = out.shape
        self.pair, self.diag, self.side, self.line = pair, diag, side, line
        self.send, self.recv, self.base = send, recv, base
        self.half = self.cols // 2
        core = place["core"]
        self.out_mine = pl.ds(pl.multiple_of(core * self.half, self.half), self.half)
        self.mine = self.out_mine if grad.shape[1] == self.cols else pl.ds(0, self.half)
        self.theirs = pl.ds(pl.multiple_of((1 - core) * self.half, self.half), self.half)
        depth = place["depth"]
        self.names = {}
        for name in ("p", "d0", "d1", "s0", "s1"):
            for i in range(depth):
                self.names[(name, i)] = len(self.names)
        self.names["o"] = len(self.names)
        self.first = len(self.names)
        self.count = self.first + 2 * depth

    @staticmethod
    def scratch(n, rows, cols, dtype):
        depth, h = n // 4, cols // 2
        return [
            pltpu.VMEM((n * rows, h), dtype),
            pltpu.VMEM((2 * depth, part_of(rows, 0)[1], h), dtype),
            pltpu.VMEM((2 * depth, rows, h), dtype),
            pltpu.VMEM((2 * depth - 2, rows, h), dtype),
        ]

    def make(self, sem, src, dst, where):
        i = self.base + sem
        return pltpu.make_async_remote_copy(
            src_ref=src,
            dst_ref=dst,
            send_sem=self.send.at[i],
            recv_sem=self.recv.at[i],
            device_id=where,
            device_id_type=MESHID,
        )

    def item(self, i):
        depth = self.p["depth"]
        return pick([line[depth - 1 - i] for line in self.p["order"]], self.p["z"])

    def rows_of(self, k, q, quarter=None):
        first, size = part_of(self.rows, quarter)
        return pl.ds(pl.multiple_of((k * 4 + q) * self.rows + first, 8), size)

    def pair_copy(self, i):
        r = self.rows * 4
        block = pl.ds(pl.multiple_of(self.item(i) * r, r), r)
        return self.make(
            self.names[("p", i)],
            self.given.at[block, self.theirs],
            self.pair.at[block, :],
            self.p["sibling"],
        )

    def diag_copy(self, i, quarter):
        p = self.p
        return self.make(
            self.names[("d0" if quarter == 0 else "d1", i)],
            self.grad.at[self.rows_of(self.item(i), p["qd"], quarter), self.mine],
            self.diag.at[i * 2 + quarter, pl.ds(0, part_of(self.rows, quarter)[1]), :],
            p["near_y"] if quarter == 0 else p["near_x"],
        )

    def side_copy(self, i, axis):
        p = self.p
        return self.make(
            self.names[("s0" if axis == 0 else "s1", i)],
            self.grad.at[self.rows_of(self.item(i), p["qx"] if axis == 0 else p["qy"]), self.mine],
            self.side.at[i * 2 + axis],
            p["near_x"] if axis == 0 else p["near_y"],
        )

    def line_copy(self, i):
        p = self.p
        k, z, depth = self.item(i), p["z"], p["depth"]
        slot = jnp.where(k > z, k - z - 1, depth - 1 + z - 1 - k)
        where = p["device"](p["r"], jnp.where(k > z, p["s"] + 4, p["s"] - 4))
        return self.make(
            self.first + slot,
            self.grad.at[self.rows_of(k, p["q"]), self.mine],
            self.line.at[slot],
            where,
        )

    def line_wait(self, slot):
        self.make(
            self.first + slot, self.line.at[slot], self.line.at[slot], self.p["sibling"]
        ).wait_recv()

    def out_copy(self, cols):
        return self.make(
            self.names["o"], self.out.at[:, cols], self.out.at[:, cols], self.p["sibling"]
        )

    def sweep(self, start, count, chunk, sources, store):
        def body(t, carry):
            at = pl.ds(pl.multiple_of(start + t * chunk, 8), chunk)
            low = pl.ds(pl.multiple_of(t * chunk, 8), chunk)
            total = self.grad[at, self.mine].astype(F32)
            for source in sources:
                total = total + source(at, low).astype(F32)
            store(at, low, total)
            return carry

        lax.fori_loop(0, count // chunk, body, 0)

    def store_grad(self, at, low, total):
        self.grad[at, self.mine] = total.astype(self.grad.dtype)

    def store_out(self, at, low, total):
        self.out[low, self.out_mine] = total

    def give(self, i):
        self.pair_copy(i).start()

    def merge(self, i):
        k = self.item(i)
        self.pair_copy(i).wait_recv()
        r4 = self.rows * 4
        self.sweep(k * r4, r4, 16, [lambda at, low: self.pair[at, :]], self.store_grad)
        self.diag_copy(i, 0).start()
        self.diag_copy(i, 1).start()

    def merge_diag(self, i):
        p = self.p
        k = self.item(i)
        for quarter, q in ((0, p["qx"]), (1, p["qy"])):
            self.diag_copy(i, quarter).wait_recv()
            slot = i * 2 + quarter
            first, size = part_of(self.rows, quarter)
            self.sweep(
                (k * 4 + q) * self.rows + first,
                size,
                8,
                [lambda at, low, slot=slot: self.diag[slot, low, :]],
                self.store_grad,
            )
            self.side_copy(i, quarter).start()

    def merge_side(self, i):
        p = self.p
        k, z, depth = self.item(i), p["z"], p["depth"]
        self.side_copy(i, 0).wait_recv()
        self.side_copy(i, 1).wait_recv()
        base = (k * 4 + p["q"]) * self.rows
        sides = [
            lambda at, low: self.side[i * 2, low, :],
            lambda at, low: self.side[i * 2 + 1, low, :],
        ]

        def total(slots, store):
            lines = [lambda at, low, slot=slot: self.line[slot, low, :] for slot in slots]
            self.sweep(base, self.rows, 16 if self.rows % 16 == 0 else 8, sides + lines, store)

        if i < depth - 1:
            has = ((k > z) & (z > 0)) | ((k < z) & (z + 1 < depth))
            slot = jnp.where(k > z, k - z, jnp.minimum(depth - 1 + z - k, 2 * depth - 3))

            @pl.when(has)
            def _():
                self.line_wait(slot)
                total([slot], self.store_grad)

            pl.when(jnp.logical_not(has))(lambda: total([], self.store_grad))
            self.line_copy(i).start()
        else:
            below, above = 0, depth - 1
            pl.when(z > 0)(lambda: self.line_wait(below))
            pl.when(z + 1 < depth)(lambda: self.line_wait(above))
            pl.when((z > 0) & (z + 1 < depth))(lambda: total([below, above], self.store_out))
            pl.when(z == 0)(lambda: total([above], self.store_out))
            pl.when(z + 1 == depth)(lambda: total([below], self.store_out))
            self.out_copy(self.out_mine).start()

    def finish(self):
        depth = self.p["depth"]
        self.out_copy(self.theirs).wait_recv()
        self.out_copy(self.out_mine).wait_send()
        for i in range(depth):
            self.pair_copy(i).wait_send()
            for side in (0, 1):
                self.diag_copy(i, side).wait_send()
                self.side_copy(i, side).wait_send()
            if i < depth - 1:
                self.line_copy(i).wait_send()

    def steps(self):
        depth = self.p["depth"]
        out = [lambda: [self.give(i) for i in range(depth)]]
        for i in range(depth + 2):
            if i < depth:
                out.append(partial(self.merge, i))
            if 0 <= i - 1 < depth:
                out.append(partial(self.merge_diag, i - 1))
            if 0 <= i - 2 < depth:
                out.append(partial(self.merge_side, i - 2))
        return out


def interleave(lists, skew, start=0):
    tagged = []
    for g, steps in enumerate(lists):
        for i, step in enumerate(steps):
            tagged.append((start + g * skew + i, g, i, step))
    tagged.sort(key=lambda entry: entry[:3])
    return [entry[3] for entry in tagged]


class Across:
    chunks = 4

    def __init__(self, place, src, dst, relay, send, recv, forward):
        p = place
        self.p, self.src, self.dst, self.relay = p, src, dst, relay
        self.send, self.recv = send, recv
        depth, z = p["depth"], p["z"]
        self.short = depth == 4
        self.at = z if forward else depth - 1 - z
        self.next = p["up"] if forward else p["down"]
        self.far = p["ahead"] if forward else p["behind"]

    def rows(self, j):
        size = self.src.shape[0] // self.chunks
        return pl.ds(j * size, size)

    def make(self, kind, j, src, dst, where):
        rows = self.rows(j)
        i = kind * self.chunks + j
        return pltpu.make_async_remote_copy(
            src_ref=src.at[rows],
            dst_ref=dst.at[rows],
            send_sem=self.send.at[i],
            recv_sem=self.recv.at[i],
            device_id=where,
            device_id_type=MESHID,
        )

    def begin(self, j):
        half = self.p["depth"] // 2
        if self.short:
            to_dst = self.make(0, j, self.src, self.dst, self.next)
            to_relay = self.make(1, j, self.src, self.relay, self.next)
            pl.when(self.at == 0)(lambda: to_dst.start())
            pl.when(self.at == 1)(lambda: to_relay.start())
        else:
            direct = self.make(0, j, self.src, self.dst, self.far)
            pl.when(self.at < half)(lambda: direct.start())

    def onward(self, j):
        if self.short:
            hold = self.make(0, j, self.src, self.dst, self.next)
            held = self.make(1, j, self.src, self.relay, self.next)
            from_dst = self.make(2, j, self.dst, self.dst, self.next)
            from_relay = self.make(3, j, self.relay, self.dst, self.next)

            @pl.when(self.at == 1)
            def _():
                hold.wait_recv()
                from_dst.start()

            @pl.when(self.at == 2)
            def _():
                held.wait_recv()
                from_relay.start()

    def arrived(self):
        half = self.p["depth"] // 2
        for j in range(self.chunks):
            if self.short:
                second = self.make(2, j, self.dst, self.dst, self.next)
                third = self.make(3, j, self.relay, self.dst, self.next)
                pl.when(self.at == 2)(lambda copy=second: copy.wait_recv())
                pl.when(self.at == 3)(lambda copy=third: copy.wait_recv())
            else:
                direct = self.make(0, j, self.src, self.dst, self.far)
                pl.when(self.at >= half)(lambda copy=direct: copy.wait_recv())

    def drain(self):
        half = self.p["depth"] // 2
        for j in range(self.chunks):
            if self.short:
                copies = (
                    self.make(0, j, self.src, self.dst, self.next),
                    self.make(1, j, self.src, self.relay, self.next),
                    self.make(2, j, self.dst, self.dst, self.next),
                    self.make(3, j, self.relay, self.dst, self.next),
                )
                pl.when(self.at == 0)(lambda: copies[0].wait_send())

                @pl.when(self.at == 1)
                def _():
                    copies[1].wait_send()
                    copies[2].wait_send()

                pl.when(self.at == 2)(lambda: copies[3].wait_send())
            else:
                direct = self.make(0, j, self.src, self.dst, self.far)
                pl.when(self.at < half)(lambda copy=direct: copy.wait_send())


VEC_ROWS = 16


def dot(a, b, ca=1, cb=0):
    return lax.dot_general(a, b, (((ca,), (cb,)), ((), ())), preferred_element_type=F32)


def mean_last(v):
    return jnp.sum(v, axis=-1, keepdims=True) * (1.0 / v.shape[-1])


def normalize(v):
    c = v - mean_last(v)
    inverse = lax.rsqrt(mean_last(c * c) + EPSILON)
    return c * inverse, inverse


def normalize_back(grad, gain, unit, inverse):
    g = grad * gain
    return inverse * (g - mean_last(g) - unit * mean_last(g * unit))


def gelu_pair(x):
    tail = jnp.exp(-0.5 * (x * x))
    t = 1.0 / (1.0 + (0.3275911 * 0.7071067811865476) * jnp.abs(x))
    poly = 1.061405429 * t - 1.453152027
    poly = poly * t + 1.421413741
    poly = poly * t - 0.284496736
    poly = poly * t + 0.254829592
    low = (0.5 * t) * poly * tail
    cdf = jnp.where(x < 0, low, 1.0 - low)
    return x * cdf, cdf + x * (tail * 0.3989422804014327)


def column_total(v):
    return jnp.sum(v, axis=0, keepdims=True)


def even_lanes(shape):
    return lax.broadcasted_iota(jnp.int32, shape, 1) % 128 < 64


def split_heads(x, even_ref, odd_ref):
    keep = even_lanes(x.shape)
    zero = jnp.zeros_like(x)
    even_ref[...] = jnp.where(keep, x, zero).astype(BF16)
    odd_ref[...] = jnp.where(keep, zero, x).astype(BF16)


def make_bias(bias, col_label, row_label, row_limit):
    length = row_label.shape[1]
    for b in range(0, length, 128):
        at = pl.ds(b, 128)
        row = lax.broadcasted_iota(jnp.int32, (128, length), 0) + b
        bias[at, :] = jnp.where(row < row_limit[...], 0.0, -1e30)
        same = col_label[at, 0:1] == row_label[...]
        bias[pl.ds(length + b, 128), :] = jnp.where(same, 0.0, -1e30)


def head_slices(j, side):
    head = pl.ds(pl.multiple_of(j * 128 + side * DH, DH), DH)
    row = pl.ds(pl.multiple_of(j * 16 + side * 8, 8), 8)
    return head, row


def attend_own(j, q_even, q_odd, keys, values_t, bias, part_t, tops, sums):
    lanes = pl.ds(pl.multiple_of(j * 128, 128), 128)
    length = q_even.shape[0]
    own = pl.ds(length, length)
    width = 256
    for b in range(0, length, width):
        block = pl.ds(b, width)
        for side, q_ref in ((0, q_even), (1, q_odd)):
            head, row = head_slices(j, side)
            scores = dot(keys[own, lanes], q_ref[block, lanes], 1, 1) + bias[own, block]
            top = jnp.max(scores, axis=0, keepdims=True)
            expo = jnp.exp(scores - top)
            part_t[head, block] = dot(values_t[head, own], expo.astype(BF16))
            tops[row, block] = jnp.broadcast_to(top, (8, width))
            sums[row, block] = jnp.broadcast_to(column_total(expo), (8, width))


def attend_far(j, q_even, q_odd, keys, values_t, bias, part_t, tops, sums, mixed_t):
    lanes = pl.ds(pl.multiple_of(j * 128, 128), 128)
    length = q_even.shape[0]
    far = pl.ds(0, length)
    width = 256
    for b in range(0, length, width):
        block = pl.ds(b, width)
        for side, q_ref in ((0, q_even), (1, q_odd)):
            head, row = head_slices(j, side)
            scores = dot(keys[far, lanes], q_ref[block, lanes], 1, 1) + bias[far, block]
            before = tops[row, block][0:1]
            top = jnp.maximum(jnp.max(scores, axis=0, keepdims=True), before)
            expo = jnp.exp(scores - top)
            fade = jnp.exp(before - top)
            total = sums[row, block][0:1] * fade + column_total(expo)
            mixed = part_t[head, block] * fade + dot(values_t[head, far], expo.astype(BF16))
            mixed_t[head, block] = (mixed * (1.0 / total)).astype(BF16)
            tops[row, block] = jnp.broadcast_to(top + jnp.log(total), (8, width))


def attend_pair_back(
    j, q_even, q_odd, g_even, g_odd, keys, keys_t, values, bias, delta, log_sums, grad_qt, grad_k, grad_v
):
    lanes = pl.ds(pl.multiple_of(j * 128, 128), 128)
    width = 256
    total_k, total_v = 0.0, 0.0
    for b in range(0, q_even.shape[0], width):
        block = pl.ds(b, width)
        for side, q_ref, g_ref in ((0, q_even, g_even), (1, q_odd, g_odd)):
            head = pl.ds(pl.multiple_of(j * 128 + side * DH, DH), DH)
            row = pl.ds(pl.multiple_of(j * 16 + side * 8, 8), 8)
            scores = dot(keys[:, lanes], q_ref[block, lanes], 1, 1) + bias[:, block]
            probs = jnp.exp(scores - log_sums[row, block][0:1])
            grad_p = dot(values[:, lanes], g_ref[block, lanes], 1, 1)
            grad_s = (probs * (grad_p - delta[row, block][0:1])).astype(BF16)
            total_v = total_v + dot(probs.astype(BF16), g_ref[block, lanes])
            total_k = total_k + dot(grad_s, q_ref[block, lanes])
            grad_qt[head, block] = (dot(keys_t[head, :], grad_s) * 0.125).astype(BF16)
    grad_k[:, lanes] = total_k.astype(BF16)
    grad_v[:, lanes] = total_v.astype(BF16)


def one_hot(rows, cols, shift):
    row = lax.broadcasted_iota(jnp.int32, (rows, cols), 0)
    col = lax.broadcasted_iota(jnp.int32, (rows, cols), 1)
    return jnp.where(col == row + shift, 1.0, 0.0)


def own_small(n, smalls, wide, out):
    s = lax.axis_index("shard")
    part = smalls[0].shape[1]
    quarter = n // 4
    out[...] = jnp.zeros_like(out)
    place = one_hot(part, D, s * part).astype(BF16)
    for i, v in enumerate(smalls):
        out[0, i : i + 1, :] = dot(v[...], place).astype(BF16)
    place = one_hot(4 * part, D, (s % quarter) * 4 * part).astype(BF16)
    piece = dot(wide[...], place)
    row = lax.broadcasted_iota(jnp.int32, (4, D), 0)
    out[0, 8:12, :] = jnp.where(row == s // quarter, piece, 0.0).astype(BF16)


def labels_of(n, prompt_ids, cont_ids, offsets, row_label, row_limit, col_label):
    half = n // 2
    s = lax.axis_index("shard")
    is_cont = s >= half
    group = lax.axis_index("rep") * half + s % half
    own = jnp.where(
        is_cont, cont_ids[pl.ds(group, 1), :], prompt_ids[pl.ds(group, 1), :]
    )
    limit = jnp.zeros_like(own)
    for k in range(offsets.shape[1]):
        limit = jnp.where(own == k, offsets[group, k], limit)
    row_label[...] = own
    row_limit[...] = jnp.where(is_cont, limit, 0)
    col_label[...] = jnp.broadcast_to(own, (128, own.shape[1])).T


PLAN_FOUR = (
    ('start', 'A'),
    ('start', 'V'),
    ('start', 'B'),
    ('tok', 0),
    ('tok', 1),
    ('spread', 'A', 0),
    ('take', 'A', 1),
    ('corner', 'A', 0),
    ('take', 'A', 2),
    ('spread', 'V', 0),
    ('take', 'V', 2),
    ('take', 'B', 1),
    ('take', 'V', 1),
    ('tok', 2),
    ('start', 'C'),
    ('pass', 0),
    ('take', 'V', 3),
    ('spread', 'A', 2),
    ('take', 'A', 3),
    ('spread', 'V', 2),
    ('spread', 'V', 1),
    ('tok', 3),
    ('spread', 'V', 3),
    ('corner', 'A', 2),
    ('spread', 'A', 1),
    ('take', 'B', 2),
    ('spread', 'A', 3),
    ('corner', 'V', 1),
    ('take', 'B', 3),
    ('corner', 'A', 1),
    ('corner', 'V', 2),
    ('pass', 1),
    ('corner', 'V', 0),
    ('spread', 'B', 1),
    ('corner', 'V', 3),
    ('spread', 'B', 0),
    ('war', 'V'),
    ('take', 'C', 2),
    ('corner', 'A', 3),
    ('spread', 'B', 2),
    ('war', 'A'),
    ('c', 'c1'),
    ('spread', 'B', 3),
    ('spread', 'C', 2),
    ('c', 'o0'),
    ('corner', 'B', 2),
    ('pass', 2),
    ('pass', 3),
    ('take', 'C', 1),
    ('start', 'D'),
    ('c', 'o1'),
    ('corner', 'B', 3),
    ('c', 'o2'),
    ('spread', 'C', 0),
    ('corner', 'B', 0),
    ('c', 'o3'),
    ('c', 'o4'),
    ('corner', 'B', 1),
    ('war', 'B'),
    ('spread', 'C', 1),
    ('c', 'o5'),
    ('take', 'D', 1),
    ('wtok',),
    ('c', 'c2'),
    ('c', 'p0'),
    ('spread', 'D', 0),
    ('take', 'C', 3),
    ('c', 'p1'),
    ('c', 'p2'),
    ('corner', 'C', 1),
    ('corner', 'C', 0),
    ('take', 'D', 2),
    ('c', 'p3'),
    ('c', 'p4'),
    ('spread', 'C', 3),
    ('c', 'p5'),
    ('corner', 'C', 2),
    ('take', 'D', 3),
    ('spread', 'D', 2),
    ('spread', 'D', 1),
    ('c', 'att'),
    ('corner', 'C', 3),
    ('war', 'C'),
    ('c', 'a0'),
    ('c', 'a1'),
    ('corner', 'D', 2),
    ('spread', 'D', 3),
    ('c', 'a2'),
    ('c', 'a3'),
    ('corner', 'D', 1),
    ('corner', 'D', 0),
    ('corner', 'D', 3),
    ('war', 'D'),
    ('c', 'b0'),
    ('c', 'b1'),
    ('c', 'b2'),
    ('c', 'b3'),
)


def default_plan(depth):
    plan = []
    for seg in "VA":
        plan.append(("start", seg))
    plan += [("tok", j) for j in range(Across.chunks)]
    plan += [("pass", j) for j in range(Across.chunks)]
    for seg in "VABCD":
        if seg in "BCD":
            plan.append(("start", seg))
        for i in range(depth):
            if i:
                plan.append(("take", seg, i))
            plan.append(("spread", seg, i))
            if i:
                plan.append(("corner", seg, i - 1))
        plan.append(("corner", seg, depth - 1))
        plan.append(("war", seg))
    plan += [("wtok",), ("c", "c1")] + [("c", "o%d" % i) for i in range(6)] + [("c", "c2")]
    plan += [("c", "p%d" % i) for i in range(6)] + [("c", "att")]
    plan += [("c", "a%d" % i) for i in range(4)] + [("c", "b%d" % i) for i in range(4)]
    return plan


def run_plan(plan, comm, single, loops):
    at = 0
    while at < len(plan):
        step = plan[at]
        if step[0] != "c":
            comm(step)
            at += 1
        elif step[1] in single:
            single[step[1]]()
            at += 1
        else:
            kind = step[1][0]
            count, chunk = loops[kind]
            after = []
            for _ in range(count):
                at += 1
                steps = []
                last = len(after) == count - 1
                while not last and plan[at][0] != "c":
                    steps.append(plan[at])
                    at += 1
                after.append(steps)

            def body(j, carry, after=after, chunk=chunk):
                chunk(j)
                for k, steps in enumerate(after):
                    if steps:

                        @pl.when(j == k)
                        def _():
                            for step in steps:
                                comm(step)

                return carry

            lax.fori_loop(0, count, body, 0)


def first_kernel(n, *refs):
    smalls = refs[0:8]
    (wide, tok, w_q, w_k, w_v, w_o, inner, outer, prompt_ids, cont_ids, offsets, cot) = refs[8:20]
    outs = refs[20:33]
    (
        four,
        vecs,
        g_four,
        g_vecs,
        g_inner,
        g_outer,
        far,
        q_even,
        q_odd,
        keys,
        values,
        mixed_t,
        log_sums,
        small,
        grad_wu,
        grad_wi,
        bias,
        values_t,
        vec,
        normed,
        low_ref,
        low_t,
        unit1,
        inverse1,
        acc,
        act,
        slope,
        g_out,
        row_label,
        row_limit,
        col_label,
        send,
        recv,
        local,
        relay,
        part_t,
        part_sums,
        far_send,
        far_recv,
        out_sem,
    ) = refs[33:]
    (
        o_result,
        o_even,
        o_odd,
        o_keys,
        o_values,
        o_mixed,
        o_logs,
        o_gfirst,
        o_small,
        o_wu,
        o_wi,
        o_four,
        o_far,
    ) = outs
    p = place_of(n)
    z, half = p["z"], p["half"]
    length = tok.shape[0]
    is_cont = z >= half
    for i, w in enumerate((w_q, w_k, w_v, w_o)):
        four[i] = w[...]
    own_small(n, smalls, wide, vecs)
    entry_barrier(p)
    across = Across(p, tok, far, relay, far_send, far_recv, True)
    segments = {}
    base = 0
    for j, (name, src, dst) in enumerate(
        (
            ("V", vecs, g_vecs),
            ("A", four.at[0:3], g_four.at[0:3]),
            ("B", four.at[3:4], g_four.at[3:4]),
            ("C", inner, g_inner),
            ("D", outer, g_outer),
        )
    ):
        segments[name] = Gather(p, src, dst, send, recv, local.at[j], base)
        base += segments[name].count

    def comm(step):
        if step[0] == "tok":
            across.begin(step[1])
        elif step[0] == "pass":
            across.onward(step[1])
        elif step[0] == "wtok":
            across.arrived()
        elif step[0] == "start":
            segments[step[1]].start()
        elif step[0] == "war":
            segments[step[1]].arrived()
        else:
            getattr(segments[step[1]], step[0])(step[2])

    pending = []

    def put(src, dst):
        copy = pltpu.make_async_copy(src, dst, out_sem.at[len(pending)])
        copy.start()
        pending.append(copy)

    def own_project():
        labels_of(n, prompt_ids, cont_ids, offsets, row_label, row_limit, col_label)
        make_bias(bias, col_label, row_label, row_limit)
        vec[...] = jnp.zeros_like(vec)

        def add_vec(i, c):
            at = pl.ds(pl.multiple_of(i * VEC_ROWS, 16), VEC_ROWS)
            vec[...] += g_vecs[0, at, :].astype(F32)
            return c

        lax.fori_loop(0, n, add_vec, 0)
        query = (dot(tok[...], g_four[0]) + vec[0:1, :]).astype(BF16)
        split_heads(query.astype(F32) * 0.125, q_even, q_odd)
        keys[length : 2 * length, :] = dot(tok[...], g_four[1]).astype(BF16)
        own_values = (dot(tok[...], g_four[2]) + vec[1:2, :]).astype(BF16)
        values[length : 2 * length, :] = own_values
        values_t[:, length : 2 * length] = own_values.T
        put(q_even, o_even)
        put(q_odd, o_odd)

    def far_project():
        idle = z == 0 if across.short else jnp.logical_not(is_cont)

        @pl.when(idle)
        def _():
            far[...] = jnp.zeros_like(far)

        keys[0:length, :] = dot(far[...], g_four[1]).astype(BF16)
        far_values = (dot(far[...], g_four[2]) + vec[1:2, :]).astype(BF16)
        values[0:length, :] = far_values
        values_t[:, 0:length] = far_values.T
        put(keys, o_keys)
        put(values, o_values)
        put(far, o_far)

    def own_pair(j):
        attend_own(j, q_even, q_odd, keys, values_t, bias, part_t, log_sums, part_sums)

    def far_pair(j):
        attend_far(j, q_even, q_odd, keys, values_t, bias, part_t, log_sums, part_sums, mixed_t)

    def after_attention():
        put(mixed_t, o_mixed)
        put(log_sums, o_logs)
        first = tok[...].astype(F32) + dot(mixed_t[...].T, g_four[3]) + vec[2:3, :]
        unit, inverse = normalize(first)
        unit1[...] = unit
        inverse1[...] = jnp.broadcast_to(inverse, inverse1.shape)
        normed[...] = unit * vec[3:4, :] + vec[4:5, :]
        low_ref[...] = normed[...].astype(BF16)
        low_t[...] = low_ref[...].T
        acc[...] = normed[...] + vec[5:6, :]
        put(g_four, o_four)

    chunks = inner.shape[2] // D

    def widen(c):
        cols = pl.ds(pl.multiple_of(c * D, D), D)
        hidden = dot(low_ref[...], g_inner[0, :, cols]) + vec[pl.ds(8 + c, 1), :]
        value, grad = gelu_pair(hidden)
        act[c] = value.astype(BF16)
        slope[c] = grad

    def narrow(c):
        rows = pl.ds(pl.multiple_of(c * D, D), D)
        acc[...] += dot(act[c], g_outer[0, rows, :])

    plan = PLAN_FOUR if p["depth"] == 4 and PLAN_FOUR else default_plan(p["depth"])
    run_plan(
        plan,
        comm,
        {"c1": own_project, "c2": far_project, "att": after_attention},
        {"o": (D // 128, own_pair), "p": (D // 128, far_pair), "a": (chunks, widen), "b": (chunks, narrow)},
    )
    unit, inverse = normalize(acc[...])
    normed[...] = unit * vec[6:7, :] + vec[7:8, :]
    put(normed, o_result)
    g = cot[...].astype(F32)
    small[...] = jnp.zeros_like(small)
    small[6:7, :] = column_total(g * unit)
    small[7:8, :] = column_total(g)
    g_second = normalize_back(g, vec[6:7, :], unit, inverse)
    g_out[...] = g_second.astype(BF16)
    small[5:6, :] = column_total(g_out[...].astype(F32))
    acc[...] = g_second

    def ff_back(c, carry):
        cols = pl.ds(pl.multiple_of(c * D, D), D)
        g_hidden = (dot(g_out[...], g_outer[0, cols, :], 1, 1) * slope[c]).astype(BF16)
        small[pl.ds(8 + c, 1), :] = column_total(g_hidden.astype(F32))
        acc[...] += dot(g_hidden, g_inner[0, :, cols], 1, 1)
        grad_wi[:, cols] = dot(low_t[...], g_hidden).astype(BF16)
        grad_wu[cols, :] = dot(act[c].T, g_out[...]).astype(BF16)
        return carry

    lax.fori_loop(0, chunks, ff_back, 0)
    put(grad_wu, o_wu)
    put(grad_wi, o_wi)
    g_normed = acc[...]
    small[3:4, :] = column_total(g_normed * unit1[...])
    small[4:5, :] = column_total(g_normed)
    acc[...] = normalize_back(g_normed, vec[3:4, :], unit1[...], inverse1[:, 0:1])
    put(acc, o_gfirst)
    put(small, o_small)
    for g in segments.values():
        g.drain()
    across.drain()
    for copy in pending:
        copy.wait()


def first_call(n, smalls, wide, tok, w_q, w_k, w_v, w_o, inner, outer, prompt_ids, cont_ids, offsets, cot):
    length = tok.shape[0]
    vmem = pl.BlockSpec(memory_space=pltpu.VMEM)
    smem = pl.BlockSpec(memory_space=pltpu.SMEM)
    hbm = pl.BlockSpec(memory_space=pl.ANY)
    sds = jax.ShapeDtypeStruct
    rows, ff = w_q.shape[0], inner.shape[2]
    chunks = ff // D
    outs = [
        sds((length, D), F32),
        sds((length, D), BF16),
        sds((length, D), BF16),
        sds((2 * length, D), BF16),
        sds((2 * length, D), BF16),
        sds((D, length), BF16),
        sds((H * 8, length), F32),
        sds((length, D), F32),
        sds((VEC_ROWS, D), F32),
        sds((ff, D), BF16),
        sds((D, ff), BF16),
        sds((4, D, D), BF16),
        sds((length, D), BF16),
    ]
    sems = 5 * (9 + 2) * (n // 4)
    return pl.pallas_call(
        partial(first_kernel, n),
        out_shape=outs,
        in_specs=[vmem] * 18 + [smem, vmem],
        out_specs=[hbm] * len(outs),
        scratch_shapes=[
            pltpu.VMEM((4, rows, D), BF16),
            pltpu.VMEM((1, VEC_ROWS, D), BF16),
            pltpu.VMEM((4, D, D), BF16),
            pltpu.VMEM((1, n * VEC_ROWS, D), BF16),
            pltpu.VMEM((1, D, ff), BF16),
            pltpu.VMEM((1, ff, D), BF16),
            pltpu.VMEM((length, D), BF16),
            pltpu.VMEM((length, D), BF16),
            pltpu.VMEM((length, D), BF16),
            pltpu.VMEM((2 * length, D), BF16),
            pltpu.VMEM((2 * length, D), BF16),
            pltpu.VMEM((D, length), BF16),
            pltpu.VMEM((H * 8, length), F32),
            pltpu.VMEM((VEC_ROWS, D), F32),
            pltpu.VMEM((ff, D), BF16),
            pltpu.VMEM((D, ff), BF16),
            pltpu.VMEM((2 * length, length), F32),
            pltpu.VMEM((D, 2 * length), BF16),
            pltpu.VMEM((VEC_ROWS, D), F32),
            pltpu.VMEM((length, D), F32),
            pltpu.VMEM((length, D), BF16),
            pltpu.VMEM((D, length), BF16),
            pltpu.VMEM((length, D), F32),
            pltpu.VMEM((length, 128), F32),
            pltpu.VMEM((length, D), F32),
            pltpu.VMEM((chunks, length, D), BF16),
            pltpu.VMEM((chunks, length, D), F32),
            pltpu.VMEM((length, D), BF16),
            pltpu.VMEM((1, length), jnp.int32),
            pltpu.VMEM((1, length), jnp.int32),
            pltpu.VMEM((length, 128), jnp.int32),
            pltpu.SemaphoreType.DMA((sems,)),
            pltpu.SemaphoreType.DMA((sems,)),
            pltpu.SemaphoreType.DMA((5,)),
            pltpu.VMEM((length, D), BF16),
            pltpu.VMEM((D, length), F32),
            pltpu.VMEM((H * 8, length), F32),
            pltpu.SemaphoreType.DMA((4 * Across.chunks,)),
            pltpu.SemaphoreType.DMA((4 * Across.chunks,)),
            pltpu.SemaphoreType.DMA((len(outs),)),
        ],
        compiler_params=pltpu.CompilerParams(
            collective_id=0, has_side_effects=True, vmem_limit_bytes=67043328
        ),
        name="forward_with_gather",
    )(*smalls, wide, tok, w_q, w_k, w_v, w_o, inner, outer, prompt_ids, cont_ids, offsets, cot)


class SmallSum:
    def __init__(self, place, total, slots, send, recv, base):
        self.p, self.total, self.slots = place, total, slots
        self.send, self.recv, self.base = send, recv, base

    def make(self, slot, where):
        return pltpu.make_async_remote_copy(
            src_ref=self.total,
            dst_ref=self.slots.at[slot],
            send_sem=self.send.at[self.base + slot],
            recv_sem=self.recv.at[self.base + slot],
            device_id=where,
            device_id_type=MESHID,
        )

    def stage(self, k):
        return self.make(k, (self.p["sibling"], self.p["near_x"], self.p["near_y"])[k])

    def begin(self):
        self.stage(0).start()

    def fold(self, k):
        copy = self.stage(k)
        copy.wait_send()
        copy.wait_recv()
        self.total[...] = self.total[...] + self.slots[k]
        if k < 2:
            self.stage(k + 1).start()
        else:
            self.along(lambda copy: copy.start())

    def along(self, act):
        p = self.p
        z, depth = p["z"], p["depth"]
        for d in range(1, depth):
            for sign in (1, -1):
                target = p["device"](p["r"], p["s"] + 4 * d * sign)
                slot = 3 + 2 * (d - 1) + (0 if sign == 1 else 1)
                ok = z + d < depth if sign == 1 else z - d >= 0
                pl.when(ok)(lambda slot=slot, target=target: act(self.make(slot, target)))

    def finish(self):
        p = self.p
        z, depth = p["z"], p["depth"]
        self.along(lambda copy: copy.wait_send())
        terms = []
        for d in range(1, depth):
            for sign in (1, -1):
                slot = 3 + 2 * (d - 1) + (0 if sign == 1 else 1)
                ok = z - d >= 0 if sign == 1 else z + d < depth
                pl.when(ok)(lambda slot=slot: self.make(slot, p["sibling"]).wait_recv())
        result = None
        for k in range(depth):
            if_own = self.total[...]
            value = if_own
            for d in range(1, depth):
                for sign in (1, -1):
                    slot = 3 + 2 * (d - 1) + (0 if sign == 1 else 1)
                    value = jnp.where(z - d * sign == k, self.slots[slot], value)
            result = value if result is None else result + value
        return result


SCATTER_FOUR = (
    ('give', 'U'),
    ('c', 'pre'),
    ('give', 'I'),
    ('load',),
    ('merge', 'U', 0),
    ('c', 'p0'),
    ('merge', 'U', 1),
    ('merge_diag', 'U', 0),
    ('c', 'p1'),
    ('merge', 'I', 0),
    ('merge_diag', 'U', 1),
    ('c', 'p2'),
    ('merge_side', 'U', 0),
    ('c', 'p3'),
    ('merge_diag', 'I', 0),
    ('merge', 'I', 2),
    ('merge', 'U', 2),
    ('merge_side', 'U', 1),
    ('merge', 'I', 1),
    ('c', 'p4'),
    ('merge_side', 'I', 0),
    ('c', 'p5'),
    ('c', 'term'),
    ('give', 'O'),
    ('back', 0),
    ('back', 1),
    ('merge_diag', 'U', 2),
    ('merge_diag', 'I', 1),
    ('c', 'wk'),
    ('give', 'K'),
    ('c', 'wv'),
    ('merge', 'I', 3),
    ('merge', 'O', 2),
    ('merge_diag', 'I', 2),
    ('c', 'wq'),
    ('give', 'Q'),
    ('merge_side', 'I', 1),
    ('merge', 'K', 2),
    ('merge', 'K', 0),
    ('pass', 0),
    ('give', 'W'),
    ('merge', 'O', 1),
    ('merge', 'W', 1),
    ('merge', 'W', 3),
    ('merge', 'Q', 0),
    ('merge', 'O', 0),
    ('back', 2),
    ('back', 3),
    ('merge_diag', 'O', 2),
    ('merge', 'Q', 1),
    ('merge', 'K', 1),
    ('merge', 'W', 0),
    ('merge', 'Q', 2),
    ('small', 0),
    ('merge', 'Q', 3),
    ('c', 'rows'),
    ('merge_side', 'I', 2),
    ('merge', 'K', 3),
    ('merge_diag', 'W', 1),
    ('merge_diag', 'K', 0),
    ('merge_diag', 'Q', 0),
    ('merge_diag', 'W', 0),
    ('merge_diag', 'Q', 1),
    ('merge_diag', 'K', 1),
    ('merge_diag', 'Q', 2),
    ('pass', 1),
    ('merge', 'W', 2),
    ('merge_side', 'U', 2),
    ('merge_diag', 'O', 0),
    ('merge', 'U', 3),
    ('merge_diag', 'K', 3),
    ('merge_side', 'K', 0),
    ('merge_diag', 'K', 2),
    ('merge_side', 'Q', 0),
    ('merge_diag', 'O', 1),
    ('merge_diag', 'W', 2),
    ('merge_side', 'W', 0),
    ('merge_diag', 'I', 3),
    ('merge', 'O', 3),
    ('merge_side', 'Q', 1),
    ('merge_diag', 'Q', 3),
    ('small', 1),
    ('merge_diag', 'W', 3),
    ('merge_side', 'O', 0),
    ('merge_side', 'K', 1),
    ('merge_diag', 'U', 3),
    ('pass', 2),
    ('merge_side', 'K', 2),
    ('merge_side', 'O', 1),
    ('merge_side', 'W', 1),
    ('merge_side', 'W', 2),
    ('merge_side', 'Q', 2),
    ('merge_side', 'O', 2),
    ('pass', 3),
    ('merge_side', 'I', 3),
    ('merge_diag', 'O', 3),
    ('small', 2),
    ('merge_side', 'K', 3),
    ('merge_side', 'Q', 3),
    ('merge_side', 'U', 3),
    ('merge_side', 'W', 3),
    ('merge_side', 'O', 3),
)


def default_scatter(depth):
    def steps(seg):
        out = []
        for i in range(depth + 2):
            if i < depth:
                out.append(("merge", seg, i))
            if 0 <= i - 1 < depth:
                out.append(("merge_diag", seg, i - 1))
            if 0 <= i - 2 < depth:
                out.append(("merge_side", seg, i - 2))
        return out

    plan = [("load",), ("give", "U"), ("give", "I"), ("c", "pre"), ("give", "O")]
    plan += [("c", "p%d" % i) for i in range(6)]
    plan += [("c", "term"), *[("back", j) for j in range(Across.chunks)], *[("pass", j) for j in range(Across.chunks)], ("c", "wq"), ("give", "Q"), ("c", "wk"), ("give", "K")]
    plan += [("c", "wv"), ("give", "W"), ("c", "rows"), ("small", 0), ("small", 1), ("small", 2)]
    for seg in "UIOQKW":
        plan += steps(seg)
    return plan


def second_kernel(n, *refs):
    (
        h_even,
        h_odd,
        h_keys,
        h_values,
        h_mixed,
        h_logs,
        h_gfirst,
        h_small,
        h_wu,
        h_wi,
        h_four,
        h_far,
        tok,
        prompt_ids,
        cont_ids,
        offsets,
    ) = refs[:16]
    out_wu, out_wi, out_wo, out_wq, out_wk, out_wv, g_rows, out_small, out_wide = refs[16:25]
    scratch = list(refs[25:])

    def take(count):
        part = scratch[:count]
        del scratch[:count]
        return part

    (
        q_even,
        q_odd,
        keys,
        values,
        mixed_t,
        log_sums,
        g_first,
        small,
        keep_wu,
        keep_wi,
        four,
        far,
    ) = take(12)
    grad_wo, grad_wq, grad_wk, grad_wv = take(4)
    (
        bias,
        keys_t,
        g_even,
        g_odd,
        delta,
        grad_qt,
        grad_k,
        grad_v,
        rows_t,
        row_label,
        row_limit,
        col_label,
        term,
        back,
        slots,
    ) = take(15)
    buffers = [take(4) for _ in range(6)]
    send, recv, load_sem, relay, back_send, back_recv, s_send, s_recv = scratch
    p = place_of(n)
    z, half, core = p["z"], p["half"], p["core"]
    length = tok.shape[0]
    loads = {}

    def mine(ref):
        width = ref.shape[1] // 2
        return ref.at[:, pl.ds(pl.multiple_of(core * width, width), width)]

    for i, (name, src, dst) in enumerate(
        (
            ("g_first", h_gfirst, g_first),
            ("four", h_four, four),
            ("mixed_t", h_mixed, mixed_t),
            ("small", h_small, small),
            ("keys", h_keys, keys),
            ("q_even", h_even, q_even),
            ("q_odd", h_odd, q_odd),
            ("values", h_values, values),
            ("log_sums", h_logs, log_sums),
            ("far", h_far, far),
            ("keep_wu", mine(h_wu), keep_wu),
            ("keep_wi", mine(h_wi), keep_wi),
        )
    ):
        loads[name] = pltpu.make_async_copy(src, dst, load_sem.at[i])
    for copy in loads.values():
        copy.start()
    entry_barrier(p)
    across = Across(p, term, back, relay, back_send, back_recv, False)
    segments = {}
    base = 0
    for name, given, grad, out, buf in (
        ("U", h_wu, keep_wu, out_wu, buffers[0]),
        ("I", h_wi, keep_wi, out_wi, buffers[1]),
        ("O", grad_wo, grad_wo, out_wo, buffers[2]),
        ("Q", grad_wq, grad_wq, out_wq, buffers[3]),
        ("K", grad_wk, grad_wk, out_wk, buffers[4]),
        ("W", grad_wv, grad_wv, out_wv, buffers[5]),
    ):
        segments[name] = Scatter(p, given, grad, out, *buf, send, recv, base)
        base += segments[name].count
    sums = SmallSum(p, small, slots, s_send, s_recv, 0)

    def comm(step):
        if step[0] == "load":
            loads["keep_wu"].wait()
            loads["keep_wi"].wait()
        elif step[0] == "give":
            for i in range(p["depth"]):
                segments[step[1]].give(i)
        elif step[0] == "back":
            across.begin(step[1])
        elif step[0] == "pass":
            across.onward(step[1])
        elif step[0] == "small":
            sums.fold(step[1])
        else:
            getattr(segments[step[1]], step[0])(step[2])

    def prepare():
        for name in ("g_first", "four", "mixed_t", "small"):
            loads[name].wait()
        g_branch = g_first[...].astype(BF16)
        small[2:3, :] = column_total(g_branch.astype(F32))
        grad_wo[...] = dot(mixed_t[...], g_branch).astype(BF16)
        g_mixed = dot(g_branch, four[3], 1, 1).astype(BF16)
        split_heads(g_mixed.astype(F32), g_even, g_odd)
        g_mixed_t = g_mixed.T
        for h in range(H):
            at = slice(h * DH, (h + 1) * DH)
            part = column_total(mixed_t[at, :].astype(F32) * g_mixed_t[at, :].astype(F32))
            delta[h * 8 : (h + 1) * 8, :] = jnp.broadcast_to(part, (8, length))
        labels_of(n, prompt_ids, cont_ids, offsets, row_label, row_limit, col_label)
        make_bias(bias, col_label, row_label, row_limit)
        for name in ("keys", "q_even", "q_odd", "values", "log_sums", "far"):
            loads[name].wait()
        keys_t[...] = keys[...].T
        rows_t[:, 0:length] = far[...].T
        rows_t[:, length : 2 * length] = tok[...].T

    def pair(j):
        attend_pair_back(
            j,
            q_even,
            q_odd,
            g_even,
            g_odd,
            keys,
            keys_t,
            values,
            bias,
            delta,
            log_sums,
            grad_qt,
            grad_k,
            grad_v,
        )

    def make_term():
        term[...] = (
            dot(grad_k[0:length, :], four[1], 1, 1) + dot(grad_v[0:length, :], four[2], 1, 1)
        ).astype(BF16)

    def query_weight():
        grad_q = grad_qt[...].T
        small[0:1, :] = column_total(grad_q.astype(F32))
        small[1:2, :] = column_total(grad_v[...].astype(F32))
        sums.begin()
        grad_wq[...] = dot(rows_t[:, length : 2 * length], grad_q).astype(BF16)

    def key_weight():
        grad_wk[...] = dot(rows_t[...], grad_k[...]).astype(BF16)

    def value_weight():
        grad_wv[...] = dot(rows_t[...], grad_v[...]).astype(BF16)

    def row_grads():
        g_rows[...] = (
            g_first[...]
            + dot(grad_qt[...].T, four[0], 1, 1)
            + dot(grad_k[length : 2 * length, :], four[1], 1, 1)
            + dot(grad_v[length : 2 * length, :], four[2], 1, 1)
        )

    plan = SCATTER_FOUR if p["depth"] == 4 and SCATTER_FOUR else default_scatter(p["depth"])
    run_plan(
        plan,
        comm,
        {
            "pre": prepare,
            "term": make_term,
            "wq": query_weight,
            "wk": key_weight,
            "wv": value_weight,
            "rows": row_grads,
        },
        {"p": (D // 128, pair)},
    )
    total = sums.finish()
    s = lax.axis_index("shard")
    part = out_small.shape[1]
    quarter = n // 4
    exact = lax.Precision.HIGHEST
    place = one_hot(part, D, s * part)
    out_small[...] = lax.dot_general(
        total[0:8, :], place, (((1,), (1,)), ((), ())), precision=exact, preferred_element_type=F32
    )
    place = one_hot(4 * part, D, (s % quarter) * 4 * part)
    wide = lax.dot_general(
        total[8:12, :], place, (((1,), (1,)), ((), ())), precision=exact, preferred_element_type=F32
    )
    row = lax.broadcasted_iota(jnp.int32, wide.shape, 0)
    out_wide[...] = column_total(jnp.where(row == s // quarter, wide, 0.0))
    for seg in segments.values():
        seg.finish()
    across.drain()
    across.arrived()

    @pl.when(z < half)
    def _():
        g_rows[...] = g_rows[...] + back[...].astype(F32)


def second_call(n, kept, tok, prompt_ids, cont_ids, offsets):
    length = tok.shape[0]
    depth = n // 4
    vmem = pl.BlockSpec(memory_space=pltpu.VMEM)
    smem = pl.BlockSpec(memory_space=pltpu.SMEM)
    hbm = pl.BlockSpec(memory_space=pl.ANY)
    sds = jax.ShapeDtypeStruct
    ff = kept[8].shape[0]
    shapes = [(ff // n, D), (D // n, ff)] + [(D // n, D)] * 4
    outs = [sds(s, F32) for s in shapes]
    outs += [sds((length, D), F32), sds((8, D // n), F32), sds((1, ff // n), F32)]
    scratch = [pltpu.VMEM(a.shape, a.dtype) for a in kept[:8]]
    scratch += [pltpu.VMEM((ff, D // 2), BF16), pltpu.VMEM((D, ff // 2), BF16)]
    scratch += [pltpu.VMEM(a.shape, a.dtype) for a in kept[10:]]
    scratch += [pltpu.VMEM((D, D), BF16)] * 4
    scratch += [
        pltpu.VMEM((2 * length, length), F32),
        pltpu.VMEM((D, 2 * length), BF16),
        pltpu.VMEM((length, D), BF16),
        pltpu.VMEM((length, D), BF16),
        pltpu.VMEM((H * 8, length), F32),
        pltpu.VMEM((D, length), BF16),
        pltpu.VMEM((2 * length, D), BF16),
        pltpu.VMEM((2 * length, D), BF16),
        pltpu.VMEM((D, 2 * length), BF16),
        pltpu.VMEM((1, length), jnp.int32),
        pltpu.VMEM((1, length), jnp.int32),
        pltpu.VMEM((length, 128), jnp.int32),
        pltpu.VMEM((length, D), BF16),
        pltpu.VMEM((length, D), BF16),
        pltpu.VMEM((3 + 2 * (depth - 1), VEC_ROWS, D), F32),
    ]
    for rows, cols in shapes:
        scratch += Scatter.scratch(n, rows, cols, BF16)
    sems = 6 * (1 + 7 * depth)
    small_sems = 3 + 2 * (depth - 1)
    scratch += [
        pltpu.SemaphoreType.DMA((sems,)),
        pltpu.SemaphoreType.DMA((sems,)),
        pltpu.SemaphoreType.DMA((12,)),
        pltpu.VMEM((length, D), BF16),
        pltpu.SemaphoreType.DMA((4 * Across.chunks,)),
        pltpu.SemaphoreType.DMA((4 * Across.chunks,)),
        pltpu.SemaphoreType.DMA((small_sems,)),
        pltpu.SemaphoreType.DMA((small_sems,)),
    ]
    return pl.pallas_call(
        partial(second_kernel, n),
        out_shape=outs,
        in_specs=[hbm] * 12 + [vmem] * 3 + [smem],
        out_specs=[vmem] * len(outs),
        scratch_shapes=scratch,
        compiler_params=pltpu.CompilerParams(
            collective_id=1, has_side_effects=True, vmem_limit_bytes=67043328
        ),
        name="backward_with_scatter",
    )(*kept, tok, prompt_ids, cont_ids, offsets)


def body(
    tokens,
    w_query,
    b_query,
    w_key,
    w_value,
    b_value,
    w_attout,
    b_attout,
    gain_first,
    beta_first,
    w_inner,
    b_inner,
    w_outer,
    b_outer,
    gain_second,
    beta_second,
    cotangent,
    prompt_ids,
    cont_ids,
    offsets,
):
    n = lax.axis_size("shard")
    reps = lax.axis_size("rep")
    small = (
        b_query,
        b_value,
        b_attout,
        gain_first,
        beta_first,
        b_outer,
        gain_second,
        beta_second,
    )
    outcome, *kept = first_call(
        n,
        [v[None] for v in small],
        b_inner[None],
        tokens,
        w_query,
        w_key,
        w_value,
        w_attout,
        w_inner[None],
        w_outer[None],
        prompt_ids,
        cont_ids,
        offsets,
        cotangent,
    )
    owned = list(second_call(n, kept, tokens, prompt_ids, cont_ids, offsets))
    grad_rows = owned.pop(6)
    if reps > 2:
        owned = [v * 0.5 for v in lax.psum(tuple(owned), "rep")]
    own_wu, own_wi, own_wo, own_wq, own_wk, own_wv, vectors, wide = owned
    s_bq, s_bv, s_bo, s_g1, s_be1, s_bu, s_g2, s_be2 = (vectors[i] for i in range(8))
    return (
        outcome,
        grad_rows,
        own_wq,
        s_bq,
        own_wk,
        own_wv,
        s_bv,
        own_wo,
        s_bo,
        s_g1,
        s_be1,
        own_wi,
        wide[0],
        own_wu,
        s_bu,
        s_g2,
        s_be2,
    )


def solution(mesh):
    return jax.shard_map(
        body,
        mesh=mesh,
        in_specs=(
            P(("rep", "shard"), None),
            P("shard", None),
            P("shard"),
            P("shard", None),
            P("shard", None),
            P("shard"),
            P("shard", None),
            P("shard"),
            P("shard"),
            P("shard"),
            P("shard", None),
            P("shard"),
            P("shard", None),
            P("shard"),
            P("shard"),
            P("shard"),
            P(("rep", "shard"), None),
            P(),
            P(),
            P(),
        ),
        out_specs=(
            P(("rep", "shard"), None),
            P(("rep", "shard"), None),
            P("shard", None),
            P("shard"),
            P("shard", None),
            P("shard", None),
            P("shard"),
            P("shard", None),
            P("shard"),
            P("shard"),
            P("shard"),
            P("shard", None),
            P("shard"),
            P("shard", None),
            P("shard"),
            P("shard"),
            P("shard"),
        ),
        check_vma=False,
    )
```

```python
from functools import partial

import jax
import jax.numpy as jnp
from jax import lax
from jax.experimental import pallas as pl
from jax.experimental.pallas import tpu as pltpu
from jax.sharding import PartitionSpec as P

D = 768
H = 12
DH = 64


EPSILON = 1e-12


MESHID = pl.DeviceIdType.MESH
BF16 = jnp.bfloat16
F32 = jnp.float32


def line_order(n):
    depth = n // 4
    order = []
    for z in range(depth):
        others = [k for k in range(depth) if k != z]
        others.sort(key=lambda k: (k // 2 != z // 2, abs(k - z), k))
        order.append([z] + others)
    return depth, order


def pick(table, z):
    out = table[-1]
    for i in range(len(table) - 2, -1, -1):
        out = jnp.where(z == i, table[i], out)
    return out


def place_of(n):
    depth, order = line_order(n)
    s = lax.axis_index("shard")
    r = lax.axis_index("rep")
    z, q = s // 4, s % 4
    y, x = q // 2, q % 2
    core = r % 2
    qx = y * 2 + 1 - x
    qy = (1 - y) * 2 + x
    qd = (1 - y) * 2 + 1 - x

    def device(rr, ss):
        return {"rep": rr, "shard": ss}

    half = depth // 2
    return dict(
        depth=depth,
        order=order,
        z=z,
        q=q,
        core=core,
        s=s,
        r=r,
        qx=qx,
        qy=qy,
        qd=qd,
        half=half,
        near_x=device(r, z * 4 + qx),
        near_y=device(r, z * 4 + qy),
        up=device(r, s + 4),
        down=device(r, s - 4),
        sibling=device(r + 1 - 2 * core, s),
        ahead=device(r, s + 4 * half),
        behind=device(r, s - 4 * half),
        device=device,
    )


def entry_barrier(p):
    bar = pltpu.get_barrier_semaphore()
    z, depth, half = p["z"], p["depth"], p["half"]

    def signal(where):
        pl.semaphore_signal(bar, inc=1, device_id=where, device_id_type=MESHID)

    signal(p["near_x"])
    signal(p["near_y"])
    signal(p["sibling"])
    pl.when(z + 1 < depth)(lambda: signal(p["up"]))
    pl.when(z > 0)(lambda: signal(p["down"]))
    pl.when(z < half)(lambda: signal(p["ahead"]))
    pl.when(z >= half)(lambda: signal(p["behind"]))
    pl.semaphore_wait(bar, 4 + jnp.where(z > 0, 1, 0) + jnp.where(z + 1 < depth, 1, 0))


def part_of(rows, quarter):
    top = (rows // 2 + 7) // 8 * 8
    if quarter is None:
        return 0, rows
    return (0, top) if quarter == 0 else (top, rows - top)


class Gather:
    def __init__(self, place, src, dst, send, recv, local, base):
        self.p, self.src, self.dst = place, src, dst
        self.rows, self.cols = src.shape[1], src.shape[2]
        self.send, self.recv, self.local, self.base = send, recv, local, base
        depth = place["depth"]
        self.names = {}
        for name in ("x", "y", "dx", "dy", "sx", "sy", "s0", "s1", "sz"):
            for i in range(depth):
                self.names[(name, i)] = len(self.names)
        self.line = len(self.names)
        self.count = self.line + 2 * depth

    def piece(self, chip, half, quarter=None):
        width = self.cols // 2
        cols = pl.ds(pl.multiple_of(half * width, width), width)
        first, size = part_of(self.rows, quarter)
        return self.dst.at[:, pl.ds(pl.multiple_of(chip * self.rows + first, 8), size), cols]

    def copy(self, sem, chip, where, quarter=None, own=False, half=None):
        half = self.p["core"] if half is None else half
        dst = self.piece(chip, half, quarter)
        src = dst
        if own:
            width = self.cols // 2
            src = self.src.at[:, :, pl.ds(pl.multiple_of(half * width, width), width)]
        i = self.base + (self.names[sem] if isinstance(sem, tuple) else self.line + sem)
        return pltpu.make_async_remote_copy(
            src_ref=src,
            dst_ref=dst,
            send_sem=self.send.at[i],
            recv_sem=self.recv.at[i],
            device_id=where,
            device_id_type=MESHID,
        )

    def item(self, i):
        return pick([line[i] for line in self.p["order"]], self.p["z"])

    def chips(self, i):
        k = self.item(i)
        p = self.p
        return tuple(k * 4 + p[name] for name in ("q", "qx", "qy", "qd"))

    def own_copy(self):
        me = self.p["s"]
        rows = pl.ds(pl.multiple_of(me * self.rows, self.rows), self.rows)
        return pltpu.make_async_copy(self.src, self.dst.at[:, rows, :], self.local)

    def start(self):
        p = self.p
        me, depth = p["s"], p["depth"]
        self.own_copy().start()
        pl.when(p["z"] + 1 < depth)(lambda: self.copy(0, me, p["up"], own=True).start())
        pl.when(p["z"] > 0)(lambda: self.copy(depth, me, p["down"], own=True).start())
        self.copy(("x", 0), me, p["near_x"], own=True).start()
        self.copy(("y", 0), me, p["near_y"], own=True).start()

    def flow(self, i):
        p = self.p
        z, s, depth = p["z"], p["s"], p["depth"]
        k = self.item(i)
        upward = k < z
        sem = jnp.where(upward, z - k - 1, depth + k - z - 1)
        onward = jnp.where(upward, z + 1 < depth, z > 0)
        target = p["device"](p["r"], jnp.where(upward, s + 4, s - 4))
        return sem, onward, target

    def take(self, i):
        p = self.p
        chip = self.chips(i)[0]
        sem, onward, target = self.flow(i)
        self.copy(sem, chip, p["sibling"]).wait_recv()
        pl.when(onward)(lambda: self.copy(sem + 1, chip, target).start())
        self.copy(("x", i), chip, p["near_x"]).start()
        self.copy(("y", i), chip, p["near_y"]).start()
        self.copy(("sz", i), chip, p["sibling"]).start()

    def spread(self, i):
        p = self.p
        _, cx, cy, _ = self.chips(i)
        self.copy(("x", i), cx, p["sibling"]).wait_recv()
        self.copy(("dy", i), cx, p["near_y"], quarter=0).start()
        self.copy(("sx", i), cx, p["sibling"]).start()
        self.copy(("y", i), cy, p["sibling"]).wait_recv()
        self.copy(("dx", i), cy, p["near_x"], quarter=1).start()
        self.copy(("sy", i), cy, p["sibling"]).start()

    def corner(self, i):
        p = self.p
        cd = self.chips(i)[3]
        self.copy(("dy", i), cd, p["sibling"], quarter=0).wait_recv()
        self.copy(("s0", i), cd, p["sibling"], quarter=0).start()
        self.copy(("dx", i), cd, p["sibling"], quarter=1).wait_recv()
        self.copy(("s1", i), cd, p["sibling"], quarter=1).start()

    def arrived(self):
        p = self.p
        other = 1 - p["core"]
        self.own_copy().wait()
        for i in range(p["depth"]):
            cm, cx, cy, cd = self.chips(i)
            if i:
                self.copy(("sz", i), cm, p["sibling"], half=other).wait_recv()
            self.copy(("sx", i), cx, p["sibling"], half=other).wait_recv()
            self.copy(("sy", i), cy, p["sibling"], half=other).wait_recv()
            self.copy(("s0", i), cd, p["sibling"], quarter=0, half=other).wait_recv()
            self.copy(("s1", i), cd, p["sibling"], quarter=1, half=other).wait_recv()

    def drain(self):
        p = self.p
        depth = p["depth"]
        me = p["s"]
        pl.when(p["z"] + 1 < depth)(lambda: self.copy(0, me, p["up"], own=True).wait_send())
        pl.when(p["z"] > 0)(lambda: self.copy(depth, me, p["down"], own=True).wait_send())
        for i in range(depth):
            cm, cx, cy, cd = self.chips(i)
            if i:
                sem, onward, target = self.flow(i)
                pl.when(onward)(
                    lambda sem=sem, target=target, cm=cm: self.copy(sem + 1, cm, target).wait_send()
                )
                self.copy(("sz", i), cm, p["sibling"]).wait_send()
            self.copy(("x", i), cm, p["near_x"]).wait_send()
            self.copy(("y", i), cm, p["near_y"]).wait_send()
            self.copy(("dy", i), cx, p["near_y"], quarter=0).wait_send()
            self.copy(("dx", i), cy, p["near_x"], quarter=1).wait_send()
            self.copy(("sx", i), cx, p["sibling"]).wait_send()
            self.copy(("sy", i), cy, p["sibling"]).wait_send()
            self.copy(("s0", i), cd, p["sibling"], quarter=0).wait_send()
            self.copy(("s1", i), cd, p["sibling"], quarter=1).wait_send()

    def early(self):
        return [
            self.start,
            partial(self.take, 1),
            partial(self.spread, 0),
            partial(self.spread, 1),
            partial(self.corner, 0),
            partial(self.corner, 1),
        ]

    def late(self):
        depth = self.p["depth"]
        steps = []
        for i in range(2, depth + 2):
            if i < depth:
                steps.append(partial(self.take, i))
            if 2 <= i - 1 < depth:
                steps.append(partial(self.spread, i - 1))
            if 2 <= i - 2 < depth:
                steps.append(partial(self.corner, i - 2))
        return steps


class Scatter:
    def __init__(self, place, given, grad, out, pair, diag, side, line, send, recv, base):
        self.p, self.given, self.grad, self.out = place, given, grad, out
        self.rows, self.cols = out.shape
        self.pair, self.diag, self.side, self.line = pair, diag, side, line
        self.send, self.recv, self.base = send, recv, base
        self.half = self.cols // 2
        core = place["core"]
        self.out_mine = pl.ds(pl.multiple_of(core * self.half, self.half), self.half)
        self.mine = self.out_mine if grad.shape[1] == self.cols else pl.ds(0, self.half)
        self.theirs = pl.ds(pl.multiple_of((1 - core) * self.half, self.half), self.half)
        depth = place["depth"]
        self.names = {}
        for name in ("p", "d0", "d1", "s0", "s1"):
            for i in range(depth):
                self.names[(name, i)] = len(self.names)
        self.names["o"] = len(self.names)
        self.first = len(self.names)
        self.count = self.first + 2 * depth

    @staticmethod
    def scratch(n, rows, cols, dtype):
        depth, h = n // 4, cols // 2
        return [
            pltpu.VMEM((n * rows, h), dtype),
            pltpu.VMEM((2 * depth, part_of(rows, 0)[1], h), dtype),
            pltpu.VMEM((2 * depth, rows, h), dtype),
            pltpu.VMEM((2 * depth - 2, rows, h), dtype),
        ]

    def make(self, sem, src, dst, where):
        i = self.base + sem
        return pltpu.make_async_remote_copy(
            src_ref=src,
            dst_ref=dst,
            send_sem=self.send.at[i],
            recv_sem=self.recv.at[i],
            device_id=where,
            device_id_type=MESHID,
        )

    def item(self, i):
        depth = self.p["depth"]
        return pick([line[depth - 1 - i] for line in self.p["order"]], self.p["z"])

    def rows_of(self, k, q, quarter=None):
        first, size = part_of(self.rows, quarter)
        return pl.ds(pl.multiple_of((k * 4 + q) * self.rows + first, 8), size)

    def pair_copy(self, i):
        r = self.rows * 4
        block = pl.ds(pl.multiple_of(self.item(i) * r, r), r)
        return self.make(
            self.names[("p", i)],
            self.given.at[block, self.theirs],
            self.pair.at[block, :],
            self.p["sibling"],
        )

    def diag_copy(self, i, quarter):
        p = self.p
        return self.make(
            self.names[("d0" if quarter == 0 else "d1", i)],
            self.grad.at[self.rows_of(self.item(i), p["qd"], quarter), self.mine],
            self.diag.at[i * 2 + quarter, pl.ds(0, part_of(self.rows, quarter)[1]), :],
            p["near_y"] if quarter == 0 else p["near_x"],
        )

    def side_copy(self, i, axis):
        p = self.p
        return self.make(
            self.names[("s0" if axis == 0 else "s1", i)],
            self.grad.at[self.rows_of(self.item(i), p["qx"] if axis == 0 else p["qy"]), self.mine],
            self.side.at[i * 2 + axis],
            p["near_x"] if axis == 0 else p["near_y"],
        )

    def line_copy(self, i):
        p = self.p
        k, z, depth = self.item(i), p["z"], p["depth"]
        slot = jnp.where(k > z, k - z - 1, depth - 1 + z - 1 - k)
        where = p["device"](p["r"], jnp.where(k > z, p["s"] + 4, p["s"] - 4))
        return self.make(
            self.first + slot,
            self.grad.at[self.rows_of(k, p["q"]), self.mine],
            self.line.at[slot],
            where,
        )

    def line_wait(self, slot):
        self.make(
            self.first + slot, self.line.at[slot], self.line.at[slot], self.p["sibling"]
        ).wait_recv()

    def out_copy(self, cols):
        return self.make(
            self.names["o"], self.out.at[:, cols], self.out.at[:, cols], self.p["sibling"]
        )

    def sweep(self, start, count, chunk, sources, store):
        def body(t, carry):
            at = pl.ds(pl.multiple_of(start + t * chunk, 8), chunk)
            low = pl.ds(pl.multiple_of(t * chunk, 8), chunk)
            total = self.grad[at, self.mine].astype(F32)
            for source in sources:
                total = total + source(at, low).astype(F32)
            store(at, low, total)
            return carry

        lax.fori_loop(0, count // chunk, body, 0)

    def store_grad(self, at, low, total):
        self.grad[at, self.mine] = total.astype(self.grad.dtype)

    def store_out(self, at, low, total):
        self.out[low, self.out_mine] = total

    def give(self, i):
        self.pair_copy(i).start()

    def merge(self, i):
        k = self.item(i)
        self.pair_copy(i).wait_recv()
        r4 = self.rows * 4
        self.sweep(k * r4, r4, 16, [lambda at, low: self.pair[at, :]], self.store_grad)
        self.diag_copy(i, 0).start()
        self.diag_copy(i, 1).start()

    def merge_diag(self, i):
        p = self.p
        k = self.item(i)
        for quarter, q in ((0, p["qx"]), (1, p["qy"])):
            self.diag_copy(i, quarter).wait_recv()
            slot = i * 2 + quarter
            first, size = part_of(self.rows, quarter)
            self.sweep(
                (k * 4 + q) * self.rows + first,
                size,
                8,
                [lambda at, low, slot=slot: self.diag[slot, low, :]],
                self.store_grad,
            )
            self.side_copy(i, quarter).start()

    def merge_side(self, i):
        p = self.p
        k, z, depth = self.item(i), p["z"], p["depth"]
        self.side_copy(i, 0).wait_recv()
        self.side_copy(i, 1).wait_recv()
        base = (k * 4 + p["q"]) * self.rows
        sides = [
            lambda at, low: self.side[i * 2, low, :],
            lambda at, low: self.side[i * 2 + 1, low, :],
        ]

        def total(slots, store):
            lines = [lambda at, low, slot=slot: self.line[slot, low, :] for slot in slots]
            self.sweep(base, self.rows, 16 if self.rows % 16 == 0 else 8, sides + lines, store)

        if i < depth - 1:
            has = ((k > z) & (z > 0)) | ((k < z) & (z + 1 < depth))
            slot = jnp.where(k > z, k - z, jnp.minimum(depth - 1 + z - k, 2 * depth - 3))

            @pl.when(has)
            def _():
                self.line_wait(slot)
                total([slot], self.store_grad)

            pl.when(jnp.logical_not(has))(lambda: total([], self.store_grad))
            self.line_copy(i).start()
        else:
            below, above = 0, depth - 1
            pl.when(z > 0)(lambda: self.line_wait(below))
            pl.when(z + 1 < depth)(lambda: self.line_wait(above))
            pl.when((z > 0) & (z + 1 < depth))(lambda: total([below, above], self.store_out))
            pl.when(z == 0)(lambda: total([above], self.store_out))
            pl.when(z + 1 == depth)(lambda: total([below], self.store_out))
            self.out_copy(self.out_mine).start()

    def finish(self):
        depth = self.p["depth"]
        self.out_copy(self.theirs).wait_recv()
        self.out_copy(self.out_mine).wait_send()
        for i in range(depth):
            self.pair_copy(i).wait_send()
            for side in (0, 1):
                self.diag_copy(i, side).wait_send()
                self.side_copy(i, side).wait_send()
            if i < depth - 1:
                self.line_copy(i).wait_send()

    def steps(self):
        depth = self.p["depth"]
        out = [lambda: [self.give(i) for i in range(depth)]]
        for i in range(depth + 2):
            if i < depth:
                out.append(partial(self.merge, i))
            if 0 <= i - 1 < depth:
                out.append(partial(self.merge_diag, i - 1))
            if 0 <= i - 2 < depth:
                out.append(partial(self.merge_side, i - 2))
        return out


def interleave(lists, skew, start=0):
    tagged = []
    for g, steps in enumerate(lists):
        for i, step in enumerate(steps):
            tagged.append((start + g * skew + i, g, i, step))
    tagged.sort(key=lambda entry: entry[:3])
    return [entry[3] for entry in tagged]


class Across:
    chunks = 4

    def __init__(self, place, src, dst, relay, send, recv, forward):
        p = place
        self.p, self.src, self.dst, self.relay = p, src, dst, relay
        self.send, self.recv = send, recv
        depth, z = p["depth"], p["z"]
        self.short = depth == 4
        self.at = z if forward else depth - 1 - z
        self.next = p["up"] if forward else p["down"]
        self.far = p["ahead"] if forward else p["behind"]

    def rows(self, j):
        size = self.src.shape[0] // self.chunks
        return pl.ds(j * size, size)

    def make(self, kind, j, src, dst, where):
        rows = self.rows(j)
        i = kind * self.chunks + j
        return pltpu.make_async_remote_copy(
            src_ref=src.at[rows],
            dst_ref=dst.at[rows],
            send_sem=self.send.at[i],
            recv_sem=self.recv.at[i],
            device_id=where,
            device_id_type=MESHID,
        )

    def begin(self, j):
        half = self.p["depth"] // 2
        if self.short:
            to_dst = self.make(0, j, self.src, self.dst, self.next)
            to_relay = self.make(1, j, self.src, self.relay, self.next)
            pl.when(self.at == 0)(lambda: to_dst.start())
            pl.when(self.at == 1)(lambda: to_relay.start())
        else:
            direct = self.make(0, j, self.src, self.dst, self.far)
            pl.when(self.at < half)(lambda: direct.start())

    def onward(self, j):
        if self.short:
            hold = self.make(0, j, self.src, self.dst, self.next)
            held = self.make(1, j, self.src, self.relay, self.next)
            from_dst = self.make(2, j, self.dst, self.dst, self.next)
            from_relay = self.make(3, j, self.relay, self.dst, self.next)

            @pl.when(self.at == 1)
            def _():
                hold.wait_recv()
                from_dst.start()

            @pl.when(self.at == 2)
            def _():
                held.wait_recv()
                from_relay.start()

    def arrived(self):
        half = self.p["depth"] // 2
        for j in range(self.chunks):
            if self.short:
                second = self.make(2, j, self.dst, self.dst, self.next)
                third = self.make(3, j, self.relay, self.dst, self.next)
                pl.when(self.at == 2)(lambda copy=second: copy.wait_recv())
                pl.when(self.at == 3)(lambda copy=third: copy.wait_recv())
            else:
                direct = self.make(0, j, self.src, self.dst, self.far)
                pl.when(self.at >= half)(lambda copy=direct: copy.wait_recv())

    def drain(self):
        half = self.p["depth"] // 2
        for j in range(self.chunks):
            if self.short:
                copies = (
                    self.make(0, j, self.src, self.dst, self.next),
                    self.make(1, j, self.src, self.relay, self.next),
                    self.make(2, j, self.dst, self.dst, self.next),
                    self.make(3, j, self.relay, self.dst, self.next),
                )
                pl.when(self.at == 0)(lambda: copies[0].wait_send())

                @pl.when(self.at == 1)
                def _():
                    copies[1].wait_send()
                    copies[2].wait_send()

                pl.when(self.at == 2)(lambda: copies[3].wait_send())
            else:
                direct = self.make(0, j, self.src, self.dst, self.far)
                pl.when(self.at < half)(lambda copy=direct: copy.wait_send())


VEC_ROWS = 16


def dot(a, b, ca=1, cb=0):
    return lax.dot_general(a, b, (((ca,), (cb,)), ((), ())), preferred_element_type=F32)


def mean_last(v):
    return jnp.sum(v, axis=-1, keepdims=True) * (1.0 / v.shape[-1])


def normalize(v):
    c = v - mean_last(v)
    inverse = lax.rsqrt(mean_last(c * c) + EPSILON)
    return c * inverse, inverse


def normalize_back(grad, gain, unit, inverse):
    g = grad * gain
    return inverse * (g - mean_last(g) - unit * mean_last(g * unit))


def gelu_pair(x):
    tail = jnp.exp(-0.5 * (x * x))
    t = 1.0 / (1.0 + (0.3275911 * 0.7071067811865476) * jnp.abs(x))
    poly = 1.061405429 * t - 1.453152027
    poly = poly * t + 1.421413741
    poly = poly * t - 0.284496736
    poly = poly * t + 0.254829592
    low = (0.5 * t) * poly * tail
    cdf = jnp.where(x < 0, low, 1.0 - low)
    return x * cdf, cdf + x * (tail * 0.3989422804014327)


def column_total(v):
    return jnp.sum(v, axis=0, keepdims=True)


def even_lanes(shape):
    return lax.broadcasted_iota(jnp.int32, shape, 1) % 128 < 64


def split_heads(x, even_ref, odd_ref):
    keep = even_lanes(x.shape)
    zero = jnp.zeros_like(x)
    even_ref[...] = jnp.where(keep, x, zero).astype(BF16)
    odd_ref[...] = jnp.where(keep, zero, x).astype(BF16)


def make_bias(bias, col_label, row_label, row_limit):
    length = row_label.shape[1]
    for b in range(0, length, 128):
        at = pl.ds(b, 128)
        row = lax.broadcasted_iota(jnp.int32, (128, length), 0) + b
        bias[at, :] = jnp.where(row < row_limit[...], 0.0, -1e30)
        same = col_label[at, 0:1] == row_label[...]
        bias[pl.ds(length + b, 128), :] = jnp.where(same, 0.0, -1e30)


def head_slices(j, side):
    head = pl.ds(pl.multiple_of(j * 128 + side * DH, DH), DH)
    row = pl.ds(pl.multiple_of(j * 16 + side * 8, 8), 8)
    return head, row


def part_block(part, j, side, b):
    index = j * 4 + side * 2 + b
    return part.at[
        pl.ds(pl.multiple_of(index // 3 * DH, DH), DH),
        pl.ds(pl.multiple_of(index % 3 * 256, 256), 256),
    ]


def attend_own(j, q_even, q_odd, keys, values_t, bias, part, tops, sums):
    lanes = pl.ds(pl.multiple_of(j * 128, 128), 128)
    length = q_even.shape[0]
    own = pl.ds(length, length)
    width = 256
    for b in range(0, length, width):
        block = pl.ds(b, width)
        for side, q_ref in ((0, q_even), (1, q_odd)):
            head, row = head_slices(j, side)
            scores = dot(keys[own, lanes], q_ref[block, lanes], 1, 1) + bias[own, block]
            top = jnp.max(scores, axis=0, keepdims=True)
            expo = jnp.exp(scores - top)
            part_block(part, j, side, b // width)[...] = dot(
                values_t[head, own], expo.astype(BF16)
            )
            tops[row, block] = jnp.broadcast_to(top, (8, width))
            sums[row, block] = jnp.broadcast_to(column_total(expo), (8, width))


def attend_far(j, q_even, q_odd, keys, values_t, bias, part, tops, sums, mixed_t):
    lanes = pl.ds(pl.multiple_of(j * 128, 128), 128)
    length = q_even.shape[0]
    far = pl.ds(0, length)
    width = 256
    for b in range(0, length, width):
        block = pl.ds(b, width)
        for side, q_ref in ((0, q_even), (1, q_odd)):
            head, row = head_slices(j, side)
            scores = dot(keys[far, lanes], q_ref[block, lanes], 1, 1) + bias[far, block]
            before = tops[row, block][0:1]
            top = jnp.maximum(jnp.max(scores, axis=0, keepdims=True), before)
            expo = jnp.exp(scores - top)
            fade = jnp.exp(before - top)
            total = sums[row, block][0:1] * fade + column_total(expo)
            mixed = part_block(part, j, side, b // width)[...] * fade + dot(values_t[head, far], expo.astype(BF16))
            mixed_t[head, block] = (mixed * (1.0 / total)).astype(BF16)
            tops[row, block] = jnp.broadcast_to(top + jnp.log(total), (8, width))


def attend_back(
    j, own, q_even, q_odd, g_even, g_odd, keys, keys_t, values, bias, delta, log_sums, part, grad_qt, grad_k, grad_v
):
    lanes = pl.ds(pl.multiple_of(j * 128, 128), 128)
    length = q_even.shape[0]
    half = pl.ds(length if own else 0, length)
    width = 256
    total_k, total_v = 0.0, 0.0
    for b in range(0, length, width):
        block = pl.ds(b, width)
        for side, q_ref, g_ref in ((0, q_even, g_even), (1, q_odd, g_odd)):
            head, row = head_slices(j, side)
            scores = dot(keys[half, lanes], q_ref[block, lanes], 1, 1) + bias[half, block]
            probs = jnp.exp(scores - log_sums[row, block][0:1])
            grad_p = dot(values[half, lanes], g_ref[block, lanes], 1, 1)
            grad_s = (probs * (grad_p - delta[row, block][0:1])).astype(BF16)
            total_v = total_v + dot(probs.astype(BF16), g_ref[block, lanes])
            total_k = total_k + dot(grad_s, q_ref[block, lanes])
            grad_q = dot(keys_t[head, half], grad_s)
            held = part_block(part, j, side, b // width)
            if own:
                grad_qt[head, block] = ((held[...] + grad_q) * 0.125).astype(BF16)
            else:
                held[...] = grad_q
    grad_k[half, lanes] = total_k.astype(BF16)
    grad_v[half, lanes] = total_v.astype(BF16)


def one_hot(rows, cols, shift):
    row = lax.broadcasted_iota(jnp.int32, (rows, cols), 0)
    col = lax.broadcasted_iota(jnp.int32, (rows, cols), 1)
    return jnp.where(col == row + shift, 1.0, 0.0)


def own_small(n, smalls, wide, out):
    s = lax.axis_index("shard")
    part = smalls[0].shape[1]
    quarter = n // 4
    out[...] = jnp.zeros_like(out)
    place = one_hot(part, D, s * part).astype(BF16)
    for i, v in enumerate(smalls):
        out[0, i : i + 1, :] = dot(v[...], place).astype(BF16)
    place = one_hot(4 * part, D, (s % quarter) * 4 * part).astype(BF16)
    piece = dot(wide[...], place)
    row = lax.broadcasted_iota(jnp.int32, (4, D), 0)
    out[0, 8:12, :] = jnp.where(row == s // quarter, piece, 0.0).astype(BF16)


def labels_of(n, prompt_ids, cont_ids, offsets, row_label, row_limit, col_label):
    half = n // 2
    s = lax.axis_index("shard")
    is_cont = s >= half
    group = lax.axis_index("rep") * half + s % half
    own = jnp.where(
        is_cont, cont_ids[pl.ds(group, 1), :], prompt_ids[pl.ds(group, 1), :]
    )
    limit = jnp.zeros_like(own)
    for k in range(offsets.shape[0]):
        limit = jnp.where(own == k, offsets[k, group], limit)
    row_label[...] = own
    row_limit[...] = jnp.where(is_cont, limit, 0)
    col_label[...] = jnp.broadcast_to(own, (128, own.shape[1])).T


PLAN_FOUR = (
    ('start', 'B'),
    ('start', 'V'),
    ('start', 'A'),
    ('spread', 'V', 0),
    ('take', 'V', 1),
    ('start', 'D'),
    ('take', 'A', 1),
    ('take', 'A', 2),
    ('take', 'V', 3),
    ('take', 'V', 2),
    ('take', 'B', 1),
    ('tok', 0),
    ('take', 'A', 3),
    ('start', 'C'),
    ('take', 'B', 2),
    ('spread', 'A', 1),
    ('spread', 'V', 3),
    ('spread', 'V', 1),
    ('pass', 0),
    ('spread', 'A', 0),
    ('tok', 1),
    ('spread', 'A', 3),
    ('spread', 'V', 2),
    ('spread', 'A', 2),
    ('take', 'C', 2),
    ('take', 'B', 3),
    ('take', 'D', 1),
    ('tok', 2),
    ('corner', 'V', 0),
    ('take', 'D', 2),
    ('corner', 'V', 1),
    ('corner', 'A', 0),
    ('spread', 'B', 0),
    ('corner', 'A', 3),
    ('corner', 'V', 3),
    ('corner', 'V', 2),
    ('take', 'C', 1),
    ('war', 'V'),
    ('corner', 'A', 1),
    ('corner', 'A', 2),
    ('spread', 'B', 2),
    ('spread', 'B', 1),
    ('tok', 3),
    ('pass', 1),
    ('war', 'A'),
    ('c', 'c1'),
    ('take', 'D', 3),
    ('c', 'o0'),
    ('c', 'o1'),
    ('pass', 2),
    ('c', 'o2'),
    ('c', 'o3'),
    ('spread', 'B', 3),
    ('take', 'C', 3),
    ('spread', 'C', 0),
    ('pass', 3),
    ('spread', 'D', 1),
    ('c', 'o4'),
    ('corner', 'B', 0),
    ('spread', 'C', 1),
    ('corner', 'B', 2),
    ('spread', 'D', 0),
    ('c', 'o5'),
    ('corner', 'B', 1),
    ('corner', 'B', 3),
    ('spread', 'C', 2),
    ('war', 'B'),
    ('spread', 'D', 2),
    ('spread', 'D', 3),
    ('wtok',),
    ('c', 'c2'),
    ('c', 'p0'),
    ('c', 'p1'),
    ('corner', 'D', 1),
    ('c', 'p2'),
    ('c', 'p3'),
    ('c', 'p4'),
    ('spread', 'C', 3),
    ('corner', 'C', 2),
    ('corner', 'C', 1),
    ('corner', 'C', 0),
    ('c', 'p5'),
    ('c', 'att'),
    ('corner', 'D', 2),
    ('corner', 'D', 0),
    ('corner', 'D', 3),
    ('war', 'D'),
    ('corner', 'C', 3),
    ('war', 'C'),
    ('c', 'a0'),
    ('c', 'a1'),
    ('c', 'a2'),
    ('c', 'a3'),
    ('c', 'b0'),
    ('c', 'b1'),
    ('c', 'b2'),
    ('c', 'b3'),
    ('c', 'ln2'),
    ('c', 'f0'),
    ('give', 'U', 0),
    ('c', 'f1'),
    ('give', 'U', 1),
    ('merge', 'U', 0),
    ('c', 'f2'),
    ('merge', 'U', 1),
    ('merge_diag', 'U', 0),
    ('c', 'f3'),
    ('give', 'I', 0),
    ('give', 'U', 2),
    ('give', 'I', 1),
    ('give', 'I', 2),
    ('merge_diag', 'U', 1),
    ('c', 'pre'),
    ('merge_side', 'U', 0),
    ('give', 'O', 0),
    ('merge', 'I', 0),
    ('give', 'I', 3),
    ('merge', 'U', 2),
    ('c', 'x0'),
    ('c', 'x1'),
    ('merge_side', 'U', 1),
    ('give', 'U', 3),
    ('merge_diag', 'I', 0),
    ('c', 'x2'),
    ('merge_diag', 'U', 2),
    ('c', 'x3'),
    ('c', 'x4'),
    ('merge_side', 'I', 0),
    ('give', 'O', 1),
    ('merge', 'I', 1),
    ('c', 'x5'),
    ('c', 'term'),
    ('back', 0),
    ('merge', 'O', 0),
    ('give', 'O', 2),
    ('merge', 'I', 3),
    ('merge', 'U', 3),
    ('back', 1),
    ('merge', 'I', 2),
    ('merge_diag', 'I', 1),
    ('c', 'y0'),
    ('c', 'y1'),
    ('back', 2),
    ('c', 'y2'),
    ('c', 'y3'),
    ('merge', 'O', 1),
    ('merge_diag', 'I', 2),
    ('back', 3),
    ('c', 'y4'),
    ('merge_side', 'U', 2),
    ('merge_diag', 'I', 3),
    ('c', 'y5'),
    ('c', 'rows'),
    ('merge', 'O', 2),
    ('onward', 0),
    ('merge_diag', 'O', 1),
    ('c', 'wq'),
    ('merge_diag', 'O', 0),
    ('give', 'Q', 0),
    ('give', 'Q', 1),
    ('c', 'wk'),
    ('give', 'K', 0),
    ('merge', 'Q', 0),
    ('small', 0),
    ('merge', 'Q', 1),
    ('give', 'Q', 2),
    ('c', 'wv'),
    ('give', 'K', 1),
    ('merge', 'K', 0),
    ('give', 'W', 0),
    ('give', 'O', 3),
    ('merge_diag', 'O', 2),
    ('give', 'W', 1),
    ('give', 'W', 2),
    ('give', 'W', 3),
    ('give', 'K', 2),
    ('onward', 1),
    ('merge_side', 'I', 1),
    ('merge_diag', 'Q', 0),
    ('small', 1),
    ('merge_side', 'I', 2),
    ('merge', 'W', 0),
    ('merge', 'Q', 2),
    ('merge', 'K', 1),
    ('merge_diag', 'K', 0),
    ('merge', 'K', 2),
    ('merge_diag', 'W', 0),
    ('small', 2),
    ('merge_diag', 'K', 1),
    ('merge_side', 'O', 0),
    ('merge_side', 'K', 0),
    ('give', 'K', 3),
    ('merge', 'W', 1),
    ('merge', 'W', 2),
    ('merge_side', 'Q', 0),
    ('give', 'Q', 3),
    ('merge_diag', 'Q', 1),
    ('merge_side', 'W', 0),
    ('merge_diag', 'Q', 2),
    ('onward', 2),
    ('merge_diag', 'K', 2),
    ('merge_diag', 'W', 2),
    ('merge_side', 'Q', 1),
    ('merge_side', 'K', 1),
    ('merge_diag', 'W', 1),
    ('merge', 'O', 3),
    ('merge', 'Q', 3),
    ('merge_side', 'O', 1),
    ('merge', 'K', 3),
    ('merge_side', 'O', 2),
    ('merge_side', 'K', 2),
    ('merge_diag', 'U', 3),
    ('merge_side', 'Q', 2),
    ('merge_diag', 'O', 3),
    ('merge', 'W', 3),
    ('merge_side', 'W', 1),
    ('merge_diag', 'Q', 3),
    ('merge_side', 'W', 2),
    ('onward', 3),
    ('merge_diag', 'K', 3),
    ('merge_diag', 'W', 3),
    ('merge_side', 'O', 3),
    ('merge_side', 'I', 3),
    ('merge_side', 'U', 3),
    ('merge_side', 'Q', 3),
    ('merge_side', 'K', 3),
    ('merge_side', 'W', 3),
)


def default_plan(depth):
    plan = [("start", "V"), ("start", "A")]
    plan += [("tok", j) for j in range(Across.chunks)]
    plan += [("pass", j) for j in range(Across.chunks)]
    for seg in "VABCD":
        if seg in "BCD":
            plan.append(("start", seg))
        for i in range(depth):
            if i:
                plan.append(("take", seg, i))
            plan.append(("spread", seg, i))
            if i:
                plan.append(("corner", seg, i - 1))
        plan.append(("corner", seg, depth - 1))
        plan.append(("war", seg))
    plan += [("wtok",), ("c", "c1")] + [("c", "o%d" % i) for i in range(6)] + [("c", "c2")]
    plan += [("c", "p%d" % i) for i in range(6)] + [("c", "att")]
    plan += [("c", "a%d" % i) for i in range(4)] + [("c", "b%d" % i) for i in range(4)]
    plan += [("c", "ln2")] + [("c", "f%d" % i) for i in range(4)] + [("c", "pre")]
    plan += [("give", s, i) for s in "UIO" for i in range(depth)]
    plan += [("c", "x%d" % i) for i in range(6)] + [("c", "term")]
    plan += [("back", j) for j in range(Across.chunks)]
    plan += [("onward", j) for j in range(Across.chunks)]
    plan += [("c", "y%d" % i) for i in range(6)]
    plan += [("c", "rows"), ("c", "wq"), ("c", "wk"), ("c", "wv")]
    plan += [("give", s, i) for s in "QKW" for i in range(depth)]
    plan += [("small", j) for j in range(3)]
    for seg in "UIOQKW":
        for i in range(depth + 2):
            if i < depth:
                plan.append(("merge", seg, i))
            if 0 <= i - 1 < depth:
                plan.append(("merge_diag", seg, i - 1))
            if 0 <= i - 2 < depth:
                plan.append(("merge_side", seg, i - 2))
    return plan


def run_plan(plan, comm, single, loops):
    at = 0
    while at < len(plan):
        step = plan[at]
        if step[0] != "c":
            comm(step)
            at += 1
        elif step[1] in single:
            single[step[1]]()
            at += 1
        else:
            kind = step[1][0]
            count, chunk = loops[kind]
            after = []
            for _ in range(count):
                at += 1
                steps = []
                last = len(after) == count - 1
                while not last and plan[at][0] != "c":
                    steps.append(plan[at])
                    at += 1
                after.append(steps)

            def body(j, carry, after=after, chunk=chunk):
                chunk(j)
                for k, steps in enumerate(after):
                    if steps:

                        @pl.when(j == k)
                        def _():
                            for step in steps:
                                comm(step)

                return carry

            lax.fori_loop(0, count, body, 0)


class SmallSum:
    def __init__(self, place, total, slots, send, recv, base):
        self.p, self.total, self.slots = place, total, slots
        self.send, self.recv, self.base = send, recv, base

    def make(self, slot, where):
        return pltpu.make_async_remote_copy(
            src_ref=self.total,
            dst_ref=self.slots.at[slot],
            send_sem=self.send.at[self.base + slot],
            recv_sem=self.recv.at[self.base + slot],
            device_id=where,
            device_id_type=MESHID,
        )

    def stage(self, k):
        return self.make(k, (self.p["sibling"], self.p["near_x"], self.p["near_y"])[k])

    def begin(self):
        self.stage(0).start()

    def fold(self, k):
        copy = self.stage(k)
        copy.wait_send()
        copy.wait_recv()
        self.total[...] = self.total[...] + self.slots[k]
        if k < 2:
            self.stage(k + 1).start()
        else:
            self.along(lambda copy: copy.start())

    def along(self, act):
        p = self.p
        z, depth = p["z"], p["depth"]
        for d in range(1, depth):
            for sign in (1, -1):
                target = p["device"](p["r"], p["s"] + 4 * d * sign)
                slot = 3 + 2 * (d - 1) + (0 if sign == 1 else 1)
                ok = z + d < depth if sign == 1 else z - d >= 0
                pl.when(ok)(lambda slot=slot, target=target: act(self.make(slot, target)))

    def finish(self):
        p = self.p
        z, depth = p["z"], p["depth"]
        self.along(lambda copy: copy.wait_send())
        terms = []
        for d in range(1, depth):
            for sign in (1, -1):
                slot = 3 + 2 * (d - 1) + (0 if sign == 1 else 1)
                ok = z - d >= 0 if sign == 1 else z + d < depth
                pl.when(ok)(lambda slot=slot: self.make(slot, p["sibling"]).wait_recv())
        result = None
        for k in range(depth):
            if_own = self.total[...]
            value = if_own
            for d in range(1, depth):
                for sign in (1, -1):
                    slot = 3 + 2 * (d - 1) + (0 if sign == 1 else 1)
                    value = jnp.where(z - d * sign == k, self.slots[slot], value)
            result = value if result is None else result + value
        return result


def scratch_of(n, length, ff):
    depth, rows = n // 4, D // n
    chunks = ff // D
    vmem, dma = pltpu.VMEM, pltpu.SemaphoreType.DMA
    gather_sems = 5 * 11 * depth
    scatter_sems = 6 * (1 + 7 * depth)
    slots = 3 + 2 * (depth - 1)
    across = 4 * Across.chunks
    spec = dict(
        four=vmem((4, rows, D), BF16),
        vecs=vmem((1, VEC_ROWS, D), BF16),
        g_four=vmem((4, D, D), BF16),
        g_vecs=vmem((1, n * VEC_ROWS, D), BF16),
        g_inner=vmem((1, D, ff), BF16),
        g_outer=vmem((1, ff, D), BF16),
        far=vmem((length, D), BF16),
        back=vmem((length, D), BF16),
        relay=vmem((length, D), BF16),
        q_even=vmem((length, D), BF16),
        q_odd=vmem((length, D), BF16),
        keys=vmem((2 * length, D), BF16),
        values=vmem((2 * length, D), BF16),
        turned=vmem((D, 2 * length), BF16),
        rows_t=vmem((D, 2 * length), BF16),
        mixed_t=vmem((D, length), BF16),
        log_sums=vmem((H * 8, length), F32),
        part_sums=vmem((H * 8, length), F32),
        small=vmem((VEC_ROWS, D), F32),
        slots=vmem((slots, VEC_ROWS, D), F32),
        bias=vmem((2 * length, length), F32),
        vec=vmem((VEC_ROWS, D), F32),
        normed=vmem((length, D), F32),
        unit1=vmem((length, D), F32),
        acc=vmem((length, D), F32),
        low_ref=vmem((length, D), BF16),
        low_t=vmem((D, length), BF16),
        g_out=vmem((length, D), BF16),
        act=vmem((chunks * length, D), BF16),
        slope=vmem((chunks * length, D), BF16),
        row_label=vmem((1, length), jnp.int32),
        row_limit=vmem((1, length), jnp.int32),
        col_label=vmem((length, 128), jnp.int32),
        send=dma((gather_sems,)),
        recv=dma((gather_sems,)),
        local=dma((5,)),
        far_send=dma((across,)),
        far_recv=dma((across,)),
        back_send=dma((across,)),
        back_recv=dma((across,)),
        sum_send=dma((slots,)),
        sum_recv=dma((slots,)),
        s_send=dma((scatter_sems,)),
        s_recv=dma((scatter_sems,)),
        hbm_sem=dma((7,)),
    )
    shapes = dict(U=(ff // n, D), I=(rows, ff), O=(rows, D), Q=(rows, D), K=(rows, D), W=(rows, D))
    for seg, (r, cols) in shapes.items():
        for name, buffer in zip("pdsl", Scatter.scratch(n, r, cols, BF16)):
            spec[seg + name] = buffer
    return spec, shapes


def layer_kernel(n, names, *refs):
    smalls = refs[0:8]
    (wide, tok, w_q, w_k, w_v, w_o, inner, outer, prompt_ids, cont_ids, offsets, h_cot) = refs[8:20]
    (out_wu, out_wi, out_wo, out_wq, out_wk, out_wv, out_small, out_wide, h_result, h_rows) = refs[20:30]
    b = dict(zip(names, refs[30:]))
    g_four, g_inner, g_outer, far, small = (
        b[k] for k in ("g_four", "g_inner", "g_outer", "far", "small")
    )
    q_even, q_odd, keys, values, turned, rows_t = (
        b[k] for k in ("q_even", "q_odd", "keys", "values", "turned", "rows_t")
    )
    mixed_t, log_sums, part_sums, bias, vec = (
        b[k] for k in ("mixed_t", "log_sums", "part_sums", "bias", "vec")
    )
    normed, unit1, acc, low_ref, low_t, g_out, act, slope = (
        b[k] for k in ("normed", "unit1", "acc", "low_ref", "low_t", "g_out", "act", "slope")
    )
    p = place_of(n)
    z, half, depth = p["z"], p["half"], p["depth"]
    length = tok.shape[0]
    chunks = inner.shape[2] // D
    cot_copy = pltpu.make_async_copy(h_cot, g_out, b["hbm_sem"].at[0])
    cot_copy.start()
    stacked = [
        pltpu.make_async_copy(w, b["four"].at[i], b["hbm_sem"].at[3 + i])
        for i, w in enumerate((w_q, w_k, w_v, w_o))
    ]
    for copy in stacked:
        copy.start()
    own_small(n, smalls, wide, b["vecs"])
    entry_barrier(p)
    for copy in stacked:
        copy.wait()
    forth = Across(p, tok, far, b["relay"], b["far_send"], b["far_recv"], True)
    term = far
    home = Across(p, term, b["back"], b["relay"], b["back_send"], b["back_recv"], False)
    segments = {}
    base = 0
    for j, (name, src, dst) in enumerate(
        (
            ("V", b["vecs"], b["g_vecs"]),
            ("A", b["four"].at[0:3], g_four.at[0:3]),
            ("B", b["four"].at[3:4], g_four.at[3:4]),
            ("C", inner, g_inner),
            ("D", outer, g_outer),
        )
    ):
        segments[name] = Gather(p, src, dst, b["send"], b["recv"], b["local"].at[j], base)
        base += segments[name].count
    base = 0
    for name, grad, out in (
        ("U", g_outer.at[0], out_wu),
        ("I", g_inner.at[0], out_wi),
        ("O", g_four.at[3], out_wo),
        ("Q", g_four.at[0], out_wq),
        ("K", g_four.at[1], out_wk),
        ("W", g_four.at[2], out_wv),
    ):
        buffers = [b[name + kind] for kind in "pdsl"]
        segments[name] = Scatter(p, grad, grad, out, *buffers, b["s_send"], b["s_recv"], base)
        base += segments[name].count
    sums = SmallSum(p, small, b["slots"], b["sum_send"], b["sum_recv"], 0)

    def comm(step):
        kind = step[0]
        if kind == "tok":
            forth.begin(step[1])
        elif kind == "pass":
            forth.onward(step[1])
        elif kind == "wtok":
            forth.arrived()
        elif kind == "back":
            home.begin(step[1])
        elif kind == "onward":
            home.onward(step[1])
        elif kind == "small":
            sums.fold(step[1])
        elif kind == "start":
            segments[step[1]].start()
        elif kind == "war":
            segments[step[1]].arrived()
        else:
            getattr(segments[step[1]], kind)(step[2])

    def own_project():
        labels_of(n, prompt_ids, cont_ids, offsets, b["row_label"], b["row_limit"], b["col_label"])
        make_bias(bias, b["col_label"], b["row_label"], b["row_limit"])
        vec[...] = jnp.zeros_like(vec)

        def add_vec(i, c):
            at = pl.ds(pl.multiple_of(i * VEC_ROWS, 16), VEC_ROWS)
            vec[...] += b["g_vecs"][0, at, :].astype(F32)
            return c

        lax.fori_loop(0, n, add_vec, 0)
        query = (dot(tok[...], g_four[0]) + vec[0:1, :]).astype(BF16)
        split_heads(query.astype(F32) * 0.125, q_even, q_odd)
        keys[length : 2 * length, :] = dot(tok[...], g_four[1]).astype(BF16)
        own_values = (dot(tok[...], g_four[2]) + vec[1:2, :]).astype(BF16)
        values[length : 2 * length, :] = own_values
        turned[:, length : 2 * length] = own_values.T
        rows_t[:, length : 2 * length] = tok[...].T

    def own_pair(j):
        attend_own(j, q_even, q_odd, keys, turned, bias, acc, log_sums, part_sums)

    def far_project():
        idle = z == 0 if forth.short else z < half

        @pl.when(idle)
        def _():
            far[...] = jnp.zeros_like(far)

        keys[0:length, :] = dot(far[...], g_four[1]).astype(BF16)
        far_values = (dot(far[...], g_four[2]) + vec[1:2, :]).astype(BF16)
        values[0:length, :] = far_values
        turned[:, 0:length] = far_values.T

    def far_pair(j):
        attend_far(j, q_even, q_odd, keys, turned, bias, acc, log_sums, part_sums, mixed_t)

    def after_attention():
        first = tok[...].astype(F32) + dot(mixed_t[...].T, g_four[3]) + vec[2:3, :]
        unit1[...] = first
        unit, _ = normalize(first)
        normed[...] = unit * vec[3:4, :] + vec[4:5, :]
        low_ref[...] = normed[...].astype(BF16)
        low_t[...] = low_ref[...].T
        acc[...] = normed[...] + vec[5:6, :]

    def chunk_of(c):
        return (
            pl.ds(pl.multiple_of(c * D, D), D),
            pl.ds(pl.multiple_of(c * length, length), length),
        )

    def widen(c):
        cols, at = chunk_of(c)
        hidden = dot(low_ref[...], g_inner[0, :, cols]) + vec[pl.ds(8 + c, 1), :]
        value, grad = gelu_pair(hidden)
        act[at, :] = value.astype(BF16)
        slope[at, :] = grad.astype(BF16)

    def narrow(c):
        cols, at = chunk_of(c)
        acc[...] += dot(act[at, :], g_outer[0, cols, :])

    result_copy = pltpu.make_async_copy(normed, h_result, b["hbm_sem"].at[1])

    def second_norm():
        for name in "VABCD":
            segments[name].drain()
        forth.drain()
        cot_copy.wait()
        unit, inverse = normalize(acc[...])
        normed[...] = unit * vec[6:7, :] + vec[7:8, :]
        result_copy.start()
        g = g_out[...].astype(F32)
        small[...] = jnp.zeros_like(small)
        small[6:7, :] = column_total(g * unit)
        small[7:8, :] = column_total(g)
        g_second = normalize_back(g, vec[6:7, :], unit, inverse)
        g_out[...] = g_second.astype(BF16)
        small[5:6, :] = column_total(g_out[...].astype(F32))
        acc[...] = g_second

    def ff_back(j):
        c = pick([segments["U"].item(i) for i in range(depth)], j) if depth == chunks else j
        cols, at = chunk_of(c)
        g_hidden = dot(g_out[...], g_outer[0, cols, :], 1, 1) * slope[at, :].astype(F32)
        g_hidden = g_hidden.astype(BF16)
        small[pl.ds(8 + c, 1), :] = column_total(g_hidden.astype(F32))
        acc[...] += dot(g_hidden, g_inner[0, :, cols], 1, 1)
        g_outer[0, cols, :] = dot(act[at, :].T, g_out[...]).astype(BF16)
        g_inner[0, :, cols] = dot(low_t[...], g_hidden).astype(BF16)

    g_even, g_odd, delta, grad_qt = low_ref, g_out, part_sums, low_t
    grad_k = act.at[pl.ds(0, 2 * length)]
    grad_v = act.at[pl.ds(2 * length, 2 * length)]

    def prepare():
        g_normed = acc[...]
        unit, inverse = normalize(unit1[...])
        small[3:4, :] = column_total(g_normed * unit)
        small[4:5, :] = column_total(g_normed)
        g_first = normalize_back(g_normed, vec[3:4, :], unit, inverse)
        acc[...] = g_first
        g_branch = g_first.astype(BF16)
        small[2:3, :] = column_total(g_branch.astype(F32))
        g_mixed = dot(g_branch, g_four[3], 1, 1).astype(BF16)
        g_four[3] = dot(mixed_t[...], g_branch).astype(BF16)
        split_heads(g_mixed.astype(F32), g_even, g_odd)
        g_mixed_t = g_mixed.T
        for h in range(H):
            at = slice(h * DH, (h + 1) * DH)
            part = column_total(mixed_t[at, :].astype(F32) * g_mixed_t[at, :].astype(F32))
            delta[h * 8 : (h + 1) * 8, :] = jnp.broadcast_to(part, (8, length))
        turned[...] = keys[...].T
        rows_t[:, 0:length] = far[...].T

    def pair_back(own, j):
        attend_back(
            j,
            own,
            q_even,
            q_odd,
            g_even,
            g_odd,
            keys,
            turned,
            values,
            bias,
            delta,
            log_sums,
            unit1,
            grad_qt,
            grad_k,
            grad_v,
        )

    def make_term():
        term[...] = (
            dot(grad_k[0:length, :], g_four[1], 1, 1) + dot(grad_v[0:length, :], g_four[2], 1, 1)
        ).astype(BF16)

    def row_grads():
        grad_q = grad_qt[...].T
        unit1[...] = (
            acc[...]
            + dot(grad_q, g_four[0], 1, 1)
            + dot(grad_k[length : 2 * length, :], g_four[1], 1, 1)
            + dot(grad_v[length : 2 * length, :], g_four[2], 1, 1)
        )
        small[0:1, :] = column_total(grad_q.astype(F32))
        small[1:2, :] = column_total(grad_v[...].astype(F32))
        sums.begin()

    def query_weight():
        g_four[0] = dot(rows_t[:, length : 2 * length], grad_qt[...].T).astype(BF16)

    def key_weight():
        g_four[1] = dot(rows_t[...], grad_k[...]).astype(BF16)

    def value_weight():
        g_four[2] = dot(rows_t[...], grad_v[...]).astype(BF16)

    plan = PLAN_FOUR if depth == 4 and PLAN_FOUR else default_plan(depth)
    pairs = D // 128
    run_plan(
        plan,
        comm,
        {
            "c1": own_project,
            "c2": far_project,
            "att": after_attention,
            "ln2": second_norm,
            "pre": prepare,
            "term": make_term,
            "rows": row_grads,
            "wq": query_weight,
            "wk": key_weight,
            "wv": value_weight,
        },
        {
            "o": (pairs, own_pair),
            "p": (pairs, far_pair),
            "a": (chunks, widen),
            "b": (chunks, narrow),
            "f": (chunks, ff_back),
            "x": (pairs, partial(pair_back, False)),
            "y": (pairs, partial(pair_back, True)),
        },
    )
    total = sums.finish()
    s = lax.axis_index("shard")
    part = out_small.shape[1]
    quarter = n // 4
    exact = lax.Precision.HIGHEST
    place = one_hot(part, D, s * part)
    out_small[...] = lax.dot_general(
        total[0:8, :], place, (((1,), (1,)), ((), ())), precision=exact, preferred_element_type=F32
    )
    place = one_hot(4 * part, D, (s % quarter) * 4 * part)
    wide_sum = lax.dot_general(
        total[8:12, :], place, (((1,), (1,)), ((), ())), precision=exact, preferred_element_type=F32
    )
    row = lax.broadcasted_iota(jnp.int32, wide_sum.shape, 0)
    out_wide[...] = column_total(jnp.where(row == s // quarter, wide_sum, 0.0))
    home.drain()
    home.arrived()

    @pl.when(z < half)
    def _():
        unit1[...] = unit1[...] + b["back"][...].astype(F32)

    rows_copy = pltpu.make_async_copy(unit1, h_rows, b["hbm_sem"].at[2])
    rows_copy.start()
    for name in "UIOQKW":
        segments[name].finish()
    result_copy.wait()
    rows_copy.wait()


def layer_call(n, smalls, wide, tok, w_q, w_k, w_v, w_o, inner, outer, prompt_ids, cont_ids, offsets, cot):
    length, ff = tok.shape[0], inner.shape[2]
    vmem = pl.BlockSpec(memory_space=pltpu.VMEM)
    smem = pl.BlockSpec(memory_space=pltpu.SMEM)
    hbm = pl.BlockSpec(memory_space=pl.ANY)
    sds = jax.ShapeDtypeStruct
    spec, shapes = scratch_of(n, length, ff)
    outs = [sds(s, F32) for s in shapes.values()]
    outs += [sds((8, D // n), F32), sds((1, ff // n), F32)]
    outs += [sds((length, D), F32), sds((length, D), F32)]
    return pl.pallas_call(
        partial(layer_kernel, n, tuple(spec)),
        out_shape=outs,
        in_specs=[vmem] * 10 + [hbm] * 4 + [vmem] * 4 + [smem, hbm],
        out_specs=[vmem] * 8 + [hbm] * 2,
        scratch_shapes=list(spec.values()),
        compiler_params=pltpu.CompilerParams(
            collective_id=0, has_side_effects=True, vmem_limit_bytes=67043328
        ),
        name="layer_step",
    )(*smalls, wide, tok, w_q, w_k, w_v, w_o, inner, outer, prompt_ids, cont_ids, offsets, cot)


def copy_out_kernel(count, *refs):
    sources, small, wide = refs[:count], refs[count], refs[count + 1]
    outs = refs[count + 2 : 2 * count + 2]
    small_outs, wide_out = refs[2 * count + 2 : 2 * count + 10], refs[2 * count + 10]
    held = refs[2 * count + 11 : 3 * count + 11]
    come, go = refs[3 * count + 11 :]
    coming = [pltpu.make_async_copy(a, h, come.at[i]) for i, (a, h) in enumerate(zip(sources, held))]
    going = [pltpu.make_async_copy(h, o, go.at[i]) for i, (h, o) in enumerate(zip(held, outs))]
    for copy in coming:
        copy.start()
    for i in range(8):
        small_outs[i][...] = small[i : i + 1, :]
    wide_out[...] = wide[...]
    for first, second in zip(coming, going):
        first.wait()
        second.start()
    for copy in going:
        copy.wait()


def copy_out(arrays, small, wide):
    vmem = pl.BlockSpec(memory_space=pltpu.VMEM)
    hbm = pl.BlockSpec(memory_space=pl.ANY)
    sds = jax.ShapeDtypeStruct
    count = len(arrays)
    outs = [sds(a.shape, a.dtype) for a in arrays]
    outs += [sds((1, small.shape[1]), F32)] * 8 + [sds(wide.shape, F32)]
    return pl.pallas_call(
        partial(copy_out_kernel, count),
        out_shape=outs,
        in_specs=[hbm] * count + [vmem] * 2,
        out_specs=[hbm] * count + [vmem] * 9,
        scratch_shapes=[pltpu.VMEM(a.shape, a.dtype) for a in arrays]
        + [pltpu.SemaphoreType.DMA((count,)), pltpu.SemaphoreType.DMA((count,))],
        compiler_params=pltpu.CompilerParams(vmem_limit_bytes=67043328),
        name="copy_out",
    )(*arrays, small, wide)


def body(
    tokens,
    w_query,
    b_query,
    w_key,
    w_value,
    b_value,
    w_attout,
    b_attout,
    gain_first,
    beta_first,
    w_inner,
    b_inner,
    w_outer,
    b_outer,
    gain_second,
    beta_second,
    cotangent,
    prompt_ids,
    cont_ids,
    offsets,
):
    n = lax.axis_size("shard")
    reps = lax.axis_size("rep")
    small = (
        b_query,
        b_value,
        b_attout,
        gain_first,
        beta_first,
        b_outer,
        gain_second,
        beta_second,
    )
    *owned, outcome, grad_rows = layer_call(
        n,
        [v[None] for v in small],
        b_inner[None],
        tokens,
        w_query,
        w_key,
        w_value,
        w_attout,
        w_inner[None],
        w_outer[None],
        prompt_ids,
        cont_ids,
        offsets.T,
        cotangent,
    )
    if reps > 2:
        owned = [v * 0.5 for v in lax.psum(tuple(owned), "rep")]
    *arrays, vectors, wide = owned
    if reps == 2:
        finished = copy_out([outcome, grad_rows] + arrays, vectors, wide)
        outcome, grad_rows, *arrays = finished[:8]
        vectors, wide = [v[0] for v in finished[8:16]], finished[16]
    own_wu, own_wi, own_wo, own_wq, own_wk, own_wv = arrays
    s_bq, s_bv, s_bo, s_g1, s_be1, s_bu, s_g2, s_be2 = (vectors[i] for i in range(8))
    return (
        outcome,
        grad_rows,
        own_wq,
        s_bq,
        own_wk,
        own_wv,
        s_bv,
        own_wo,
        s_bo,
        s_g1,
        s_be1,
        own_wi,
        wide[0],
        own_wu,
        s_bu,
        s_g2,
        s_be2,
    )


def solution(mesh):
    return jax.shard_map(
        body,
        mesh=mesh,
        in_specs=(
            P(("rep", "shard"), None),
            P("shard", None),
            P("shard"),
            P("shard", None),
            P("shard", None),
            P("shard"),
            P("shard", None),
            P("shard"),
            P("shard"),
            P("shard"),
            P("shard", None),
            P("shard"),
            P("shard", None),
            P("shard"),
            P("shard"),
            P("shard"),
            P(("rep", "shard"), None),
            P(),
            P(),
            P(),
        ),
        out_specs=(
            P(("rep", "shard"), None),
            P(("rep", "shard"), None),
            P("shard", None),
            P("shard"),
            P("shard", None),
            P("shard", None),
            P("shard"),
            P("shard", None),
            P("shard"),
            P("shard"),
            P("shard"),
            P("shard", None),
            P("shard"),
            P("shard", None),
            P("shard"),
            P("shard"),
            P("shard"),
        ),
        check_vma=False,
    )
```

```python
from functools import partial

import jax
import jax.numpy as jnp
from jax import lax
from jax.experimental import pallas as pl
from jax.experimental.pallas import tpu as pltpu
from jax.sharding import PartitionSpec as P

D = 768
H = 12
DH = 64


EPSILON = 1e-12


MESHID = pl.DeviceIdType.MESH
BF16 = jnp.bfloat16
F32 = jnp.float32


def line_order(n):
    depth = n // 4
    order = []
    for z in range(depth):
        others = [k for k in range(depth) if k != z]
        others.sort(key=lambda k: (k // 2 != z // 2, abs(k - z), k))
        order.append([z] + others)
    return depth, order


def pick(table, z):
    out = table[-1]
    for i in range(len(table) - 2, -1, -1):
        out = jnp.where(z == i, table[i], out)
    return out


def place_of(n):
    depth, order = line_order(n)
    s = lax.axis_index("shard")
    r = lax.axis_index("rep")
    z, q = s // 4, s % 4
    y, x = q // 2, q % 2
    core = r % 2
    qx = y * 2 + 1 - x
    qy = (1 - y) * 2 + x
    qd = (1 - y) * 2 + 1 - x

    def device(rr, ss):
        return {"rep": rr, "shard": ss}

    half = depth // 2
    return dict(
        depth=depth,
        order=order,
        z=z,
        q=q,
        core=core,
        s=s,
        r=r,
        qx=qx,
        qy=qy,
        qd=qd,
        half=half,
        near_x=device(r, z * 4 + qx),
        near_y=device(r, z * 4 + qy),
        up=device(r, s + 4),
        down=device(r, s - 4),
        sibling=device(r + 1 - 2 * core, s),
        ahead=device(r, s + 4 * half),
        behind=device(r, s - 4 * half),
        device=device,
    )


def entry_barrier(p):
    bar = pltpu.get_barrier_semaphore()
    z, depth, half = p["z"], p["depth"], p["half"]

    def signal(where):
        pl.semaphore_signal(bar, inc=1, device_id=where, device_id_type=MESHID)

    signal(p["near_x"])
    signal(p["near_y"])
    signal(p["sibling"])
    pl.when(z + 1 < depth)(lambda: signal(p["up"]))
    pl.when(z > 0)(lambda: signal(p["down"]))
    pl.when(z < half)(lambda: signal(p["ahead"]))
    pl.when(z >= half)(lambda: signal(p["behind"]))
    pl.semaphore_wait(bar, 4 + jnp.where(z > 0, 1, 0) + jnp.where(z + 1 < depth, 1, 0))


def part_of(rows, quarter):
    top = (rows // 2 + 7) // 8 * 8
    if quarter is None:
        return 0, rows
    return (0, top) if quarter == 0 else (top, rows - top)


class Gather:
    def __init__(self, place, src, dst, send, recv, local, base):
        self.p, self.src, self.dst = place, src, dst
        self.rows, self.cols = src.shape[1], src.shape[2]
        self.send, self.recv, self.local, self.base = send, recv, local, base
        depth = place["depth"]
        self.names = {}
        for name in ("x", "y", "dx", "dy", "sx", "sy", "s0", "s1", "sz"):
            for i in range(depth):
                self.names[(name, i)] = len(self.names)
        self.line = len(self.names)
        self.count = self.line + 2 * depth

    def piece(self, chip, half, quarter=None):
        width = self.cols // 2
        cols = pl.ds(pl.multiple_of(half * width, width), width)
        first, size = part_of(self.rows, quarter)
        return self.dst.at[:, pl.ds(pl.multiple_of(chip * self.rows + first, 8), size), cols]

    def copy(self, sem, chip, where, quarter=None, own=False, half=None):
        half = self.p["core"] if half is None else half
        dst = self.piece(chip, half, quarter)
        src = dst
        if own:
            width = self.cols // 2
            src = self.src.at[:, :, pl.ds(pl.multiple_of(half * width, width), width)]
        i = self.base + (self.names[sem] if isinstance(sem, tuple) else self.line + sem)
        return pltpu.make_async_remote_copy(
            src_ref=src,
            dst_ref=dst,
            send_sem=self.send.at[i],
            recv_sem=self.recv.at[i],
            device_id=where,
            device_id_type=MESHID,
        )

    def item(self, i):
        return pick([line[i] for line in self.p["order"]], self.p["z"])

    def chips(self, i):
        k = self.item(i)
        p = self.p
        return tuple(k * 4 + p[name] for name in ("q", "qx", "qy", "qd"))

    def own_copy(self):
        me = self.p["s"]
        rows = pl.ds(pl.multiple_of(me * self.rows, self.rows), self.rows)
        return pltpu.make_async_copy(self.src, self.dst.at[:, rows, :], self.local)

    def start(self):
        p = self.p
        me, depth = p["s"], p["depth"]
        self.own_copy().start()
        pl.when(p["z"] + 1 < depth)(lambda: self.copy(0, me, p["up"], own=True).start())
        pl.when(p["z"] > 0)(lambda: self.copy(depth, me, p["down"], own=True).start())
        self.copy(("x", 0), me, p["near_x"], own=True).start()
        self.copy(("y", 0), me, p["near_y"], own=True).start()

    def flow(self, i):
        p = self.p
        z, s, depth = p["z"], p["s"], p["depth"]
        k = self.item(i)
        upward = k < z
        sem = jnp.where(upward, z - k - 1, depth + k - z - 1)
        onward = jnp.where(upward, z + 1 < depth, z > 0)
        target = p["device"](p["r"], jnp.where(upward, s + 4, s - 4))
        return sem, onward, target

    def take(self, i):
        p = self.p
        chip = self.chips(i)[0]
        sem, onward, target = self.flow(i)
        self.copy(sem, chip, p["sibling"]).wait_recv()
        pl.when(onward)(lambda: self.copy(sem + 1, chip, target).start())
        self.copy(("x", i), chip, p["near_x"]).start()
        self.copy(("y", i), chip, p["near_y"]).start()
        self.copy(("sz", i), chip, p["sibling"]).start()

    def spread(self, i):
        p = self.p
        _, cx, cy, _ = self.chips(i)
        self.copy(("x", i), cx, p["sibling"]).wait_recv()
        self.copy(("dy", i), cx, p["near_y"], quarter=0).start()
        self.copy(("sx", i), cx, p["sibling"]).start()
        self.copy(("y", i), cy, p["sibling"]).wait_recv()
        self.copy(("dx", i), cy, p["near_x"], quarter=1).start()
        self.copy(("sy", i), cy, p["sibling"]).start()

    def corner(self, i):
        p = self.p
        cd = self.chips(i)[3]
        self.copy(("dy", i), cd, p["sibling"], quarter=0).wait_recv()
        self.copy(("s0", i), cd, p["sibling"], quarter=0).start()
        self.copy(("dx", i), cd, p["sibling"], quarter=1).wait_recv()
        self.copy(("s1", i), cd, p["sibling"], quarter=1).start()

    def here(self, i):
        p = self.p
        other = 1 - p["core"]
        cm, cx, cy, cd = self.chips(i)
        if i:
            self.copy(("sz", i), cm, p["sibling"], half=other).wait_recv()
        else:
            self.own_copy().wait()
        self.copy(("sx", i), cx, p["sibling"], half=other).wait_recv()
        self.copy(("sy", i), cy, p["sibling"], half=other).wait_recv()
        self.copy(("s0", i), cd, p["sibling"], quarter=0, half=other).wait_recv()
        self.copy(("s1", i), cd, p["sibling"], quarter=1, half=other).wait_recv()

    def arrived(self):
        for i in range(self.p["depth"]):
            self.here(i)

    def drain(self):
        p = self.p
        depth = p["depth"]
        me = p["s"]
        pl.when(p["z"] + 1 < depth)(lambda: self.copy(0, me, p["up"], own=True).wait_send())
        pl.when(p["z"] > 0)(lambda: self.copy(depth, me, p["down"], own=True).wait_send())
        for i in range(depth):
            cm, cx, cy, cd = self.chips(i)
            if i:
                sem, onward, target = self.flow(i)
                pl.when(onward)(
                    lambda sem=sem, target=target, cm=cm: self.copy(sem + 1, cm, target).wait_send()
                )
                self.copy(("sz", i), cm, p["sibling"]).wait_send()
            self.copy(("x", i), cm, p["near_x"]).wait_send()
            self.copy(("y", i), cm, p["near_y"]).wait_send()
            self.copy(("dy", i), cx, p["near_y"], quarter=0).wait_send()
            self.copy(("dx", i), cy, p["near_x"], quarter=1).wait_send()
            self.copy(("sx", i), cx, p["sibling"]).wait_send()
            self.copy(("sy", i), cy, p["sibling"]).wait_send()
            self.copy(("s0", i), cd, p["sibling"], quarter=0).wait_send()
            self.copy(("s1", i), cd, p["sibling"], quarter=1).wait_send()


class Scatter:
    def __init__(self, place, grad, out, pair, diag, side, line, send, recv, base):
        self.p, self.grad, self.out = place, grad, out
        self.rows, self.cols = out.shape[1], out.shape[2]
        self.pair, self.diag, self.side, self.line = pair, diag, side, line
        self.send, self.recv, self.base = send, recv, base
        self.half = self.cols // 2
        core = place["core"]
        self.mine = pl.ds(pl.multiple_of(core * self.half, self.half), self.half)
        self.theirs = pl.ds(pl.multiple_of((1 - core) * self.half, self.half), self.half)
        depth = place["depth"]
        self.names = {}
        for name in ("p", "d0", "d1", "s0", "s1"):
            for i in range(depth):
                self.names[(name, i)] = len(self.names)
        self.names["o"] = len(self.names)
        self.first = len(self.names)
        self.count = self.first + 2 * depth

    @staticmethod
    def scratch(n, layers, rows, cols, dtype):
        depth, h = n // 4, cols // 2
        return [
            pltpu.VMEM((layers, n * rows, h), dtype),
            pltpu.VMEM((2 * depth, layers, part_of(rows, 0)[1], h), dtype),
            pltpu.VMEM((2 * depth, layers, rows, h), dtype),
            pltpu.VMEM((2 * depth - 2, layers, rows, h), dtype),
        ]

    def make(self, sem, src, dst, where):
        i = self.base + sem
        return pltpu.make_async_remote_copy(
            src_ref=src,
            dst_ref=dst,
            send_sem=self.send.at[i],
            recv_sem=self.recv.at[i],
            device_id=where,
            device_id_type=MESHID,
        )

    def item(self, i):
        depth = self.p["depth"]
        return pick([line[depth - 1 - i] for line in self.p["order"]], self.p["z"])

    def rows_of(self, k, q, quarter=None):
        first, size = part_of(self.rows, quarter)
        return pl.ds(pl.multiple_of((k * 4 + q) * self.rows + first, 8), size)

    def pair_copy(self, i):
        r = self.rows * 4
        block = pl.ds(pl.multiple_of(self.item(i) * r, r), r)
        return self.make(
            self.names[("p", i)],
            self.grad.at[:, block, self.theirs],
            self.pair.at[:, block, :],
            self.p["sibling"],
        )

    def diag_copy(self, i, quarter):
        p = self.p
        return self.make(
            self.names[("d0" if quarter == 0 else "d1", i)],
            self.grad.at[:, self.rows_of(self.item(i), p["qd"], quarter), self.mine],
            self.diag.at[i * 2 + quarter, :, pl.ds(0, part_of(self.rows, quarter)[1]), :],
            p["near_y"] if quarter == 0 else p["near_x"],
        )

    def side_copy(self, i, axis):
        p = self.p
        return self.make(
            self.names[("s0" if axis == 0 else "s1", i)],
            self.grad.at[:, self.rows_of(self.item(i), p["qx"] if axis == 0 else p["qy"]), self.mine],
            self.side.at[i * 2 + axis],
            p["near_x"] if axis == 0 else p["near_y"],
        )

    def line_copy(self, i):
        p = self.p
        k, z, depth = self.item(i), p["z"], p["depth"]
        slot = jnp.where(k > z, k - z - 1, depth - 1 + z - 1 - k)
        where = p["device"](p["r"], jnp.where(k > z, p["s"] + 4, p["s"] - 4))
        return self.make(
            self.first + slot,
            self.grad.at[:, self.rows_of(k, p["q"]), self.mine],
            self.line.at[slot],
            where,
        )

    def line_wait(self, slot):
        self.make(
            self.first + slot, self.line.at[slot], self.line.at[slot], self.p["sibling"]
        ).wait_recv()

    def out_copy(self, cols):
        return self.make(
            self.names["o"], self.out.at[:, :, cols], self.out.at[:, :, cols], self.p["sibling"]
        )

    def sweep(self, start, count, chunk, sources, store):
        def body(t, carry):
            at = pl.ds(pl.multiple_of(start + t * chunk, 8), chunk)
            low = pl.ds(pl.multiple_of(t * chunk, 8), chunk)
            total = self.grad[:, at, self.mine].astype(F32)
            for source in sources:
                total = total + source(at, low).astype(F32)
            store(at, low, total)
            return carry

        lax.fori_loop(0, count // chunk, body, 0)

    def store_grad(self, at, low, total):
        self.grad[:, at, self.mine] = total.astype(self.grad.dtype)

    def store_out(self, at, low, total):
        self.out[:, low, self.mine] = total

    def give(self, i):
        self.pair_copy(i).start()

    def merge(self, i):
        k = self.item(i)
        self.pair_copy(i).wait_recv()
        r4 = self.rows * 4
        self.sweep(k * r4, r4, 16, [lambda at, low: self.pair[:, at, :]], self.store_grad)
        self.diag_copy(i, 0).start()
        self.diag_copy(i, 1).start()

    def merge_diag(self, i):
        p = self.p
        k = self.item(i)
        for quarter, q in ((0, p["qx"]), (1, p["qy"])):
            self.diag_copy(i, quarter).wait_recv()
            slot = i * 2 + quarter
            first, size = part_of(self.rows, quarter)
            self.sweep(
                (k * 4 + q) * self.rows + first,
                size,
                8,
                [lambda at, low, slot=slot: self.diag[slot, :, low, :]],
                self.store_grad,
            )
            self.side_copy(i, quarter).start()

    def merge_side(self, i):
        p = self.p
        k, z, depth = self.item(i), p["z"], p["depth"]
        self.side_copy(i, 0).wait_recv()
        self.side_copy(i, 1).wait_recv()
        base = (k * 4 + p["q"]) * self.rows
        sides = [
            lambda at, low: self.side[i * 2, :, low, :],
            lambda at, low: self.side[i * 2 + 1, :, low, :],
        ]

        def total(slots, store):
            lines = [lambda at, low, slot=slot: self.line[slot, :, low, :] for slot in slots]
            self.sweep(base, self.rows, 16 if self.rows % 16 == 0 else 8, sides + lines, store)

        if i < depth - 1:
            has = ((k > z) & (z > 0)) | ((k < z) & (z + 1 < depth))
            slot = jnp.where(k > z, k - z, jnp.minimum(depth - 1 + z - k, 2 * depth - 3))

            @pl.when(has)
            def _():
                self.line_wait(slot)
                total([slot], self.store_grad)

            pl.when(jnp.logical_not(has))(lambda: total([], self.store_grad))
            self.line_copy(i).start()
        else:
            below, above = 0, depth - 1
            pl.when(z > 0)(lambda: self.line_wait(below))
            pl.when(z + 1 < depth)(lambda: self.line_wait(above))
            pl.when((z > 0) & (z + 1 < depth))(lambda: total([below, above], self.store_out))
            pl.when(z == 0)(lambda: total([above], self.store_out))
            pl.when(z + 1 == depth)(lambda: total([below], self.store_out))
            self.out_copy(self.mine).start()

    def finish(self):
        depth = self.p["depth"]
        self.out_copy(self.theirs).wait_recv()
        self.out_copy(self.mine).wait_send()
        for i in range(depth):
            self.pair_copy(i).wait_send()
            for side in (0, 1):
                self.diag_copy(i, side).wait_send()
                self.side_copy(i, side).wait_send()
            if i < depth - 1:
                self.line_copy(i).wait_send()


class Across:
    chunks = 4

    def __init__(self, place, src, dst, relay, send, recv, forward):
        p = place
        self.p, self.src, self.dst, self.relay = p, src, dst, relay
        self.send, self.recv = send, recv
        depth, z = p["depth"], p["z"]
        self.short = depth == 4
        self.at = z if forward else depth - 1 - z
        self.next = p["up"] if forward else p["down"]
        self.far = p["ahead"] if forward else p["behind"]

    def rows(self, j):
        size = self.src.shape[0] // self.chunks
        return pl.ds(j * size, size)

    def make(self, kind, j, src, dst, where):
        rows = self.rows(j)
        i = kind * self.chunks + j
        return pltpu.make_async_remote_copy(
            src_ref=src.at[rows],
            dst_ref=dst.at[rows],
            send_sem=self.send.at[i],
            recv_sem=self.recv.at[i],
            device_id=where,
            device_id_type=MESHID,
        )

    def begin(self, j):
        half = self.p["depth"] // 2
        if self.short:
            to_dst = self.make(0, j, self.src, self.dst, self.next)
            to_relay = self.make(1, j, self.src, self.relay, self.next)
            pl.when(self.at == 0)(lambda: to_dst.start())
            pl.when(self.at == 1)(lambda: to_relay.start())
        else:
            direct = self.make(0, j, self.src, self.dst, self.far)
            pl.when(self.at < half)(lambda: direct.start())

    def onward(self, j):
        if self.short:
            hold = self.make(0, j, self.src, self.dst, self.next)
            held = self.make(1, j, self.src, self.relay, self.next)
            from_dst = self.make(2, j, self.dst, self.dst, self.next)
            from_relay = self.make(3, j, self.relay, self.dst, self.next)

            @pl.when(self.at == 1)
            def _():
                hold.wait_recv()
                from_dst.start()

            @pl.when(self.at == 2)
            def _():
                held.wait_recv()
                from_relay.start()

    def arrived(self):
        half = self.p["depth"] // 2
        for j in range(self.chunks):
            if self.short:
                second = self.make(2, j, self.dst, self.dst, self.next)
                third = self.make(3, j, self.relay, self.dst, self.next)
                pl.when(self.at == 2)(lambda copy=second: copy.wait_recv())
                pl.when(self.at == 3)(lambda copy=third: copy.wait_recv())
            else:
                direct = self.make(0, j, self.src, self.dst, self.far)
                pl.when(self.at >= half)(lambda copy=direct: copy.wait_recv())

    def drain(self):
        half = self.p["depth"] // 2
        for j in range(self.chunks):
            if self.short:
                copies = (
                    self.make(0, j, self.src, self.dst, self.next),
                    self.make(1, j, self.src, self.relay, self.next),
                    self.make(2, j, self.dst, self.dst, self.next),
                    self.make(3, j, self.relay, self.dst, self.next),
                )
                pl.when(self.at == 0)(lambda: copies[0].wait_send())

                @pl.when(self.at == 1)
                def _():
                    copies[1].wait_send()
                    copies[2].wait_send()

                pl.when(self.at == 2)(lambda: copies[3].wait_send())
            else:
                direct = self.make(0, j, self.src, self.dst, self.far)
                pl.when(self.at < half)(lambda copy=direct: copy.wait_send())


VEC_ROWS = 16


def dot(a, b, ca=1, cb=0):
    return lax.dot_general(a, b, (((ca,), (cb,)), ((), ())), preferred_element_type=F32)


def mean_last(v):
    return jnp.sum(v, axis=-1, keepdims=True) * (1.0 / v.shape[-1])


def normalize(v):
    c = v - mean_last(v)
    inverse = lax.rsqrt(mean_last(c * c) + EPSILON)
    return c * inverse, inverse


def normalize_back(grad, gain, unit, inverse):
    g = grad * gain
    return inverse * (g - mean_last(g) - unit * mean_last(g * unit))


def gelu_pair(x):
    tail = jnp.exp(-0.5 * (x * x))
    t = 1.0 / (1.0 + (0.3275911 * 0.7071067811865476) * jnp.abs(x))
    poly = 1.061405429 * t - 1.453152027
    poly = poly * t + 1.421413741
    poly = poly * t - 0.284496736
    poly = poly * t + 0.254829592
    low = (0.5 * t) * poly * tail
    cdf = jnp.where(x < 0, low, 1.0 - low)
    return x * cdf, cdf + x * (tail * 0.3989422804014327)


def column_total(v):
    return jnp.sum(v, axis=0, keepdims=True)


def even_lanes(shape):
    return lax.broadcasted_iota(jnp.int32, shape, 1) % 128 < 64


def split_heads(x, even_ref, odd_ref):
    keep = even_lanes(x.shape)
    zero = jnp.zeros_like(x)
    even_ref[...] = jnp.where(keep, x, zero).astype(BF16)
    odd_ref[...] = jnp.where(keep, zero, x).astype(BF16)


def make_bias(bias, col_label, row_label, row_limit):
    length = row_label.shape[1]
    for b in range(0, length, 128):
        at = pl.ds(b, 128)
        row = lax.broadcasted_iota(jnp.int32, (128, length), 0) + b
        bias[at, :] = jnp.where(row < row_limit[...], 0.0, -1e30)
        same = col_label[at, 0:1] == row_label[...]
        bias[pl.ds(length + b, 128), :] = jnp.where(same, 0.0, -1e30)


def head_slices(j, side):
    head = pl.ds(pl.multiple_of(j * 128 + side * DH, DH), DH)
    row = pl.ds(pl.multiple_of(j * 16 + side * 8, 8), 8)
    return head, row


def part_block(part, j, side, b):
    index = j * 4 + side * 2 + b
    return part.at[
        pl.ds(pl.multiple_of(index // 3 * DH, DH), DH),
        pl.ds(pl.multiple_of(index % 3 * 256, 256), 256),
    ]


def attend_own(j, q_even, q_odd, keys, values_t, bias, part, tops, sums):
    lanes = pl.ds(pl.multiple_of(j * 128, 128), 128)
    length = q_even.shape[0]
    own = pl.ds(length, length)
    width = 256
    for b in range(0, length, width):
        block = pl.ds(b, width)
        for side, q_ref in ((0, q_even), (1, q_odd)):
            head, row = head_slices(j, side)
            scores = dot(keys[own, lanes], q_ref[block, lanes], 1, 1) + bias[own, block]
            top = jnp.max(scores, axis=0, keepdims=True)
            expo = jnp.exp(scores - top)
            part_block(part, j, side, b // width)[...] = dot(
                values_t[head, own], expo.astype(BF16)
            )
            tops[row, block] = jnp.broadcast_to(top, (8, width))
            sums[row, block] = jnp.broadcast_to(column_total(expo), (8, width))


def attend_far(j, q_even, q_odd, keys, values_t, bias, part, tops, sums, mixed_t):
    lanes = pl.ds(pl.multiple_of(j * 128, 128), 128)
    length = q_even.shape[0]
    far = pl.ds(0, length)
    width = 256
    for b in range(0, length, width):
        block = pl.ds(b, width)
        for side, q_ref in ((0, q_even), (1, q_odd)):
            head, row = head_slices(j, side)
            scores = dot(keys[far, lanes], q_ref[block, lanes], 1, 1) + bias[far, block]
            before = tops[row, block][0:1]
            top = jnp.maximum(jnp.max(scores, axis=0, keepdims=True), before)
            expo = jnp.exp(scores - top)
            fade = jnp.exp(before - top)
            total = sums[row, block][0:1] * fade + column_total(expo)
            mixed = part_block(part, j, side, b // width)[...] * fade + dot(values_t[head, far], expo.astype(BF16))
            mixed_t[head, block] = (mixed * (1.0 / total)).astype(BF16)
            tops[row, block] = jnp.broadcast_to(top + jnp.log(total), (8, width))


def attend_back(
    j, own, q_even, q_odd, g_even, g_odd, keys, keys_t, values, bias, delta, log_sums, part, grad_qt, grad_k, grad_v
):
    lanes = pl.ds(pl.multiple_of(j * 128, 128), 128)
    length = q_even.shape[0]
    half = pl.ds(length if own else 0, length)
    width = 256
    total_k, total_v = 0.0, 0.0
    for b in range(0, length, width):
        block = pl.ds(b, width)
        for side, q_ref, g_ref in ((0, q_even, g_even), (1, q_odd, g_odd)):
            head, row = head_slices(j, side)
            scores = dot(keys[half, lanes], q_ref[block, lanes], 1, 1) + bias[half, block]
            probs = jnp.exp(scores - log_sums[row, block][0:1])
            grad_p = dot(values[half, lanes], g_ref[block, lanes], 1, 1)
            grad_s = (probs * (grad_p - delta[row, block][0:1])).astype(BF16)
            total_v = total_v + dot(probs.astype(BF16), g_ref[block, lanes])
            total_k = total_k + dot(grad_s, q_ref[block, lanes])
            grad_q = dot(keys_t[head, half], grad_s)
            held = part_block(part, j, side, b // width)
            if own:
                grad_qt[head, block] = ((held[...] + grad_q) * 0.125).astype(BF16)
            else:
                held[...] = grad_q
    grad_k[half, lanes] = total_k.astype(BF16)
    grad_v[half, lanes] = total_v.astype(BF16)


def one_hot(rows, cols, shift):
    row = lax.broadcasted_iota(jnp.int32, (rows, cols), 0)
    col = lax.broadcasted_iota(jnp.int32, (rows, cols), 1)
    return jnp.where(col == row + shift, 1.0, 0.0)


def own_small(n, smalls, wide, out):
    s = lax.axis_index("shard")
    part = smalls[0].shape[1]
    quarter = n // 4
    out[...] = jnp.zeros_like(out)
    place = one_hot(part, D, s * part).astype(BF16)
    for i, v in enumerate(smalls):
        out[0, i : i + 1, :] = dot(v[...], place).astype(BF16)
    place = one_hot(4 * part, D, (s % quarter) * 4 * part).astype(BF16)
    piece = dot(wide[...], place)
    row = lax.broadcasted_iota(jnp.int32, (4, D), 0)
    out[0, 8:12, :] = jnp.where(row == s // quarter, piece, 0.0).astype(BF16)


def labels_of(n, prompt_ids, cont_ids, offsets, row_label, row_limit, col_label):
    half = n // 2
    s = lax.axis_index("shard")
    is_cont = s >= half
    group = lax.axis_index("rep") * half + s % half
    own = jnp.where(
        is_cont, cont_ids[pl.ds(group, 1), :], prompt_ids[pl.ds(group, 1), :]
    )
    limit = jnp.zeros_like(own)
    for k in range(offsets.shape[0]):
        limit = jnp.where(own == k, offsets[k, group], limit)
    row_label[...] = own
    row_limit[...] = jnp.where(is_cont, limit, 0)
    col_label[...] = jnp.broadcast_to(own, (128, own.shape[1])).T


PLAN_FOUR = (
    ('start', 'V'),
    ('start', 'A'),
    ('spread', 'V', 0),
    ('take', 'V', 1),
    ('start', 'D'),
    ('take', 'A', 1),
    ('take', 'A', 2),
    ('take', 'V', 3),
    ('take', 'V', 2),
    ('tok', 0),
    ('take', 'A', 3),
    ('start', 'C'),
    ('spread', 'A', 1),
    ('spread', 'V', 3),
    ('spread', 'V', 1),
    ('pass', 0),
    ('spread', 'A', 0),
    ('tok', 1),
    ('spread', 'A', 3),
    ('spread', 'V', 2),
    ('spread', 'A', 2),
    ('take', 'C', 2),
    ('take', 'D', 1),
    ('tok', 2),
    ('corner', 'V', 0),
    ('take', 'D', 2),
    ('corner', 'V', 1),
    ('corner', 'A', 0),
    ('corner', 'A', 3),
    ('corner', 'V', 3),
    ('corner', 'V', 2),
    ('take', 'C', 1),
    ('war', 'V'),
    ('corner', 'A', 1),
    ('corner', 'A', 2),
    ('tok', 3),
    ('pass', 1),
    ('war', 'A'),
    ('c', 'c1'),
    ('take', 'D', 3),
    ('c', 'o0'),
    ('c', 'o1'),
    ('pass', 2),
    ('c', 'o2'),
    ('c', 'o3'),
    ('take', 'C', 3),
    ('spread', 'C', 0),
    ('pass', 3),
    ('spread', 'D', 1),
    ('c', 'o4'),
    ('spread', 'C', 1),
    ('spread', 'D', 0),
    ('c', 'o5'),
    ('spread', 'C', 2),
    ('spread', 'D', 2),
    ('spread', 'D', 3),
    ('wtok',),
    ('c', 'c2'),
    ('c', 'p0'),
    ('c', 'p1'),
    ('corner', 'D', 1),
    ('c', 'p2'),
    ('c', 'p3'),
    ('c', 'p4'),
    ('spread', 'C', 3),
    ('corner', 'C', 2),
    ('corner', 'C', 1),
    ('corner', 'C', 0),
    ('c', 'p5'),
    ('c', 'att'),
    ('corner', 'D', 2),
    ('corner', 'D', 0),
    ('corner', 'D', 3),
    ('here', 'D', 0),
    ('here', 'D', 1),
    ('here', 'D', 2),
    ('here', 'D', 3),
    ('corner', 'C', 3),
    ('war', 'C'),
    ('c', 'a0'),
    ('c', 'a1'),
    ('c', 'a2'),
    ('c', 'a3'),
    ('c', 'b0'),
    ('c', 'b1'),
    ('c', 'b2'),
    ('c', 'b3'),
    ('c', 'ln2'),
    ('c', 'f0'),
    ('give', 'U', 0),
    ('c', 'f1'),
    ('give', 'U', 1),
    ('merge', 'U', 0),
    ('c', 'f2'),
    ('merge', 'U', 1),
    ('merge_diag', 'U', 0),
    ('c', 'f3'),
    ('c', 'g0'),
    ('c', 'g1'),
    ('c', 'g2'),
    ('c', 'g3'),
    ('give', 'I', 0),
    ('give', 'U', 2),
    ('give', 'I', 1),
    ('give', 'I', 2),
    ('merge_diag', 'U', 1),
    ('c', 'pre'),
    ('merge_side', 'U', 0),
    ('give', 'O', 0),
    ('merge', 'I', 0),
    ('give', 'I', 3),
    ('merge', 'U', 2),
    ('c', 'x0'),
    ('c', 'x1'),
    ('merge_side', 'U', 1),
    ('give', 'U', 3),
    ('merge_diag', 'I', 0),
    ('c', 'x2'),
    ('merge_diag', 'U', 2),
    ('c', 'x3'),
    ('c', 'x4'),
    ('merge_side', 'I', 0),
    ('give', 'O', 1),
    ('merge', 'I', 1),
    ('c', 'x5'),
    ('c', 'term'),
    ('back', 0),
    ('merge', 'O', 0),
    ('give', 'O', 2),
    ('merge', 'I', 3),
    ('merge', 'U', 3),
    ('back', 1),
    ('merge', 'I', 2),
    ('merge_diag', 'I', 1),
    ('c', 'y0'),
    ('c', 'y1'),
    ('back', 2),
    ('c', 'y2'),
    ('c', 'y3'),
    ('merge', 'O', 1),
    ('merge_diag', 'I', 2),
    ('back', 3),
    ('c', 'y4'),
    ('merge_side', 'U', 2),
    ('merge_diag', 'I', 3),
    ('c', 'y5'),
    ('c', 'rows'),
    ('merge', 'O', 2),
    ('onward', 0),
    ('merge_diag', 'O', 1),
    ('c', 'wq'),
    ('merge_diag', 'O', 0),
    ('c', 'wk'),
    ('small', 0),
    ('c', 'wv'),
    ('give', 'Q', 0),
    ('give', 'O', 3),
    ('merge_diag', 'O', 2),
    ('give', 'Q', 1),
    ('give', 'Q', 2),
    ('give', 'Q', 3),
    ('onward', 1),
    ('merge_side', 'I', 1),
    ('small', 1),
    ('merge_side', 'I', 2),
    ('merge', 'Q', 0),
    ('merge_diag', 'Q', 0),
    ('small', 2),
    ('merge_side', 'O', 0),
    ('merge', 'Q', 1),
    ('merge', 'Q', 2),
    ('merge_side', 'Q', 0),
    ('onward', 2),
    ('merge_diag', 'Q', 2),
    ('merge_diag', 'Q', 1),
    ('merge', 'O', 3),
    ('merge_side', 'O', 1),
    ('merge_side', 'O', 2),
    ('merge_diag', 'U', 3),
    ('merge_diag', 'O', 3),
    ('merge', 'Q', 3),
    ('merge_side', 'Q', 1),
    ('merge_side', 'Q', 2),
    ('onward', 3),
    ('merge_diag', 'Q', 3),
    ('merge_side', 'O', 3),
    ('merge_side', 'I', 3),
    ('merge_side', 'U', 3),
    ('merge_side', 'Q', 3),
)


def default_plan(depth):
    plan = [("start", "V"), ("start", "A")]
    plan += [("tok", j) for j in range(Across.chunks)]
    plan += [("pass", j) for j in range(Across.chunks)]
    for seg in "VACD":
        if seg in "CD":
            plan.append(("start", seg))
        for i in range(depth):
            if i:
                plan.append(("take", seg, i))
            plan.append(("spread", seg, i))
            if i:
                plan.append(("corner", seg, i - 1))
        plan.append(("corner", seg, depth - 1))
        plan += [("war", seg)] if seg != "D" else [("here", seg, i) for i in range(depth)]
    plan += [("wtok",), ("c", "c1")] + [("c", "o%d" % i) for i in range(6)] + [("c", "c2")]
    plan += [("c", "p%d" % i) for i in range(6)] + [("c", "att")]
    plan += [("c", "a%d" % i) for i in range(4)] + [("c", "b%d" % i) for i in range(4)]
    plan += [("c", "ln2")] + [("c", "f%d" % i) for i in range(4)]
    plan += [("c", "g%d" % i) for i in range(4)] + [("c", "pre")]
    plan += [("give", s, i) for s in "UIO" for i in range(depth)]
    plan += [("c", "x%d" % i) for i in range(6)] + [("c", "term")]
    plan += [("back", j) for j in range(Across.chunks)]
    plan += [("onward", j) for j in range(Across.chunks)]
    plan += [("c", "y%d" % i) for i in range(6)]
    plan += [("c", "rows"), ("c", "wq"), ("c", "wk"), ("c", "wv")]
    plan += [("give", s, i) for s in "Q" for i in range(depth)]
    plan += [("small", j) for j in range(3)]
    for seg in "UIOQ":
        for i in range(depth + 2):
            if i < depth:
                plan.append(("merge", seg, i))
            if 0 <= i - 1 < depth:
                plan.append(("merge_diag", seg, i - 1))
            if 0 <= i - 2 < depth:
                plan.append(("merge_side", seg, i - 2))
    return plan


def run_plan(plan, comm, single, loops):
    at = 0
    while at < len(plan):
        step = plan[at]
        if step[0] != "c":
            comm(step)
            at += 1
        elif step[1] in single:
            single[step[1]]()
            at += 1
        else:
            kind = step[1][0]
            count, chunk = loops[kind]
            after = []
            for _ in range(count):
                at += 1
                steps = []
                last = len(after) == count - 1
                while not last and plan[at][0] != "c":
                    steps.append(plan[at])
                    at += 1
                after.append(steps)

            def body(j, carry, after=after, chunk=chunk):
                chunk(j)
                for k, steps in enumerate(after):
                    if steps:

                        @pl.when(j == k)
                        def _():
                            for step in steps:
                                comm(step)

                return carry

            lax.fori_loop(0, count, body, 0)


class SmallSum:
    def __init__(self, place, total, slots, send, recv, base):
        self.p, self.total, self.slots = place, total, slots
        self.send, self.recv, self.base = send, recv, base

    def make(self, slot, where):
        return pltpu.make_async_remote_copy(
            src_ref=self.total,
            dst_ref=self.slots.at[slot],
            send_sem=self.send.at[self.base + slot],
            recv_sem=self.recv.at[self.base + slot],
            device_id=where,
            device_id_type=MESHID,
        )

    def stage(self, k):
        return self.make(k, (self.p["sibling"], self.p["near_x"], self.p["near_y"])[k])

    def begin(self):
        self.stage(0).start()

    def fold(self, k):
        copy = self.stage(k)
        copy.wait_send()
        copy.wait_recv()
        self.total[...] = self.total[...] + self.slots[k]
        if k < 2:
            self.stage(k + 1).start()
        else:
            self.along(lambda copy: copy.start())

    def along(self, act):
        p = self.p
        z, depth = p["z"], p["depth"]
        for d in range(1, depth):
            for sign in (1, -1):
                target = p["device"](p["r"], p["s"] + 4 * d * sign)
                slot = 3 + 2 * (d - 1) + (0 if sign == 1 else 1)
                ok = z + d < depth if sign == 1 else z - d >= 0
                pl.when(ok)(lambda slot=slot, target=target: act(self.make(slot, target)))

    def finish(self):
        p = self.p
        z, depth = p["z"], p["depth"]
        self.along(lambda copy: copy.wait_send())
        terms = []
        for d in range(1, depth):
            for sign in (1, -1):
                slot = 3 + 2 * (d - 1) + (0 if sign == 1 else 1)
                ok = z - d >= 0 if sign == 1 else z + d < depth
                pl.when(ok)(lambda slot=slot: self.make(slot, p["sibling"]).wait_recv())
        result = None
        for k in range(depth):
            if_own = self.total[...]
            value = if_own
            for d in range(1, depth):
                for sign in (1, -1):
                    slot = 3 + 2 * (d - 1) + (0 if sign == 1 else 1)
                    value = jnp.where(z - d * sign == k, self.slots[slot], value)
            result = value if result is None else result + value
        return result


def scratch_of(n, length, ff):
    depth, rows = n // 4, D // n
    chunks = ff // D
    vmem, dma = pltpu.VMEM, pltpu.SemaphoreType.DMA
    gather_sems = 4 * 11 * depth
    scatter_sems = 4 * (1 + 7 * depth)
    slots = 3 + 2 * (depth - 1)
    across = 4 * Across.chunks
    spec = dict(
        four=vmem((4, rows, D), BF16),
        vecs=vmem((1, VEC_ROWS, D), BF16),
        g_four=vmem((4, D, D), BF16),
        g_vecs=vmem((1, n * VEC_ROWS, D), BF16),
        g_inner=vmem((1, D, ff), BF16),
        g_outer=vmem((1, ff, D), BF16),
        far=vmem((length, D), BF16),
        back=vmem((length, D), BF16),
        relay=vmem((length, D), BF16),
        q_even=vmem((length, D), BF16),
        q_odd=vmem((length, D), BF16),
        keys=vmem((2 * length, D), BF16),
        values=vmem((2 * length, D), BF16),
        turned=vmem((D, 2 * length), BF16),
        rows_t=vmem((D, 2 * length), BF16),
        mixed_t=vmem((D, length), BF16),
        log_sums=vmem((H * 8, length), F32),
        part_sums=vmem((H * 8, length), F32),
        small=vmem((VEC_ROWS, D), F32),
        slots=vmem((slots, VEC_ROWS, D), F32),
        bias=vmem((2 * length, length), F32),
        vec=vmem((VEC_ROWS, D), F32),
        normed=vmem((length, D), F32),
        unit1=vmem((length, D), F32),
        acc=vmem((length, D), F32),
        low_ref=vmem((length, D), BF16),
        low_t=vmem((D, length), BF16),
        g_out=vmem((length, D), BF16),
        act=vmem((chunks * length, D), BF16),
        slope=vmem((chunks * length, D), BF16),
        row_label=vmem((1, length), jnp.int32),
        row_limit=vmem((1, length), jnp.int32),
        col_label=vmem((length, 128), jnp.int32),
        send=dma((gather_sems,)),
        recv=dma((gather_sems,)),
        local=dma((4,)),
        far_send=dma((across,)),
        far_recv=dma((across,)),
        back_send=dma((across,)),
        back_recv=dma((across,)),
        sum_send=dma((slots,)),
        sum_recv=dma((slots,)),
        s_send=dma((scatter_sems,)),
        s_recv=dma((scatter_sems,)),
        hbm_sem=dma((7,)),
    )
    shapes = dict(U=(1, ff // n, D), I=(1, rows, ff), O=(1, rows, D), Q=(3, rows, D))
    for seg, shape in shapes.items():
        for name, buffer in zip("pdsl", Scatter.scratch(n, *shape, BF16)):
            spec[seg + name] = buffer
    return spec, shapes


def layer_kernel(n, names, *refs):
    smalls = refs[0:8]
    (wide, tok, w_q, w_k, w_v, w_o, inner, outer, prompt_ids, cont_ids, offsets, h_cot) = refs[8:20]
    out_wu, out_wi, out_wo, out_three, out_small, out_wide, h_result, h_rows = refs[20:28]
    b = dict(zip(names, refs[28:]))
    g_four, g_inner, g_outer, far, small = (
        b[k] for k in ("g_four", "g_inner", "g_outer", "far", "small")
    )
    q_even, q_odd, keys, values, turned, rows_t = (
        b[k] for k in ("q_even", "q_odd", "keys", "values", "turned", "rows_t")
    )
    mixed_t, log_sums, part_sums, bias, vec = (
        b[k] for k in ("mixed_t", "log_sums", "part_sums", "bias", "vec")
    )
    normed, unit1, acc, low_ref, low_t, g_out, act, slope = (
        b[k] for k in ("normed", "unit1", "acc", "low_ref", "low_t", "g_out", "act", "slope")
    )
    p = place_of(n)
    z, half, depth = p["z"], p["half"], p["depth"]
    length = tok.shape[0]
    chunks = inner.shape[2] // D
    cot_copy = pltpu.make_async_copy(h_cot, g_out, b["hbm_sem"].at[0])
    cot_copy.start()
    stacked = [
        pltpu.make_async_copy(w, b["four"].at[i], b["hbm_sem"].at[3 + i])
        for i, w in enumerate((w_q, w_k, w_v, w_o))
    ]
    for copy in stacked:
        copy.start()
    own_small(n, smalls, wide, b["vecs"])
    entry_barrier(p)
    for copy in stacked:
        copy.wait()
    forth = Across(p, tok, far, b["relay"], b["far_send"], b["far_recv"], True)
    term = far
    home = Across(p, term, b["back"], b["relay"], b["back_send"], b["back_recv"], False)
    segments = {}
    base = 0
    for j, (name, src, dst) in enumerate(
        (
            ("V", b["vecs"], b["g_vecs"]),
            ("A", b["four"], g_four),
            ("C", inner, g_inner),
            ("D", outer, g_outer),
        )
    ):
        segments[name] = Gather(p, src, dst, b["send"], b["recv"], b["local"].at[j], base)
        base += segments[name].count
    base = 0
    for name, grad, out in (
        ("U", g_outer, out_wu),
        ("I", g_inner, out_wi),
        ("O", g_four.at[3:4], out_wo),
        ("Q", g_four.at[0:3], out_three),
    ):
        buffers = [b[name + kind] for kind in "pdsl"]
        segments[name] = Scatter(p, grad, out, *buffers, b["s_send"], b["s_recv"], base)
        base += segments[name].count
    sums = SmallSum(p, small, b["slots"], b["sum_send"], b["sum_recv"], 0)

    def comm(step):
        kind = step[0]
        if kind == "tok":
            forth.begin(step[1])
        elif kind == "pass":
            forth.onward(step[1])
        elif kind == "wtok":
            forth.arrived()
        elif kind == "back":
            home.begin(step[1])
        elif kind == "onward":
            home.onward(step[1])
        elif kind == "small":
            sums.fold(step[1])
        elif kind == "start":
            segments[step[1]].start()
        elif kind == "war":
            segments[step[1]].arrived()
        else:
            getattr(segments[step[1]], kind)(step[2])

    def own_project():
        labels_of(n, prompt_ids, cont_ids, offsets, b["row_label"], b["row_limit"], b["col_label"])
        make_bias(bias, b["col_label"], b["row_label"], b["row_limit"])
        vec[...] = jnp.zeros_like(vec)

        def add_vec(i, c):
            at = pl.ds(pl.multiple_of(i * VEC_ROWS, 16), VEC_ROWS)
            vec[...] += b["g_vecs"][0, at, :].astype(F32)
            return c

        lax.fori_loop(0, n, add_vec, 0)
        query = (dot(tok[...], g_four[0]) + vec[0:1, :]).astype(BF16)
        split_heads(query.astype(F32) * 0.125, q_even, q_odd)
        keys[length : 2 * length, :] = dot(tok[...], g_four[1]).astype(BF16)
        own_values = (dot(tok[...], g_four[2]) + vec[1:2, :]).astype(BF16)
        values[length : 2 * length, :] = own_values
        turned[:, length : 2 * length] = own_values.T
        rows_t[:, length : 2 * length] = tok[...].T

    def own_pair(j):
        attend_own(j, q_even, q_odd, keys, turned, bias, acc, log_sums, part_sums)

    def far_project():
        idle = z == 0 if forth.short else z < half

        @pl.when(idle)
        def _():
            far[...] = jnp.zeros_like(far)

        keys[0:length, :] = dot(far[...], g_four[1]).astype(BF16)
        far_values = (dot(far[...], g_four[2]) + vec[1:2, :]).astype(BF16)
        values[0:length, :] = far_values
        turned[:, 0:length] = far_values.T

    def far_pair(j):
        attend_far(j, q_even, q_odd, keys, turned, bias, acc, log_sums, part_sums, mixed_t)

    def after_attention():
        first = tok[...].astype(F32) + dot(mixed_t[...].T, g_four[3]) + vec[2:3, :]
        unit1[...] = first
        unit, _ = normalize(first)
        normed[...] = unit * vec[3:4, :] + vec[4:5, :]
        low_ref[...] = normed[...].astype(BF16)
        low_t[...] = low_ref[...].T
        acc[...] = normed[...] + vec[5:6, :]

    def chunk_of(c):
        return (
            pl.ds(pl.multiple_of(c * D, D), D),
            pl.ds(pl.multiple_of(c * length, length), length),
        )

    def widen(c):
        cols, at = chunk_of(c)
        hidden = dot(low_ref[...], g_inner[0, :, cols]) + vec[pl.ds(8 + c, 1), :]
        value, grad = gelu_pair(hidden)
        act[at, :] = value.astype(BF16)
        slope[at, :] = grad.astype(BF16)

    def narrow(j):
        c = pick([segments["D"].item(i) for i in range(depth)], j) if depth == chunks else j
        cols, at = chunk_of(c)
        acc[...] += dot(act[at, :], g_outer[0, cols, :])

    result_copy = pltpu.make_async_copy(normed, h_result, b["hbm_sem"].at[1])

    def second_norm():
        for name in "VACD":
            segments[name].drain()
        forth.drain()
        cot_copy.wait()
        unit, inverse = normalize(acc[...])
        normed[...] = unit * vec[6:7, :] + vec[7:8, :]
        result_copy.start()
        g = g_out[...].astype(F32)
        small[...] = jnp.zeros_like(small)
        small[6:7, :] = column_total(g * unit)
        small[7:8, :] = column_total(g)
        g_second = normalize_back(g, vec[6:7, :], unit, inverse)
        g_out[...] = g_second.astype(BF16)
        small[5:6, :] = column_total(g_out[...].astype(F32))
        acc[...] = g_second

    def outer_back(j):
        c = pick([segments["U"].item(i) for i in range(depth)], j) if depth == chunks else j
        cols, at = chunk_of(c)
        g_hidden = dot(g_out[...], g_outer[0, cols, :], 1, 1) * slope[at, :].astype(F32)
        g_hidden = g_hidden.astype(BF16)
        slope[at, :] = g_hidden
        small[pl.ds(8 + c, 1), :] = column_total(g_hidden.astype(F32))
        g_outer[0, cols, :] = dot(act[at, :].T, g_out[...]).astype(BF16)

    def inner_back(c):
        cols, at = chunk_of(c)
        g_hidden = slope[at, :]
        acc[...] += dot(g_hidden, g_inner[0, :, cols], 1, 1)
        g_inner[0, :, cols] = dot(low_t[...], g_hidden).astype(BF16)

    g_even, g_odd, delta, grad_qt = low_ref, g_out, part_sums, low_t
    grad_k = act.at[pl.ds(0, 2 * length)]
    grad_v = act.at[pl.ds(2 * length, 2 * length)]

    def prepare():
        g_normed = acc[...]
        unit, inverse = normalize(unit1[...])
        small[3:4, :] = column_total(g_normed * unit)
        small[4:5, :] = column_total(g_normed)
        g_first = normalize_back(g_normed, vec[3:4, :], unit, inverse)
        acc[...] = g_first
        g_branch = g_first.astype(BF16)
        small[2:3, :] = column_total(g_branch.astype(F32))
        g_mixed = dot(g_branch, g_four[3], 1, 1).astype(BF16)
        g_four[3] = dot(mixed_t[...], g_branch).astype(BF16)
        split_heads(g_mixed.astype(F32), g_even, g_odd)
        g_mixed_t = g_mixed.T
        for h in range(H):
            at = slice(h * DH, (h + 1) * DH)
            part = column_total(mixed_t[at, :].astype(F32) * g_mixed_t[at, :].astype(F32))
            delta[h * 8 : (h + 1) * 8, :] = jnp.broadcast_to(part, (8, length))
        turned[...] = keys[...].T
        rows_t[:, 0:length] = far[...].T

    def pair_back(own, j):
        attend_back(
            j,
            own,
            q_even,
            q_odd,
            g_even,
            g_odd,
            keys,
            turned,
            values,
            bias,
            delta,
            log_sums,
            unit1,
            grad_qt,
            grad_k,
            grad_v,
        )

    def make_term():
        term[...] = (
            dot(grad_k[0:length, :], g_four[1], 1, 1) + dot(grad_v[0:length, :], g_four[2], 1, 1)
        ).astype(BF16)

    def row_grads():
        grad_q = grad_qt[...].T
        unit1[...] = (
            acc[...]
            + dot(grad_q, g_four[0], 1, 1)
            + dot(grad_k[length : 2 * length, :], g_four[1], 1, 1)
            + dot(grad_v[length : 2 * length, :], g_four[2], 1, 1)
        )
        small[0:1, :] = column_total(grad_q.astype(F32))
        small[1:2, :] = column_total(grad_v[...].astype(F32))
        sums.begin()

    def query_weight():
        g_four[0] = dot(rows_t[:, length : 2 * length], grad_qt[...].T).astype(BF16)

    def key_weight():
        g_four[1] = dot(rows_t[...], grad_k[...]).astype(BF16)

    def value_weight():
        g_four[2] = dot(rows_t[...], grad_v[...]).astype(BF16)

    plan = PLAN_FOUR if depth == 4 and PLAN_FOUR else default_plan(depth)
    pairs = D // 128
    run_plan(
        plan,
        comm,
        {
            "c1": own_project,
            "c2": far_project,
            "att": after_attention,
            "ln2": second_norm,
            "pre": prepare,
            "term": make_term,
            "rows": row_grads,
            "wq": query_weight,
            "wk": key_weight,
            "wv": value_weight,
        },
        {
            "o": (pairs, own_pair),
            "p": (pairs, far_pair),
            "a": (chunks, widen),
            "b": (chunks, narrow),
            "f": (chunks, outer_back),
            "g": (chunks, inner_back),
            "x": (pairs, partial(pair_back, False)),
            "y": (pairs, partial(pair_back, True)),
        },
    )
    total = sums.finish()
    s = lax.axis_index("shard")
    part = out_small.shape[1]
    quarter = n // 4
    exact = lax.Precision.HIGHEST
    place = one_hot(part, D, s * part)
    out_small[...] = lax.dot_general(
        total[0:8, :], place, (((1,), (1,)), ((), ())), precision=exact, preferred_element_type=F32
    )
    place = one_hot(4 * part, D, (s % quarter) * 4 * part)
    wide_sum = lax.dot_general(
        total[8:12, :], place, (((1,), (1,)), ((), ())), precision=exact, preferred_element_type=F32
    )
    row = lax.broadcasted_iota(jnp.int32, wide_sum.shape, 0)
    out_wide[...] = column_total(jnp.where(row == s // quarter, wide_sum, 0.0))
    home.drain()
    home.arrived()

    @pl.when(z < half)
    def _():
        unit1[...] = unit1[...] + b["back"][...].astype(F32)

    rows_copy = pltpu.make_async_copy(unit1, h_rows, b["hbm_sem"].at[2])
    rows_copy.start()
    for name in "UIOQ":
        segments[name].finish()
    result_copy.wait()
    rows_copy.wait()


def layer_call(n, smalls, wide, tok, w_q, w_k, w_v, w_o, inner, outer, prompt_ids, cont_ids, offsets, cot):
    length, ff = tok.shape[0], inner.shape[2]
    vmem = pl.BlockSpec(memory_space=pltpu.VMEM)
    smem = pl.BlockSpec(memory_space=pltpu.SMEM)
    hbm = pl.BlockSpec(memory_space=pl.ANY)
    sds = jax.ShapeDtypeStruct
    spec, shapes = scratch_of(n, length, ff)
    outs = [sds(s, F32) for s in shapes.values()]
    outs += [sds((8, D // n), F32), sds((1, ff // n), F32)]
    outs += [sds((length, D), F32), sds((length, D), F32)]
    return pl.pallas_call(
        partial(layer_kernel, n, tuple(spec)),
        out_shape=outs,
        in_specs=[vmem] * 10 + [hbm] * 4 + [vmem] * 4 + [smem, hbm],
        out_specs=[vmem] * 6 + [hbm] * 2,
        scratch_shapes=list(spec.values()),
        compiler_params=pltpu.CompilerParams(
            collective_id=0, has_side_effects=True, vmem_limit_bytes=67043328
        ),
        name="layer_step",
    )(*smalls, wide, tok, w_q, w_k, w_v, w_o, inner, outer, prompt_ids, cont_ids, offsets, cot)


def copy_out_kernel(count, *refs):
    sources, three, small, wide = refs[: count - 3], refs[count - 3], *refs[count - 2 : count]
    refs = refs[count:]
    outs, small_outs, wide_out = refs[:count], refs[count : count + 8], refs[count + 8]
    held = refs[count + 9 : 2 * count + 9]
    come, go = refs[2 * count + 9 :]
    sources = list(sources) + [three.at[i] for i in range(3)]
    coming = [pltpu.make_async_copy(a, h, come.at[i]) for i, (a, h) in enumerate(zip(sources, held))]
    going = [pltpu.make_async_copy(h, o, go.at[i]) for i, (h, o) in enumerate(zip(held, outs))]
    for copy in coming:
        copy.start()
    for i in range(8):
        small_outs[i][...] = small[i : i + 1, :]
    wide_out[...] = wide[...]
    for first, second in zip(coming, going):
        first.wait()
        second.start()
    for copy in going:
        copy.wait()


def copy_out(arrays, three, small, wide):
    vmem = pl.BlockSpec(memory_space=pltpu.VMEM)
    hbm = pl.BlockSpec(memory_space=pl.ANY)
    sds = jax.ShapeDtypeStruct
    count = len(arrays) + 3
    shapes = [a.shape for a in arrays] + [three.shape[1:]] * 3
    outs = [sds(s, F32) for s in shapes]
    outs += [sds((1, small.shape[1]), F32)] * 8 + [sds(wide.shape, F32)]
    return pl.pallas_call(
        partial(copy_out_kernel, count),
        out_shape=outs,
        in_specs=[hbm] * (count - 2) + [vmem] * 2,
        out_specs=[hbm] * count + [vmem] * 9,
        scratch_shapes=[pltpu.VMEM(s, F32) for s in shapes]
        + [pltpu.SemaphoreType.DMA((count,)), pltpu.SemaphoreType.DMA((count,))],
        compiler_params=pltpu.CompilerParams(vmem_limit_bytes=67043328),
        name="copy_out",
    )(*arrays, three, small, wide)


def body(
    tokens,
    w_query,
    b_query,
    w_key,
    w_value,
    b_value,
    w_attout,
    b_attout,
    gain_first,
    beta_first,
    w_inner,
    b_inner,
    w_outer,
    b_outer,
    gain_second,
    beta_second,
    cotangent,
    prompt_ids,
    cont_ids,
    offsets,
):
    n = lax.axis_size("shard")
    reps = lax.axis_size("rep")
    small = (
        b_query,
        b_value,
        b_attout,
        gain_first,
        beta_first,
        b_outer,
        gain_second,
        beta_second,
    )
    *owned, outcome, grad_rows = layer_call(
        n,
        [v[None] for v in small],
        b_inner[None],
        tokens,
        w_query,
        w_key,
        w_value,
        w_attout,
        w_inner[None],
        w_outer[None],
        prompt_ids,
        cont_ids,
        offsets.T,
        cotangent,
    )
    if reps > 2:
        owned = [v * 0.5 for v in lax.psum(tuple(owned), "rep")]
    own_wu, own_wi, own_wo, three, vectors, wide = owned
    own_wu, own_wi, own_wo = own_wu[0], own_wi[0], own_wo[0]
    own_wq, own_wk, own_wv = three[0], three[1], three[2]
    if reps == 2:
        finished = copy_out([outcome, grad_rows, own_wu, own_wi, own_wo], three, vectors, wide)
        outcome, grad_rows, own_wu, own_wi, own_wo, own_wq, own_wk, own_wv = finished[:8]
        vectors, wide = [v[0] for v in finished[8:16]], finished[16]
    s_bq, s_bv, s_bo, s_g1, s_be1, s_bu, s_g2, s_be2 = (vectors[i] for i in range(8))
    return (
        outcome,
        grad_rows,
        own_wq,
        s_bq,
        own_wk,
        own_wv,
        s_bv,
        own_wo,
        s_bo,
        s_g1,
        s_be1,
        own_wi,
        wide[0],
        own_wu,
        s_bu,
        s_g2,
        s_be2,
    )


def solution(mesh):
    return jax.shard_map(
        body,
        mesh=mesh,
        in_specs=(
            P(("rep", "shard"), None),
            P("shard", None),
            P("shard"),
            P("shard", None),
            P("shard", None),
            P("shard"),
            P("shard", None),
            P("shard"),
            P("shard"),
            P("shard"),
            P("shard", None),
            P("shard"),
            P("shard", None),
            P("shard"),
            P("shard"),
            P("shard"),
            P(("rep", "shard"), None),
            P(),
            P(),
            P(),
        ),
        out_specs=(
            P(("rep", "shard"), None),
            P(("rep", "shard"), None),
            P("shard", None),
            P("shard"),
            P("shard", None),
            P("shard", None),
            P("shard"),
            P("shard", None),
            P("shard"),
            P("shard"),
            P("shard"),
            P("shard", None),
            P("shard"),
            P("shard", None),
            P("shard"),
            P("shard"),
            P("shard"),
        ),
        check_vma=False,
    )
```

```python
from functools import partial

import jax
import jax.numpy as jnp
from jax import lax
from jax.experimental import pallas as pl
from jax.experimental.pallas import tpu as pltpu
from jax.sharding import PartitionSpec as P

D = 768
H = 12
DH = 64


EPSILON = 1e-12


MESHID = pl.DeviceIdType.MESH
BF16 = jnp.bfloat16
F32 = jnp.float32


def line_order(n):
    depth = n // 4
    order = []
    for z in range(depth):
        others = [k for k in range(depth) if k != z]
        others.sort(key=lambda k: (k // 2 != z // 2, abs(k - z), k))
        order.append([z] + others)
    return depth, order


def pick(table, z):
    out = table[-1]
    for i in range(len(table) - 2, -1, -1):
        out = jnp.where(z == i, table[i], out)
    return out


def place_of(n):
    depth, order = line_order(n)
    s = lax.axis_index("shard")
    r = lax.axis_index("rep")
    z, q = s // 4, s % 4
    y, x = q // 2, q % 2
    core = r % 2
    qx = y * 2 + 1 - x
    qy = (1 - y) * 2 + x
    qd = (1 - y) * 2 + 1 - x

    def device(rr, ss):
        return {"rep": rr, "shard": ss}

    half = depth // 2
    return dict(
        depth=depth,
        order=order,
        z=z,
        q=q,
        core=core,
        s=s,
        r=r,
        qx=qx,
        qy=qy,
        qd=qd,
        half=half,
        near_x=device(r, z * 4 + qx),
        near_y=device(r, z * 4 + qy),
        up=device(r, s + 4),
        down=device(r, s - 4),
        sibling=device(r + 1 - 2 * core, s),
        ahead=device(r, s + 4 * half),
        behind=device(r, s - 4 * half),
        device=device,
    )


def entry_barrier(p):
    bar = pltpu.get_barrier_semaphore()
    z, depth, half = p["z"], p["depth"], p["half"]

    def signal(where):
        pl.semaphore_signal(bar, inc=1, device_id=where, device_id_type=MESHID)

    signal(p["near_x"])
    signal(p["near_y"])
    signal(p["sibling"])
    pl.when(z + 1 < depth)(lambda: signal(p["up"]))
    pl.when(z > 0)(lambda: signal(p["down"]))
    pl.when(z < half)(lambda: signal(p["ahead"]))
    pl.when(z >= half)(lambda: signal(p["behind"]))
    pl.semaphore_wait(bar, 4 + jnp.where(z > 0, 1, 0) + jnp.where(z + 1 < depth, 1, 0))


def part_of(rows, quarter):
    top = (rows // 2 + 7) // 8 * 8
    if quarter is None:
        return 0, rows
    return (0, top) if quarter == 0 else (top, rows - top)


class Gather:
    def __init__(self, place, src, dst, send, recv, local, base):
        self.p, self.src, self.dst = place, src, dst
        self.rows, self.cols = src.shape[1], src.shape[2]
        self.send, self.recv, self.local, self.base = send, recv, local, base
        depth = place["depth"]
        self.names = {}
        for name in ("x", "y", "dx", "dy", "sx", "sy", "s0", "s1", "sz"):
            for i in range(depth):
                self.names[(name, i)] = len(self.names)
        self.line = len(self.names)
        self.count = self.line + 2 * depth

    def piece(self, chip, half, quarter=None):
        width = self.cols // 2
        cols = pl.ds(pl.multiple_of(half * width, width), width)
        first, size = part_of(self.rows, quarter)
        return self.dst.at[:, pl.ds(pl.multiple_of(chip * self.rows + first, 8), size), cols]

    def copy(self, sem, chip, where, quarter=None, own=False, half=None):
        half = self.p["core"] if half is None else half
        dst = self.piece(chip, half, quarter)
        src = dst
        if own:
            width = self.cols // 2
            src = self.src.at[:, :, pl.ds(pl.multiple_of(half * width, width), width)]
        i = self.base + (self.names[sem] if isinstance(sem, tuple) else self.line + sem)
        return pltpu.make_async_remote_copy(
            src_ref=src,
            dst_ref=dst,
            send_sem=self.send.at[i],
            recv_sem=self.recv.at[i],
            device_id=where,
            device_id_type=MESHID,
        )

    def item(self, i):
        return pick([line[i] for line in self.p["order"]], self.p["z"])

    def chips(self, i):
        k = self.item(i)
        p = self.p
        return tuple(k * 4 + p[name] for name in ("q", "qx", "qy", "qd"))

    def own_copy(self):
        me = self.p["s"]
        rows = pl.ds(pl.multiple_of(me * self.rows, self.rows), self.rows)
        return pltpu.make_async_copy(self.src, self.dst.at[:, rows, :], self.local)

    def start(self):
        p = self.p
        me, depth = p["s"], p["depth"]
        self.own_copy().start()
        pl.when(p["z"] + 1 < depth)(lambda: self.copy(0, me, p["up"], own=True).start())
        pl.when(p["z"] > 0)(lambda: self.copy(depth, me, p["down"], own=True).start())
        self.copy(("x", 0), me, p["near_x"], own=True).start()
        self.copy(("y", 0), me, p["near_y"], own=True).start()

    def flow(self, i):
        p = self.p
        z, s, depth = p["z"], p["s"], p["depth"]
        k = self.item(i)
        upward = k < z
        sem = jnp.where(upward, z - k - 1, depth + k - z - 1)
        onward = jnp.where(upward, z + 1 < depth, z > 0)
        target = p["device"](p["r"], jnp.where(upward, s + 4, s - 4))
        return sem, onward, target

    def take(self, i):
        p = self.p
        chip = self.chips(i)[0]
        sem, onward, target = self.flow(i)
        self.copy(sem, chip, p["sibling"]).wait_recv()
        pl.when(onward)(lambda: self.copy(sem + 1, chip, target).start())
        self.copy(("x", i), chip, p["near_x"]).start()
        self.copy(("y", i), chip, p["near_y"]).start()
        self.copy(("sz", i), chip, p["sibling"]).start()

    def spread(self, i):
        p = self.p
        _, cx, cy, _ = self.chips(i)
        self.copy(("x", i), cx, p["sibling"]).wait_recv()
        self.copy(("dy", i), cx, p["near_y"], quarter=0).start()
        self.copy(("sx", i), cx, p["sibling"]).start()
        self.copy(("y", i), cy, p["sibling"]).wait_recv()
        self.copy(("dx", i), cy, p["near_x"], quarter=1).start()
        self.copy(("sy", i), cy, p["sibling"]).start()

    def corner(self, i):
        p = self.p
        cd = self.chips(i)[3]
        self.copy(("dy", i), cd, p["sibling"], quarter=0).wait_recv()
        self.copy(("s0", i), cd, p["sibling"], quarter=0).start()
        self.copy(("dx", i), cd, p["sibling"], quarter=1).wait_recv()
        self.copy(("s1", i), cd, p["sibling"], quarter=1).start()

    def here(self, i):
        p = self.p
        other = 1 - p["core"]
        cm, cx, cy, cd = self.chips(i)
        if i:
            self.copy(("sz", i), cm, p["sibling"], half=other).wait_recv()
        else:
            self.own_copy().wait()
        self.copy(("sx", i), cx, p["sibling"], half=other).wait_recv()
        self.copy(("sy", i), cy, p["sibling"], half=other).wait_recv()
        self.copy(("s0", i), cd, p["sibling"], quarter=0, half=other).wait_recv()
        self.copy(("s1", i), cd, p["sibling"], quarter=1, half=other).wait_recv()

    def arrived(self):
        for i in range(self.p["depth"]):
            self.here(i)

    def drain(self):
        p = self.p
        depth = p["depth"]
        me = p["s"]
        pl.when(p["z"] + 1 < depth)(lambda: self.copy(0, me, p["up"], own=True).wait_send())
        pl.when(p["z"] > 0)(lambda: self.copy(depth, me, p["down"], own=True).wait_send())
        for i in range(depth):
            cm, cx, cy, cd = self.chips(i)
            if i:
                sem, onward, target = self.flow(i)
                pl.when(onward)(
                    lambda sem=sem, target=target, cm=cm: self.copy(sem + 1, cm, target).wait_send()
                )
                self.copy(("sz", i), cm, p["sibling"]).wait_send()
            self.copy(("x", i), cm, p["near_x"]).wait_send()
            self.copy(("y", i), cm, p["near_y"]).wait_send()
            self.copy(("dy", i), cx, p["near_y"], quarter=0).wait_send()
            self.copy(("dx", i), cy, p["near_x"], quarter=1).wait_send()
            self.copy(("sx", i), cx, p["sibling"]).wait_send()
            self.copy(("sy", i), cy, p["sibling"]).wait_send()
            self.copy(("s0", i), cd, p["sibling"], quarter=0).wait_send()
            self.copy(("s1", i), cd, p["sibling"], quarter=1).wait_send()


class Scatter:
    def __init__(self, place, grad, out, pair, diag, side, line, send, recv, base):
        self.p, self.grad, self.out = place, grad, out
        self.rows, self.cols = out.shape[1], out.shape[2]
        self.pair, self.diag, self.side, self.line = pair, diag, side, line
        self.send, self.recv, self.base = send, recv, base
        self.half = self.cols // 2
        core = place["core"]
        self.mine = pl.ds(pl.multiple_of(core * self.half, self.half), self.half)
        self.theirs = pl.ds(pl.multiple_of((1 - core) * self.half, self.half), self.half)
        depth = place["depth"]
        self.names = {}
        for name in ("p", "d0", "d1", "s0", "s1"):
            for i in range(depth):
                self.names[(name, i)] = len(self.names)
        self.names["o"] = len(self.names)
        self.first = len(self.names)
        self.count = self.first + 2 * depth

    @staticmethod
    def scratch(n, layers, rows, cols, dtype):
        depth, h = n // 4, cols // 2
        return [
            pltpu.VMEM((layers, n * rows, h), dtype),
            pltpu.VMEM((2 * depth, layers, part_of(rows, 0)[1], h), dtype),
            pltpu.VMEM((2 * depth, layers, rows, h), dtype),
            pltpu.VMEM((2 * depth - 2, layers, rows, h), dtype),
        ]

    def make(self, sem, src, dst, where):
        i = self.base + sem
        return pltpu.make_async_remote_copy(
            src_ref=src,
            dst_ref=dst,
            send_sem=self.send.at[i],
            recv_sem=self.recv.at[i],
            device_id=where,
            device_id_type=MESHID,
        )

    def item(self, i):
        depth = self.p["depth"]
        return pick([line[depth - 1 - i] for line in self.p["order"]], self.p["z"])

    def rows_of(self, k, q, quarter=None):
        first, size = part_of(self.rows, quarter)
        return pl.ds(pl.multiple_of((k * 4 + q) * self.rows + first, 8), size)

    def pair_copy(self, i):
        r = self.rows * 4
        block = pl.ds(pl.multiple_of(self.item(i) * r, r), r)
        return self.make(
            self.names[("p", i)],
            self.grad.at[:, block, self.theirs],
            self.pair.at[:, block, :],
            self.p["sibling"],
        )

    def diag_copy(self, i, quarter):
        p = self.p
        return self.make(
            self.names[("d0" if quarter == 0 else "d1", i)],
            self.grad.at[:, self.rows_of(self.item(i), p["qd"], quarter), self.mine],
            self.diag.at[i * 2 + quarter, :, pl.ds(0, part_of(self.rows, quarter)[1]), :],
            p["near_y"] if quarter == 0 else p["near_x"],
        )

    def side_copy(self, i, axis):
        p = self.p
        return self.make(
            self.names[("s0" if axis == 0 else "s1", i)],
            self.grad.at[:, self.rows_of(self.item(i), p["qx"] if axis == 0 else p["qy"]), self.mine],
            self.side.at[i * 2 + axis],
            p["near_x"] if axis == 0 else p["near_y"],
        )

    def line_copy(self, i):
        p = self.p
        k, z, depth = self.item(i), p["z"], p["depth"]
        slot = jnp.where(k > z, k - z - 1, depth - 1 + z - 1 - k)
        where = p["device"](p["r"], jnp.where(k > z, p["s"] + 4, p["s"] - 4))
        return self.make(
            self.first + slot,
            self.grad.at[:, self.rows_of(k, p["q"]), self.mine],
            self.line.at[slot],
            where,
        )

    def line_wait(self, slot):
        self.make(
            self.first + slot, self.line.at[slot], self.line.at[slot], self.p["sibling"]
        ).wait_recv()

    def out_copy(self, cols):
        return self.make(
            self.names["o"], self.out.at[:, :, cols], self.out.at[:, :, cols], self.p["sibling"]
        )

    def sweep(self, start, count, chunk, sources, store):
        def body(t, carry):
            at = pl.ds(pl.multiple_of(start + t * chunk, 8), chunk)
            low = pl.ds(pl.multiple_of(t * chunk, 8), chunk)
            total = self.grad[:, at, self.mine].astype(F32)
            for source in sources:
                total = total + source(at, low).astype(F32)
            store(at, low, total)
            return carry

        lax.fori_loop(0, count // chunk, body, 0)

    def store_grad(self, at, low, total):
        self.grad[:, at, self.mine] = total.astype(self.grad.dtype)

    def store_out(self, at, low, total):
        self.out[:, low, self.mine] = total

    def give(self, i):
        self.pair_copy(i).start()

    def merge(self, i):
        k = self.item(i)
        self.pair_copy(i).wait_recv()
        r4 = self.rows * 4
        self.sweep(k * r4, r4, 16, [lambda at, low: self.pair[:, at, :]], self.store_grad)
        self.diag_copy(i, 0).start()
        self.diag_copy(i, 1).start()

    def merge_diag(self, i):
        p = self.p
        k = self.item(i)
        for quarter, q in ((0, p["qx"]), (1, p["qy"])):
            self.diag_copy(i, quarter).wait_recv()
            slot = i * 2 + quarter
            first, size = part_of(self.rows, quarter)
            self.sweep(
                (k * 4 + q) * self.rows + first,
                size,
                8,
                [lambda at, low, slot=slot: self.diag[slot, :, low, :]],
                self.store_grad,
            )
            self.side_copy(i, quarter).start()

    def merge_side(self, i):
        p = self.p
        k, z, depth = self.item(i), p["z"], p["depth"]
        self.side_copy(i, 0).wait_recv()
        self.side_copy(i, 1).wait_recv()
        base = (k * 4 + p["q"]) * self.rows
        sides = [
            lambda at, low: self.side[i * 2, :, low, :],
            lambda at, low: self.side[i * 2 + 1, :, low, :],
        ]

        def total(slots, store):
            lines = [lambda at, low, slot=slot: self.line[slot, :, low, :] for slot in slots]
            self.sweep(base, self.rows, 16 if self.rows % 16 == 0 else 8, sides + lines, store)

        if i < depth - 1:
            has = ((k > z) & (z > 0)) | ((k < z) & (z + 1 < depth))
            slot = jnp.where(k > z, k - z, jnp.minimum(depth - 1 + z - k, 2 * depth - 3))

            @pl.when(has)
            def _():
                self.line_wait(slot)
                total([slot], self.store_grad)

            pl.when(jnp.logical_not(has))(lambda: total([], self.store_grad))
            self.line_copy(i).start()
        else:
            below, above = 0, depth - 1
            pl.when(z > 0)(lambda: self.line_wait(below))
            pl.when(z + 1 < depth)(lambda: self.line_wait(above))
            pl.when((z > 0) & (z + 1 < depth))(lambda: total([below, above], self.store_out))
            pl.when(z == 0)(lambda: total([above], self.store_out))
            pl.when(z + 1 == depth)(lambda: total([below], self.store_out))
            self.out_copy(self.mine).start()

    def finish(self):
        depth = self.p["depth"]
        self.out_copy(self.theirs).wait_recv()
        self.out_copy(self.mine).wait_send()
        for i in range(depth):
            self.pair_copy(i).wait_send()
            for side in (0, 1):
                self.diag_copy(i, side).wait_send()
                self.side_copy(i, side).wait_send()
            if i < depth - 1:
                self.line_copy(i).wait_send()


class Across:
    chunks = 4

    def __init__(self, place, src, dst, relay, send, recv, forward):
        p = place
        self.p, self.src, self.dst, self.relay = p, src, dst, relay
        self.send, self.recv = send, recv
        depth, z = p["depth"], p["z"]
        self.short = depth == 4
        self.at = z if forward else depth - 1 - z
        self.next = p["up"] if forward else p["down"]
        self.far = p["ahead"] if forward else p["behind"]

    def rows(self, j):
        size = self.src.shape[0] // self.chunks
        return pl.ds(j * size, size)

    def make(self, kind, j, src, dst, where):
        rows = self.rows(j)
        i = kind * self.chunks + j
        return pltpu.make_async_remote_copy(
            src_ref=src.at[rows],
            dst_ref=dst.at[rows],
            send_sem=self.send.at[i],
            recv_sem=self.recv.at[i],
            device_id=where,
            device_id_type=MESHID,
        )

    def begin(self, j):
        half = self.p["depth"] // 2
        if self.short:
            to_dst = self.make(0, j, self.src, self.dst, self.next)
            to_relay = self.make(1, j, self.src, self.relay, self.next)
            pl.when(self.at == 0)(lambda: to_dst.start())
            pl.when(self.at == 1)(lambda: to_relay.start())
        else:
            direct = self.make(0, j, self.src, self.dst, self.far)
            pl.when(self.at < half)(lambda: direct.start())

    def onward(self, j):
        if self.short:
            hold = self.make(0, j, self.src, self.dst, self.next)
            held = self.make(1, j, self.src, self.relay, self.next)
            from_dst = self.make(2, j, self.dst, self.dst, self.next)
            from_relay = self.make(3, j, self.relay, self.dst, self.next)

            @pl.when(self.at == 1)
            def _():
                hold.wait_recv()
                from_dst.start()

            @pl.when(self.at == 2)
            def _():
                held.wait_recv()
                from_relay.start()

    def arrived(self):
        half = self.p["depth"] // 2
        for j in range(self.chunks):
            if self.short:
                second = self.make(2, j, self.dst, self.dst, self.next)
                third = self.make(3, j, self.relay, self.dst, self.next)
                pl.when(self.at == 2)(lambda copy=second: copy.wait_recv())
                pl.when(self.at == 3)(lambda copy=third: copy.wait_recv())
            else:
                direct = self.make(0, j, self.src, self.dst, self.far)
                pl.when(self.at >= half)(lambda copy=direct: copy.wait_recv())

    def drain(self):
        half = self.p["depth"] // 2
        for j in range(self.chunks):
            if self.short:
                copies = (
                    self.make(0, j, self.src, self.dst, self.next),
                    self.make(1, j, self.src, self.relay, self.next),
                    self.make(2, j, self.dst, self.dst, self.next),
                    self.make(3, j, self.relay, self.dst, self.next),
                )
                pl.when(self.at == 0)(lambda: copies[0].wait_send())

                @pl.when(self.at == 1)
                def _():
                    copies[1].wait_send()
                    copies[2].wait_send()

                pl.when(self.at == 2)(lambda: copies[3].wait_send())
            else:
                direct = self.make(0, j, self.src, self.dst, self.far)
                pl.when(self.at < half)(lambda copy=direct: copy.wait_send())


VEC_ROWS = 16


def dot(a, b, ca=1, cb=0):
    return lax.dot_general(a, b, (((ca,), (cb,)), ((), ())), preferred_element_type=F32)


def mean_last(v):
    return jnp.sum(v, axis=-1, keepdims=True) * (1.0 / v.shape[-1])


def normalize(v):
    c = v - mean_last(v)
    inverse = lax.rsqrt(mean_last(c * c) + EPSILON)
    return c * inverse, inverse


def normalize_back(grad, gain, unit, inverse):
    g = grad * gain
    return inverse * (g - mean_last(g) - unit * mean_last(g * unit))


def gelu_pair(x):
    tail = jnp.exp(-0.5 * (x * x))
    t = 1.0 / (1.0 + (0.3275911 * 0.7071067811865476) * jnp.abs(x))
    poly = 1.061405429 * t - 1.453152027
    poly = poly * t + 1.421413741
    poly = poly * t - 0.284496736
    poly = poly * t + 0.254829592
    low = (0.5 * t) * poly * tail
    cdf = jnp.where(x < 0, low, 1.0 - low)
    return x * cdf, cdf + x * (tail * 0.3989422804014327)


def column_total(v):
    return jnp.sum(v, axis=0, keepdims=True)


def even_lanes(shape):
    return lax.broadcasted_iota(jnp.int32, shape, 1) % 128 < 64


def split_heads(x, even_ref, odd_ref):
    keep = even_lanes(x.shape)
    zero = jnp.zeros_like(x)
    even_ref[...] = jnp.where(keep, x, zero).astype(BF16)
    odd_ref[...] = jnp.where(keep, zero, x).astype(BF16)


def make_bias(bias, col_label, row_label, row_limit):
    length = row_label.shape[1]
    for b in range(0, length, 128):
        at = pl.ds(b, 128)
        row = lax.broadcasted_iota(jnp.int32, (128, length), 0) + b
        bias[at, :] = jnp.where(row < row_limit[...], 0.0, -1e30)
        same = col_label[at, 0:1] == row_label[...]
        bias[pl.ds(length + b, 128), :] = jnp.where(same, 0.0, -1e30)


def head_slices(j, side):
    head = pl.ds(pl.multiple_of(j * 128 + side * DH, DH), DH)
    row = pl.ds(pl.multiple_of(j * 16 + side * 8, 8), 8)
    return head, row


def part_block(part, j, side, b):
    index = j * 4 + side * 2 + b
    return part.at[
        pl.ds(pl.multiple_of(index // 3 * DH, DH), DH),
        pl.ds(pl.multiple_of(index % 3 * 256, 256), 256),
    ]


def attend_own(j, q_even, q_odd, keys, values_t, bias, part, tops, sums):
    lanes = pl.ds(pl.multiple_of(j * 128, 128), 128)
    length = q_even.shape[0]
    own = pl.ds(length, length)
    width = 256
    for b in range(0, length, width):
        block = pl.ds(b, width)
        for side, q_ref in ((0, q_even), (1, q_odd)):
            head, row = head_slices(j, side)
            scores = dot(keys[own, lanes], q_ref[block, lanes], 1, 1) + bias[own, block]
            top = jnp.max(scores, axis=0, keepdims=True)
            expo = jnp.exp(scores - top)
            part_block(part, j, side, b // width)[...] = dot(
                values_t[head, own], expo.astype(BF16)
            )
            tops[row, block] = jnp.broadcast_to(top, (8, width))
            sums[row, block] = jnp.broadcast_to(column_total(expo), (8, width))


def attend_far(j, q_even, q_odd, keys, values_t, bias, part, tops, sums, mixed_t):
    lanes = pl.ds(pl.multiple_of(j * 128, 128), 128)
    length = q_even.shape[0]
    far = pl.ds(0, length)
    width = 256
    for b in range(0, length, width):
        block = pl.ds(b, width)
        for side, q_ref in ((0, q_even), (1, q_odd)):
            head, row = head_slices(j, side)
            scores = dot(keys[far, lanes], q_ref[block, lanes], 1, 1) + bias[far, block]
            before = tops[row, block][0:1]
            top = jnp.maximum(jnp.max(scores, axis=0, keepdims=True), before)
            expo = jnp.exp(scores - top)
            fade = jnp.exp(before - top)
            total = sums[row, block][0:1] * fade + column_total(expo)
            mixed = part_block(part, j, side, b // width)[...] * fade + dot(values_t[head, far], expo.astype(BF16))
            mixed_t[head, block] = (mixed * (1.0 / total)).astype(BF16)
            tops[row, block] = jnp.broadcast_to(top + jnp.log(total), (8, width))


def attend_back(
    j, own, q_even, q_odd, g_even, g_odd, keys, keys_t, values, bias, delta, log_sums, part, grad_qt, grad_k, grad_v
):
    lanes = pl.ds(pl.multiple_of(j * 128, 128), 128)
    length = q_even.shape[0]
    half = pl.ds(length if own else 0, length)
    width = 256
    total_k, total_v = 0.0, 0.0
    for b in range(0, length, width):
        block = pl.ds(b, width)
        for side, q_ref, g_ref in ((0, q_even, g_even), (1, q_odd, g_odd)):
            head, row = head_slices(j, side)
            scores = dot(keys[half, lanes], q_ref[block, lanes], 1, 1) + bias[half, block]
            probs = jnp.exp(scores - log_sums[row, block][0:1])
            grad_p = dot(values[half, lanes], g_ref[block, lanes], 1, 1)
            grad_s = (probs * (grad_p - delta[row, block][0:1])).astype(BF16)
            total_v = total_v + dot(probs.astype(BF16), g_ref[block, lanes])
            total_k = total_k + dot(grad_s, q_ref[block, lanes])
            grad_q = dot(keys_t[head, half], grad_s)
            held = part_block(part, j, side, b // width)
            if own:
                grad_qt[head, block] = ((held[...] + grad_q) * 0.125).astype(BF16)
            else:
                held[...] = grad_q
    grad_k[half, lanes] = total_k.astype(BF16)
    grad_v[half, lanes] = total_v.astype(BF16)


def one_hot(rows, cols, shift):
    row = lax.broadcasted_iota(jnp.int32, (rows, cols), 0)
    col = lax.broadcasted_iota(jnp.int32, (rows, cols), 1)
    return jnp.where(col == row + shift, 1.0, 0.0)


def own_small(n, smalls, wide, out):
    s = lax.axis_index("shard")
    part = smalls[0].shape[1]
    quarter = n // 4
    out[...] = jnp.zeros_like(out)
    place = one_hot(part, D, s * part).astype(BF16)
    for i, v in enumerate(smalls):
        out[0, i : i + 1, :] = dot(v[...], place).astype(BF16)
    place = one_hot(4 * part, D, (s % quarter) * 4 * part).astype(BF16)
    piece = dot(wide[...].astype(F32)[None, :].astype(BF16), place)
    row = lax.broadcasted_iota(jnp.int32, (4, D), 0)
    out[0, 8:12, :] = jnp.where(row == s // quarter, piece, 0.0).astype(BF16)


def labels_of(n, prompt_ids, cont_ids, offsets, row_label, row_limit, col_label):
    half = n // 2
    s = lax.axis_index("shard")
    is_cont = s >= half
    group = lax.axis_index("rep") * half + s % half
    own = jnp.where(
        is_cont, cont_ids[pl.ds(group, 1), :], prompt_ids[pl.ds(group, 1), :]
    )
    limit = jnp.zeros_like(own)
    for k in range(offsets.shape[0]):
        limit = jnp.where(own == k, offsets[k, group], limit)
    row_label[...] = own
    row_limit[...] = jnp.where(is_cont, limit, 0)
    col_label[...] = jnp.broadcast_to(own, (128, own.shape[1])).T


PLAN_FOUR = (
    ('start', 'V'),
    ('start', 'A'),
    ('spread', 'V', 0),
    ('take', 'V', 1),
    ('start', 'D'),
    ('take', 'A', 1),
    ('take', 'A', 2),
    ('take', 'V', 3),
    ('take', 'V', 2),
    ('tok', 0),
    ('take', 'A', 3),
    ('start', 'C'),
    ('spread', 'A', 1),
    ('spread', 'V', 3),
    ('spread', 'V', 1),
    ('pass', 0),
    ('spread', 'A', 0),
    ('tok', 1),
    ('spread', 'A', 3),
    ('spread', 'V', 2),
    ('spread', 'A', 2),
    ('take', 'C', 2),
    ('take', 'D', 1),
    ('tok', 2),
    ('corner', 'V', 0),
    ('take', 'D', 2),
    ('corner', 'V', 1),
    ('corner', 'A', 0),
    ('corner', 'A', 3),
    ('corner', 'V', 3),
    ('corner', 'V', 2),
    ('take', 'C', 1),
    ('war', 'V'),
    ('corner', 'A', 1),
    ('corner', 'A', 2),
    ('tok', 3),
    ('pass', 1),
    ('war', 'A'),
    ('c', 'c1'),
    ('take', 'D', 3),
    ('c', 'o0'),
    ('c', 'o1'),
    ('pass', 2),
    ('c', 'o2'),
    ('c', 'o3'),
    ('take', 'C', 3),
    ('spread', 'C', 0),
    ('pass', 3),
    ('spread', 'D', 1),
    ('c', 'o4'),
    ('spread', 'C', 1),
    ('spread', 'D', 0),
    ('c', 'o5'),
    ('spread', 'C', 2),
    ('spread', 'D', 2),
    ('spread', 'D', 3),
    ('wtok',),
    ('c', 'c2'),
    ('c', 'p0'),
    ('c', 'p1'),
    ('corner', 'D', 1),
    ('c', 'p2'),
    ('c', 'p3'),
    ('c', 'p4'),
    ('spread', 'C', 3),
    ('corner', 'C', 2),
    ('corner', 'C', 1),
    ('corner', 'C', 0),
    ('c', 'p5'),
    ('c', 'att'),
    ('corner', 'D', 2),
    ('corner', 'D', 0),
    ('corner', 'D', 3),
    ('here', 'D', 0),
    ('here', 'D', 1),
    ('here', 'D', 2),
    ('here', 'D', 3),
    ('corner', 'C', 3),
    ('war', 'C'),
    ('c', 'a0'),
    ('c', 'a1'),
    ('c', 'a2'),
    ('c', 'a3'),
    ('c', 'b0'),
    ('c', 'b1'),
    ('c', 'b2'),
    ('c', 'b3'),
    ('c', 'ln2'),
    ('c', 'f0'),
    ('give', 'U', 0),
    ('c', 'f1'),
    ('give', 'U', 1),
    ('merge', 'U', 0),
    ('c', 'f2'),
    ('merge', 'U', 1),
    ('merge_diag', 'U', 0),
    ('c', 'f3'),
    ('c', 'g0'),
    ('c', 'g1'),
    ('c', 'g2'),
    ('c', 'g3'),
    ('give', 'I', 0),
    ('give', 'U', 2),
    ('give', 'I', 1),
    ('give', 'I', 2),
    ('merge_diag', 'U', 1),
    ('c', 'pre'),
    ('merge_side', 'U', 0),
    ('give', 'O', 0),
    ('merge', 'I', 0),
    ('give', 'I', 3),
    ('merge', 'U', 2),
    ('c', 'x0'),
    ('c', 'x1'),
    ('merge_side', 'U', 1),
    ('give', 'U', 3),
    ('merge_diag', 'I', 0),
    ('c', 'x2'),
    ('merge_diag', 'U', 2),
    ('c', 'x3'),
    ('c', 'x4'),
    ('merge_side', 'I', 0),
    ('give', 'O', 1),
    ('merge', 'I', 1),
    ('c', 'x5'),
    ('c', 'term'),
    ('back', 0),
    ('merge', 'O', 0),
    ('give', 'O', 2),
    ('merge', 'I', 3),
    ('merge', 'U', 3),
    ('back', 1),
    ('merge', 'I', 2),
    ('merge_diag', 'I', 1),
    ('c', 'y0'),
    ('c', 'y1'),
    ('back', 2),
    ('c', 'y2'),
    ('c', 'y3'),
    ('merge', 'O', 1),
    ('merge_diag', 'I', 2),
    ('back', 3),
    ('c', 'y4'),
    ('merge_side', 'U', 2),
    ('merge_diag', 'I', 3),
    ('c', 'y5'),
    ('c', 'rows'),
    ('merge', 'O', 2),
    ('onward', 0),
    ('merge_diag', 'O', 1),
    ('c', 'wq'),
    ('merge_diag', 'O', 0),
    ('c', 'wk'),
    ('small', 0),
    ('c', 'wv'),
    ('give', 'Q', 0),
    ('give', 'O', 3),
    ('merge_diag', 'O', 2),
    ('give', 'Q', 1),
    ('give', 'Q', 2),
    ('give', 'Q', 3),
    ('onward', 1),
    ('merge_side', 'I', 1),
    ('small', 1),
    ('merge_side', 'I', 2),
    ('merge', 'Q', 0),
    ('merge_diag', 'Q', 0),
    ('small', 2),
    ('merge_side', 'O', 0),
    ('merge', 'Q', 1),
    ('merge', 'Q', 2),
    ('merge_side', 'Q', 0),
    ('onward', 2),
    ('merge_diag', 'Q', 2),
    ('merge_diag', 'Q', 1),
    ('merge', 'O', 3),
    ('merge_side', 'O', 1),
    ('merge_side', 'O', 2),
    ('merge_diag', 'U', 3),
    ('merge_diag', 'O', 3),
    ('merge', 'Q', 3),
    ('merge_side', 'Q', 1),
    ('merge_side', 'Q', 2),
    ('onward', 3),
    ('merge_diag', 'Q', 3),
    ('merge_side', 'O', 3),
    ('merge_side', 'I', 3),
    ('merge_side', 'U', 3),
    ('merge_side', 'Q', 3),
)


def default_plan(depth):
    plan = [("start", "V"), ("start", "A")]
    plan += [("tok", j) for j in range(Across.chunks)]
    plan += [("pass", j) for j in range(Across.chunks)]
    for seg in "VACD":
        if seg in "CD":
            plan.append(("start", seg))
        for i in range(depth):
            if i:
                plan.append(("take", seg, i))
            plan.append(("spread", seg, i))
            if i:
                plan.append(("corner", seg, i - 1))
        plan.append(("corner", seg, depth - 1))
        plan += [("war", seg)] if seg != "D" else [("here", seg, i) for i in range(depth)]
    plan += [("wtok",), ("c", "c1")] + [("c", "o%d" % i) for i in range(6)] + [("c", "c2")]
    plan += [("c", "p%d" % i) for i in range(6)] + [("c", "att")]
    plan += [("c", "a%d" % i) for i in range(4)] + [("c", "b%d" % i) for i in range(4)]
    plan += [("c", "ln2")] + [("c", "f%d" % i) for i in range(4)]
    plan += [("c", "g%d" % i) for i in range(4)] + [("c", "pre")]
    plan += [("give", s, i) for s in "UIO" for i in range(depth)]
    plan += [("c", "x%d" % i) for i in range(6)] + [("c", "term")]
    plan += [("back", j) for j in range(Across.chunks)]
    plan += [("onward", j) for j in range(Across.chunks)]
    plan += [("c", "y%d" % i) for i in range(6)]
    plan += [("c", "rows"), ("c", "wq"), ("c", "wk"), ("c", "wv")]
    plan += [("give", s, i) for s in "Q" for i in range(depth)]
    plan += [("small", j) for j in range(3)]
    for seg in "UIOQ":
        for i in range(depth + 2):
            if i < depth:
                plan.append(("merge", seg, i))
            if 0 <= i - 1 < depth:
                plan.append(("merge_diag", seg, i - 1))
            if 0 <= i - 2 < depth:
                plan.append(("merge_side", seg, i - 2))
    return plan


def run_plan(plan, comm, single, loops):
    at = 0
    while at < len(plan):
        step = plan[at]
        if step[0] != "c":
            comm(step)
            at += 1
        elif step[1] in single:
            single[step[1]]()
            at += 1
        else:
            kind = step[1][0]
            count, chunk = loops[kind]
            after = []
            for _ in range(count):
                at += 1
                steps = []
                last = len(after) == count - 1
                while not last and plan[at][0] != "c":
                    steps.append(plan[at])
                    at += 1
                after.append(steps)

            def body(j, carry, after=after, chunk=chunk):
                chunk(j)
                for k, steps in enumerate(after):
                    if steps:

                        @pl.when(j == k)
                        def _():
                            for step in steps:
                                comm(step)

                return carry

            lax.fori_loop(0, count, body, 0)


class SmallSum:
    def __init__(self, place, total, slots, send, recv, base):
        self.p, self.total, self.slots = place, total, slots
        self.send, self.recv, self.base = send, recv, base

    def make(self, slot, where):
        return pltpu.make_async_remote_copy(
            src_ref=self.total,
            dst_ref=self.slots.at[slot],
            send_sem=self.send.at[self.base + slot],
            recv_sem=self.recv.at[self.base + slot],
            device_id=where,
            device_id_type=MESHID,
        )

    def stage(self, k):
        return self.make(k, (self.p["sibling"], self.p["near_x"], self.p["near_y"])[k])

    def begin(self):
        self.stage(0).start()

    def fold(self, k):
        copy = self.stage(k)
        copy.wait_send()
        copy.wait_recv()
        self.total[...] = self.total[...] + self.slots[k]
        if k < 2:
            self.stage(k + 1).start()
        else:
            self.along(lambda copy: copy.start())

    def along(self, act):
        p = self.p
        z, depth = p["z"], p["depth"]
        for d in range(1, depth):
            for sign in (1, -1):
                target = p["device"](p["r"], p["s"] + 4 * d * sign)
                slot = 3 + 2 * (d - 1) + (0 if sign == 1 else 1)
                ok = z + d < depth if sign == 1 else z - d >= 0
                pl.when(ok)(lambda slot=slot, target=target: act(self.make(slot, target)))

    def finish(self):
        p = self.p
        z, depth = p["z"], p["depth"]
        self.along(lambda copy: copy.wait_send())
        terms = []
        for d in range(1, depth):
            for sign in (1, -1):
                slot = 3 + 2 * (d - 1) + (0 if sign == 1 else 1)
                ok = z - d >= 0 if sign == 1 else z + d < depth
                pl.when(ok)(lambda slot=slot: self.make(slot, p["sibling"]).wait_recv())
        result = None
        for k in range(depth):
            if_own = self.total[...]
            value = if_own
            for d in range(1, depth):
                for sign in (1, -1):
                    slot = 3 + 2 * (d - 1) + (0 if sign == 1 else 1)
                    value = jnp.where(z - d * sign == k, self.slots[slot], value)
            result = value if result is None else result + value
        return result


def scratch_of(n, length, ff):
    depth, rows = n // 4, D // n
    chunks = ff // D
    vmem, dma = pltpu.VMEM, pltpu.SemaphoreType.DMA
    gather_sems = 4 * 11 * depth
    scatter_sems = 4 * (1 + 7 * depth)
    slots = 3 + 2 * (depth - 1)
    across = 4 * Across.chunks
    spec = dict(
        four=vmem((4, rows, D), BF16),
        vecs=vmem((1, VEC_ROWS, D), BF16),
        g_four=vmem((4, D, D), BF16),
        g_vecs=vmem((1, n * VEC_ROWS, D), BF16),
        g_inner=vmem((1, D, ff), BF16),
        g_outer=vmem((1, ff, D), BF16),
        far=vmem((length, D), BF16),
        back=vmem((length, D), BF16),
        relay=vmem((length, D), BF16),
        q_even=vmem((length, D), BF16),
        q_odd=vmem((length, D), BF16),
        keys=vmem((2 * length, D), BF16),
        values=vmem((2 * length, D), BF16),
        turned=vmem((D, 2 * length), BF16),
        rows_t=vmem((D, 2 * length), BF16),
        mixed_t=vmem((D, length), BF16),
        log_sums=vmem((H * 8, length), F32),
        part_sums=vmem((H * 8, length), F32),
        small=vmem((VEC_ROWS, D), F32),
        slots=vmem((slots, VEC_ROWS, D), F32),
        bias=vmem((2 * length, length), F32),
        vec=vmem((VEC_ROWS, D), F32),
        normed=vmem((length, D), F32),
        unit1=vmem((length, D), F32),
        acc=vmem((length, D), F32),
        low_ref=vmem((length, D), BF16),
        low_t=vmem((D, length), BF16),
        g_out=vmem((length, D), BF16),
        act=vmem((chunks * length, D), BF16),
        slope=vmem((chunks * length, D), BF16),
        row_label=vmem((1, length), jnp.int32),
        row_limit=vmem((1, length), jnp.int32),
        col_label=vmem((length, 128), jnp.int32),
        send=dma((gather_sems,)),
        recv=dma((gather_sems,)),
        local=dma((4,)),
        far_send=dma((across,)),
        far_recv=dma((across,)),
        back_send=dma((across,)),
        back_recv=dma((across,)),
        sum_send=dma((slots,)),
        sum_recv=dma((slots,)),
        s_send=dma((scatter_sems,)),
        s_recv=dma((scatter_sems,)),
        hbm_sem=dma((7,)),
    )
    shapes = dict(U=(1, ff // n, D), I=(1, rows, ff), O=(1, rows, D), Q=(3, rows, D))
    for seg, shape in shapes.items():
        for name, buffer in zip("pdsl", Scatter.scratch(n, *shape, BF16)):
            spec[seg + name] = buffer
    return spec, shapes


def layer_kernel(n, names, *refs):
    smalls = refs[0:8]
    (wide, tok, w_q, w_k, w_v, w_o, inner, outer, prompt_ids, cont_ids, offsets, h_cot) = refs[8:20]
    out_wu, out_wi, out_wo, out_three, out_small, out_wide, h_result, h_rows = refs[20:28]
    b = dict(zip(names, refs[28:]))
    g_four, g_inner, g_outer, far, small = (
        b[k] for k in ("g_four", "g_inner", "g_outer", "far", "small")
    )
    q_even, q_odd, keys, values, turned, rows_t = (
        b[k] for k in ("q_even", "q_odd", "keys", "values", "turned", "rows_t")
    )
    mixed_t, log_sums, part_sums, bias, vec = (
        b[k] for k in ("mixed_t", "log_sums", "part_sums", "bias", "vec")
    )
    normed, unit1, acc, low_ref, low_t, g_out, act, slope = (
        b[k] for k in ("normed", "unit1", "acc", "low_ref", "low_t", "g_out", "act", "slope")
    )
    p = place_of(n)
    z, half, depth = p["z"], p["half"], p["depth"]
    length = tok.shape[0]
    chunks = inner.shape[2] // D
    cot_copy = pltpu.make_async_copy(h_cot, g_out, b["hbm_sem"].at[0])
    cot_copy.start()
    stacked = [
        pltpu.make_async_copy(w, b["four"].at[i], b["hbm_sem"].at[3 + i])
        for i, w in enumerate((w_q, w_k, w_v, w_o))
    ]
    for copy in stacked:
        copy.start()
    own_small(n, smalls, wide, b["vecs"])
    entry_barrier(p)
    for copy in stacked:
        copy.wait()
    forth = Across(p, tok, far, b["relay"], b["far_send"], b["far_recv"], True)
    term = far
    home = Across(p, term, b["back"], b["relay"], b["back_send"], b["back_recv"], False)
    segments = {}
    base = 0
    for j, (name, src, dst) in enumerate(
        (
            ("V", b["vecs"], b["g_vecs"]),
            ("A", b["four"], g_four),
            ("C", inner, g_inner),
            ("D", outer, g_outer),
        )
    ):
        segments[name] = Gather(p, src, dst, b["send"], b["recv"], b["local"].at[j], base)
        base += segments[name].count
    base = 0
    for name, grad, out in (
        ("U", g_outer, out_wu),
        ("I", g_inner, out_wi),
        ("O", g_four.at[3:4], out_wo),
        ("Q", g_four.at[0:3], out_three),
    ):
        buffers = [b[name + kind] for kind in "pdsl"]
        segments[name] = Scatter(p, grad, out, *buffers, b["s_send"], b["s_recv"], base)
        base += segments[name].count
    sums = SmallSum(p, small, b["slots"], b["sum_send"], b["sum_recv"], 0)

    def comm(step):
        kind = step[0]
        if kind == "tok":
            forth.begin(step[1])
        elif kind == "pass":
            forth.onward(step[1])
        elif kind == "wtok":
            forth.arrived()
        elif kind == "back":
            home.begin(step[1])
        elif kind == "onward":
            home.onward(step[1])
        elif kind == "small":
            sums.fold(step[1])
        elif kind == "start":
            segments[step[1]].start()
        elif kind == "war":
            segments[step[1]].arrived()
        else:
            getattr(segments[step[1]], kind)(step[2])

    def own_project():
        labels_of(n, prompt_ids, cont_ids, offsets, b["row_label"], b["row_limit"], b["col_label"])
        make_bias(bias, b["col_label"], b["row_label"], b["row_limit"])
        vec[...] = jnp.zeros_like(vec)

        def add_vec(i, c):
            at = pl.ds(pl.multiple_of(i * VEC_ROWS, 16), VEC_ROWS)
            vec[...] += b["g_vecs"][0, at, :].astype(F32)
            return c

        lax.fori_loop(0, n, add_vec, 0)
        query = (dot(tok[...], g_four[0]) + vec[0:1, :]).astype(BF16)
        split_heads(query.astype(F32) * 0.125, q_even, q_odd)
        keys[length : 2 * length, :] = dot(tok[...], g_four[1]).astype(BF16)
        own_values = (dot(tok[...], g_four[2]) + vec[1:2, :]).astype(BF16)
        values[length : 2 * length, :] = own_values
        turned[:, length : 2 * length] = own_values.T
        rows_t[:, length : 2 * length] = tok[...].T

    def own_pair(j):
        attend_own(j, q_even, q_odd, keys, turned, bias, acc, log_sums, part_sums)

    def far_project():
        idle = z == 0 if forth.short else z < half

        @pl.when(idle)
        def _():
            far[...] = jnp.zeros_like(far)

        keys[0:length, :] = dot(far[...], g_four[1]).astype(BF16)
        far_values = (dot(far[...], g_four[2]) + vec[1:2, :]).astype(BF16)
        values[0:length, :] = far_values
        turned[:, 0:length] = far_values.T

    def far_pair(j):
        attend_far(j, q_even, q_odd, keys, turned, bias, acc, log_sums, part_sums, mixed_t)

    def after_attention():
        first = tok[...].astype(F32) + dot(mixed_t[...].T, g_four[3]) + vec[2:3, :]
        unit1[...] = first
        unit, _ = normalize(first)
        normed[...] = unit * vec[3:4, :] + vec[4:5, :]
        low_ref[...] = normed[...].astype(BF16)
        low_t[...] = low_ref[...].T
        acc[...] = normed[...] + vec[5:6, :]

    def chunk_of(c):
        return (
            pl.ds(pl.multiple_of(c * D, D), D),
            pl.ds(pl.multiple_of(c * length, length), length),
        )

    def widen(c):
        cols, at = chunk_of(c)
        hidden = dot(low_ref[...], g_inner[0, :, cols]) + vec[pl.ds(8 + c, 1), :]
        value, grad = gelu_pair(hidden)
        act[at, :] = value.astype(BF16)
        slope[at, :] = grad.astype(BF16)

    def narrow(j):
        c = pick([segments["D"].item(i) for i in range(depth)], j) if depth == chunks else j
        cols, at = chunk_of(c)
        acc[...] += dot(act[at, :], g_outer[0, cols, :])

    result_copy = pltpu.make_async_copy(normed, h_result, b["hbm_sem"].at[1])

    def second_norm():
        for name in "VACD":
            segments[name].drain()
        forth.drain()
        cot_copy.wait()
        unit, inverse = normalize(acc[...])
        normed[...] = unit * vec[6:7, :] + vec[7:8, :]
        result_copy.start()
        g = g_out[...].astype(F32)
        small[...] = jnp.zeros_like(small)
        small[6:7, :] = column_total(g * unit)
        small[7:8, :] = column_total(g)
        g_second = normalize_back(g, vec[6:7, :], unit, inverse)
        g_out[...] = g_second.astype(BF16)
        small[5:6, :] = column_total(g_out[...].astype(F32))
        acc[...] = g_second

    def outer_back(j):
        c = pick([segments["U"].item(i) for i in range(depth)], j) if depth == chunks else j
        cols, at = chunk_of(c)
        g_hidden = dot(g_out[...], g_outer[0, cols, :], 1, 1) * slope[at, :].astype(F32)
        g_hidden = g_hidden.astype(BF16)
        slope[at, :] = g_hidden
        small[pl.ds(8 + c, 1), :] = column_total(g_hidden.astype(F32))
        g_outer[0, cols, :] = dot(act[at, :].T, g_out[...]).astype(BF16)

    def inner_back(c):
        cols, at = chunk_of(c)
        g_hidden = slope[at, :]
        acc[...] += dot(g_hidden, g_inner[0, :, cols], 1, 1)
        g_inner[0, :, cols] = dot(low_t[...], g_hidden).astype(BF16)

    g_even, g_odd, delta, grad_qt = low_ref, g_out, part_sums, low_t
    grad_k = act.at[pl.ds(0, 2 * length)]
    grad_v = act.at[pl.ds(2 * length, 2 * length)]

    def prepare():
        g_normed = acc[...]
        unit, inverse = normalize(unit1[...])
        small[3:4, :] = column_total(g_normed * unit)
        small[4:5, :] = column_total(g_normed)
        g_first = normalize_back(g_normed, vec[3:4, :], unit, inverse)
        acc[...] = g_first
        g_branch = g_first.astype(BF16)
        small[2:3, :] = column_total(g_branch.astype(F32))
        g_mixed = dot(g_branch, g_four[3], 1, 1).astype(BF16)
        g_four[3] = dot(mixed_t[...], g_branch).astype(BF16)
        split_heads(g_mixed.astype(F32), g_even, g_odd)
        g_mixed_t = g_mixed.T
        for h in range(H):
            at = slice(h * DH, (h + 1) * DH)
            part = column_total(mixed_t[at, :].astype(F32) * g_mixed_t[at, :].astype(F32))
            delta[h * 8 : (h + 1) * 8, :] = jnp.broadcast_to(part, (8, length))
        turned[...] = keys[...].T
        rows_t[:, 0:length] = far[...].T

    def pair_back(own, j):
        attend_back(
            j,
            own,
            q_even,
            q_odd,
            g_even,
            g_odd,
            keys,
            turned,
            values,
            bias,
            delta,
            log_sums,
            unit1,
            grad_qt,
            grad_k,
            grad_v,
        )

    def make_term():
        term[...] = (
            dot(grad_k[0:length, :], g_four[1], 1, 1) + dot(grad_v[0:length, :], g_four[2], 1, 1)
        ).astype(BF16)

    def row_grads():
        grad_q = grad_qt[...].T
        unit1[...] = (
            acc[...]
            + dot(grad_q, g_four[0], 1, 1)
            + dot(grad_k[length : 2 * length, :], g_four[1], 1, 1)
            + dot(grad_v[length : 2 * length, :], g_four[2], 1, 1)
        )
        small[0:1, :] = column_total(grad_q.astype(F32))
        small[1:2, :] = column_total(grad_v[...].astype(F32))
        sums.begin()

    def query_weight():
        g_four[0] = dot(rows_t[:, length : 2 * length], grad_qt[...].T).astype(BF16)

    def key_weight():
        g_four[1] = dot(rows_t[...], grad_k[...]).astype(BF16)

    def value_weight():
        g_four[2] = dot(rows_t[...], grad_v[...]).astype(BF16)

    plan = PLAN_FOUR if depth == 4 and PLAN_FOUR else default_plan(depth)
    pairs = D // 128
    run_plan(
        plan,
        comm,
        {
            "c1": own_project,
            "c2": far_project,
            "att": after_attention,
            "ln2": second_norm,
            "pre": prepare,
            "term": make_term,
            "rows": row_grads,
            "wq": query_weight,
            "wk": key_weight,
            "wv": value_weight,
        },
        {
            "o": (pairs, own_pair),
            "p": (pairs, far_pair),
            "a": (chunks, widen),
            "b": (chunks, narrow),
            "f": (chunks, outer_back),
            "g": (chunks, inner_back),
            "x": (pairs, partial(pair_back, False)),
            "y": (pairs, partial(pair_back, True)),
        },
    )
    total = sums.finish()
    s = lax.axis_index("shard")
    part = out_small.shape[1]
    quarter = n // 4
    exact = lax.Precision.HIGHEST
    place = one_hot(part, D, s * part)
    out_small[...] = lax.dot_general(
        total[0:8, :], place, (((1,), (1,)), ((), ())), precision=exact, preferred_element_type=F32
    )
    place = one_hot(4 * part, D, (s % quarter) * 4 * part)
    wide_sum = lax.dot_general(
        total[8:12, :], place, (((1,), (1,)), ((), ())), precision=exact, preferred_element_type=F32
    )
    row = lax.broadcasted_iota(jnp.int32, wide_sum.shape, 0)
    out_wide[...] = column_total(jnp.where(row == s // quarter, wide_sum, 0.0))
    home.drain()
    home.arrived()

    @pl.when(z < half)
    def _():
        unit1[...] = unit1[...] + b["back"][...].astype(F32)

    rows_copy = pltpu.make_async_copy(unit1, h_rows, b["hbm_sem"].at[2])
    rows_copy.start()
    for name in "UIOQ":
        segments[name].finish()
    result_copy.wait()
    rows_copy.wait()


def layer_call(n, smalls, wide, tok, w_q, w_k, w_v, w_o, inner, outer, prompt_ids, cont_ids, offsets, cot):
    length, ff = tok.shape[0], inner.shape[2]
    vmem = pl.BlockSpec(memory_space=pltpu.VMEM)
    smem = pl.BlockSpec(memory_space=pltpu.SMEM)
    hbm = pl.BlockSpec(memory_space=pl.ANY)
    sds = jax.ShapeDtypeStruct
    spec, shapes = scratch_of(n, length, ff)
    outs = [sds(s, F32) for s in shapes.values()]
    outs += [sds((8, D // n), F32), sds((1, ff // n), F32)]
    outs += [sds((length, D), F32), sds((length, D), F32)]
    return pl.pallas_call(
        partial(layer_kernel, n, tuple(spec)),
        out_shape=outs,
        in_specs=[vmem] * 10 + [hbm] * 4 + [vmem] * 4 + [smem, hbm],
        out_specs=[vmem] * 6 + [hbm] * 2,
        scratch_shapes=list(spec.values()),
        compiler_params=pltpu.CompilerParams(
            collective_id=0, has_side_effects=True, vmem_limit_bytes=67043328
        ),
        name="layer_step",
    )(*smalls, wide, tok, w_q, w_k, w_v, w_o, inner, outer, prompt_ids, cont_ids, offsets, cot)


def copy_out_kernel(count, *refs):
    sources, three, small, wide = refs[: count - 3], refs[count - 3], *refs[count - 2 : count]
    refs = refs[count:]
    outs, small_outs, wide_out = refs[:count], refs[count : count + 8], refs[count + 8]
    held = refs[count + 9 : 2 * count + 9]
    come, go = refs[2 * count + 9 :]
    sources = list(sources) + [three.at[i] for i in range(3)]
    coming = [pltpu.make_async_copy(a, h, come.at[i]) for i, (a, h) in enumerate(zip(sources, held))]
    going = [pltpu.make_async_copy(h, o, go.at[i]) for i, (h, o) in enumerate(zip(held, outs))]
    for copy in coming:
        copy.start()
    for i in range(8):
        small_outs[i][...] = small[i : i + 1, :]
    wide_out[...] = wide[...]
    for first, second in zip(coming, going):
        first.wait()
        second.start()
    for copy in going:
        copy.wait()


def copy_out(arrays, three, small, wide):
    vmem = pl.BlockSpec(memory_space=pltpu.VMEM)
    hbm = pl.BlockSpec(memory_space=pl.ANY)
    sds = jax.ShapeDtypeStruct
    count = len(arrays) + 3
    shapes = [a.shape for a in arrays] + [three.shape[1:]] * 3
    outs = [sds(s, F32) for s in shapes]
    outs += [sds((1, small.shape[1]), F32)] * 8 + [sds(wide.shape, F32)]
    return pl.pallas_call(
        partial(copy_out_kernel, count),
        out_shape=outs,
        in_specs=[hbm] * (count - 2) + [vmem] * 2,
        out_specs=[hbm] * count + [vmem] * 9,
        scratch_shapes=[pltpu.VMEM(s, F32) for s in shapes]
        + [pltpu.SemaphoreType.DMA((count,)), pltpu.SemaphoreType.DMA((count,))],
        compiler_params=pltpu.CompilerParams(vmem_limit_bytes=67043328),
        name="copy_out",
    )(*arrays, three, small, wide)


def body(
    tokens,
    w_query,
    b_query,
    w_key,
    w_value,
    b_value,
    w_attout,
    b_attout,
    gain_first,
    beta_first,
    w_inner,
    b_inner,
    w_outer,
    b_outer,
    gain_second,
    beta_second,
    cotangent,
    prompt_ids,
    cont_ids,
    offsets,
):
    n = lax.axis_size("shard")
    reps = lax.axis_size("rep")
    small = (
        b_query,
        b_value,
        b_attout,
        gain_first,
        beta_first,
        b_outer,
        gain_second,
        beta_second,
    )
    *owned, outcome, grad_rows = layer_call(
        n,
        [v[None] for v in small],
        b_inner,
        tokens,
        w_query,
        w_key,
        w_value,
        w_attout,
        w_inner[None],
        w_outer[None],
        prompt_ids,
        cont_ids,
        offsets.T,
        cotangent,
    )
    if reps > 2:
        owned = [v * 0.5 for v in lax.psum(tuple(owned), "rep")]
    own_wu, own_wi, own_wo, three, vectors, wide = owned
    own_wu, own_wi, own_wo = own_wu[0], own_wi[0], own_wo[0]
    own_wq, own_wk, own_wv = three[0], three[1], three[2]
    if reps == 2:
        finished = copy_out([outcome, grad_rows, own_wu, own_wi, own_wo], three, vectors, wide)
        outcome, grad_rows, own_wu, own_wi, own_wo, own_wq, own_wk, own_wv = finished[:8]
        vectors, wide = [v[0] for v in finished[8:16]], finished[16]
    s_bq, s_bv, s_bo, s_g1, s_be1, s_bu, s_g2, s_be2 = (vectors[i] for i in range(8))
    return (
        outcome,
        grad_rows,
        own_wq,
        s_bq,
        own_wk,
        own_wv,
        s_bv,
        own_wo,
        s_bo,
        s_g1,
        s_be1,
        own_wi,
        wide[0],
        own_wu,
        s_bu,
        s_g2,
        s_be2,
    )


def solution(mesh):
    return jax.shard_map(
        body,
        mesh=mesh,
        in_specs=(
            P(("rep", "shard"), None),
            P("shard", None),
            P("shard"),
            P("shard", None),
            P("shard", None),
            P("shard"),
            P("shard", None),
            P("shard"),
            P("shard"),
            P("shard"),
            P("shard", None),
            P("shard"),
            P("shard", None),
            P("shard"),
            P("shard"),
            P("shard"),
            P(("rep", "shard"), None),
            P(),
            P(),
            P(),
        ),
        out_specs=(
            P(("rep", "shard"), None),
            P(("rep", "shard"), None),
            P("shard", None),
            P("shard"),
            P("shard", None),
            P("shard", None),
            P("shard"),
            P("shard", None),
            P("shard"),
            P("shard"),
            P("shard"),
            P("shard", None),
            P("shard"),
            P("shard", None),
            P("shard"),
            P("shard"),
            P("shard"),
        ),
        check_vma=False,
    )
```
